32 devices in a mesh: shard: 4 (over x, core), rep: 8 (over z, y).
Axes of the slice: x: 2, y: 2, z: 4, core: 2. Of those that a mesh axis runs over, the one named last changes fastest.
Arguments:
- tokens: bfloat16 [2, 32, 1024, 768], P(None, ('shard', 'rep')), may hold values from -6 to 6
- segment_ids: int32 [2, 32, 1024], P(None, ('shard', 'rep')), may hold values from 0 to 7, never falling along the last dimension, each value on 1 to 512 neighbouring positions
- cotangent: bfloat16 [2, 32, 1024, 768], P(None, ('shard', 'rep')), may hold values from -6 to 6
- w_qkv: bfloat16 [768, 2304], P('shard'), may hold values from -0.21875 to 0.21875
- b_query: bfloat16 [768], P('shard'), may hold values from -1.75 to 1.75
- b_value: bfloat16 [768], P('shard'), may hold values from -1.75 to 1.75
- w_out: bfloat16 [768, 768], P('shard'), may hold values from -0.875 to 0.875
- b_out: bfloat16 [768], P('shard'), may hold values from -1.75 to 1.75
- gain_one: bfloat16 [768], P('shard'), may hold values from 0.25 to 1.75
- shift_one: bfloat16 [768], P('shard'), may hold values from -1.75 to 1.75
- w_in: bfloat16 [768, 3072], P('shard'), may hold values from -0.21875 to 0.21875
- b_in: bfloat16 [3072], P('shard'), may hold values from -1.75 to 1.75
- w_ffo: bfloat16 [3072, 768], P('shard'), may hold values from -0.109375 to 0.109375
- b_ffo: bfloat16 [768], P('shard'), may hold values from -1.75 to 1.75
- gain_two: bfloat16 [768], P('shard'), may hold values from 0.25 to 1.75
- shift_two: bfloat16 [768], P('shard'), may hold values from -1.75 to 1.75
Outputs:
- layer_output: bfloat16 [2, 32, 1024, 768], P(None, ('shard', 'rep'))
- input_grad: bfloat16 [2, 32, 1024, 768], P(None, ('shard', 'rep'))
- grad_qkv: float32 [768, 2304], P('shard')
- grad_query_bias: float32 [768], P('shard')
- grad_value_bias: float32 [768], P('shard')
- grad_out_proj: float32 [768, 768], P('shard')
- grad_out_bias: float32 [768], P('shard')
- grad_gain_one: float32 [768], P('shard')
- grad_shift_one: float32 [768], P('shard')
- grad_in_proj: float32 [768, 3072], P('shard')
- grad_in_bias: float32 [3072], P('shard')
- grad_ffo_proj: float32 [3072, 768], P('shard')
- grad_ffo_bias: float32 [768], P('shard')
- grad_gain_two: float32 [768], P('shard')
- grad_shift_two: float32 [768], P('shard')
The draws below stay inside these ranges and needn't reach their ends.
Inputs may be any that keep to these rules, and one draw needn't show every extreme that they name: `segment_ids`: along each sequence the ids never fall; each of the 8 documents has 1 to 512 tokens, and a document of exactly 512 tokens occurs.
All inputs are finite; a program needn't handle non-finite values.
Results may differ from the reference program's by a relative error of at most 0.02.
Values may be sent and summed in bfloat16 or wider, within the bound.
A program may use at most 320 MiB of HBM per device.

```python
import math
import jax
import jax.numpy as jnp
import numpy as np
from jax import lax

D = 768
HEADS = 12
HEAD_DIM = 64
FF = 3072
SEQ = 1024
DOCS = 8
MB = 2
NSEQ = 32


def steps_of(key, shape, cuts, low, largest):
    def one(position, parts):
        heights = jax.random.uniform(jax.random.fold_in(jax.random.fold_in(key, 6), position), (parts,), jnp.float32, low / len(cuts), largest / len(cuts))
        return jnp.repeat(jnp.exp(heights), shape[position] // parts).reshape((-1,) + (1,) * (len(shape) - position - 1))

    loudness = one(*cuts[0])
    for cut in cuts[1:]:
        loudness = loudness * one(*cut)
    return loudness


def profile(amount, total, bound, slope):
    weights = [(1 << 20) // math.isqrt(rank ** slope) + 1 for rank in range(2, amount + 1)]
    surplus, counts = total - bound - (amount - 1), [1] * (amount - 1)
    while surplus > 0:
        movable = [i for i in range(amount - 1) if counts[i] < bound]
        mass, left = sum([weights[i] for i in movable]), surplus
        for i in movable:
            addition = min(bound - counts[i], max(1, left * weights[i] // mass), surplus)
            counts[i] = counts[i] + addition
            surplus = surplus - addition
    return np.array([bound] + counts)


def ragged(stream_key, amount, total, reach, slope):
    if amount == 2:
        one = jax.random.randint(stream_key, (), max(1, total - reach), min(reach, total - 1) + 1)
        return jnp.stack([one, total - one])
    tallies = jnp.asarray(profile(amount, total, reach, slope), jnp.int32)
    twos = (amount - 1) // 2
    donor, taker = tallies[1:1 + 2 * twos:2], tallies[2:2 + 2 * twos:2]
    slack = jnp.minimum(donor - 1, reach - taker)
    moved = jax.random.randint(jax.random.fold_in(stream_key, 1), (twos,), 0, 1 << 20) % (slack + 1)
    tallies = tallies.at[1:1 + 2 * twos:2].set(donor - moved).at[2:2 + 2 * twos:2].set(taker + moved)
    return tallies[jax.random.permutation(jax.random.fold_in(stream_key, 2), amount)]


def noise(own_key, shape, deviation, bound, shards=(), held_as=jnp.bfloat16):
    array = deviation * jax.random.normal(own_key, shape, jnp.float32)
    if shards:
        array = array * steps_of(own_key, shape, shards, -0.22, 0.18)
    return jnp.clip(array, -bound, bound).astype(held_as)


def setup_inputs(seed: int = 0) -> dict:
    keys = jax.random.split(jax.random.key(seed), 17)
    tokens = noise(keys[0], (MB, NSEQ, SEQ, D), 1.0, 6.0, ((1, 32),))
    segment_ids = jax.vmap(lambda own: jnp.searchsorted(jnp.cumsum(ragged(own, DOCS, SEQ, SEQ // 2, 2)), jnp.arange(SEQ), side="right"))(jax.random.split(keys[1], MB * NSEQ)).reshape((MB, NSEQ, SEQ)).astype(jnp.int32)
    cotangent = noise(keys[2], (MB, NSEQ, SEQ, D), 1.0, 6.0, ((1, 32),))
    w_qkv = noise(keys[3], (D, 3 * D), D ** -0.5, 0.21875, ((0, 4),))
    b_query = noise(keys[4], (D,), 0.3, 1.75, ((0, 4),))
    b_value = noise(keys[5], (D,), 0.3, 1.75, ((0, 4),))
    w_out = noise(keys[6], (D, D), (D // 16) ** -0.5, 0.875, ((0, 4),))
    b_out = noise(keys[7], (D,), 0.3, 1.75, ((0, 4),))
    gain_one = jnp.clip(1.0 + 0.15 * jax.random.normal(keys[8], (D,), jnp.float32), 0.25, 1.75).astype(jnp.bfloat16)
    shift_one = noise(keys[9], (D,), 0.3, 1.75, ((0, 4),))
    w_in = noise(keys[10], (D, FF), D ** -0.5, 0.21875, ((0, 4),))
    b_in = noise(keys[11], (FF,), 0.3, 1.75, ((0, 4),))
    w_ffo = noise(keys[12], (FF, D), FF ** -0.5, 0.109375, ((0, 4),))
    b_ffo = noise(keys[13], (D,), 0.3, 1.75, ((0, 4),))
    gain_two = jnp.clip(1.0 + 0.15 * jax.random.normal(keys[14], (D,), jnp.float32), 0.25, 1.75).astype(jnp.bfloat16)
    shift_two = noise(keys[15], (D,), 0.3, 1.75, ((0, 4),))
    return {"tokens": tokens, "segment_ids": segment_ids, "cotangent": cotangent, "w_qkv": w_qkv, "b_query": b_query, "b_value": b_value, "w_out": w_out, "b_out": b_out, "gain_one": gain_one, "shift_one": shift_one, "w_in": w_in, "b_in": b_in, "w_ffo": w_ffo, "b_ffo": b_ffo, "gain_two": gain_two, "shift_two": shift_two}


epsilon = 1e-05
masked_score = -1e+30

@jax.custom_vjp
def low(v):
    return lax.optimization_barrier(v.astype(jnp.bfloat16)).astype(jnp.float32)

@jax.custom_vjp
def low_back(v):
    return v

def low_keep(v):
    return (low(v), None)

def low_pass(kept, grad):
    return (grad,)

def back_keep(v):
    return (v, None)

def back_low(kept, grad):
    return (low(grad),)
low.defvjp(low_keep, low_pass)
low_back.defvjp(back_keep, back_low)

def matmul(left, right):
    return jnp.dot(left, right, precision=lax.Precision.HIGHEST)

def normalize(values, gain_vec, shift_vec):
    center = values - lax.optimization_barrier(jnp.mean(values, axis=-1, keepdims=True))
    spread = lax.optimization_barrier(jnp.mean(center * center, axis=-1, keepdims=True))
    return center * lax.rsqrt(spread + epsilon) * gain_vec + shift_vec

def one_sequence(params, sample, segment):
    w_qkv, b_query, b_value, w_out, b_out, gain_one, shift_one, w_in, b_in, w_ffo, b_ffo, gain_two, shift_two = params
    model_width = sample.shape[-1]
    length = sample.shape[0]
    bias_all = jnp.concatenate([b_query, jnp.zeros_like(b_query), b_value])
    projected = low(low_back(matmul(sample, w_qkv) + bias_all))
    queries = projected[:, :model_width].reshape(length, HEADS, HEAD_DIM)
    key_rows = projected[:, model_width:2 * model_width].reshape(length, HEADS, HEAD_DIM)
    value_rows = projected[:, 2 * model_width:].reshape(length, HEADS, HEAD_DIM)
    scale = 1.0 / math.sqrt(HEAD_DIM)
    scores = jnp.einsum('qhd,khd->hqk', queries, key_rows, precision=lax.Precision.HIGHEST) * scale
    scores = low_back(scores)
    same_doc = segment[:, None] == segment[None, :]
    scores = jnp.where(same_doc[None], scores, masked_score)
    row_top = lax.optimization_barrier(jnp.max(scores, axis=-1, keepdims=True))
    exponent = jnp.exp(scores - row_top)
    weights_soft = low(exponent / lax.optimization_barrier(jnp.sum(exponent, axis=-1, keepdims=True)))
    attended = jnp.einsum('hqk,khd->qhd', weights_soft, value_rows, precision=lax.Precision.HIGHEST)
    attended = low(low_back(attended.reshape(length, model_width)))
    branch = low_back(matmul(attended, w_out) + b_out)
    normed_one = low(normalize(sample + branch, gain_one, shift_one))
    ffn_pre = low_back(matmul(normed_one, w_in) + b_in)
    hidden = low(jax.nn.gelu(ffn_pre, approximate=False))
    second = low_back(matmul(hidden, w_ffo) + b_ffo)
    return normalize(normed_one + second, gain_two, shift_two)

def reference(tokens, segment_ids, cotangent, w_qkv, b_query, b_value, w_out, b_out, gain_one, shift_one, w_in, b_in, w_ffo, b_ffo, gain_two, shift_two):
    params = tuple((entry.astype(jnp.float32) for entry in (w_qkv, b_query, b_value, w_out, b_out, gain_one, shift_one, w_in, b_in, w_ffo, b_ffo, gain_two, shift_two)))
    flat_tokens = tokens.astype(jnp.float32).reshape(-1, SEQ, D)
    flat_segments = segment_ids.reshape(-1, SEQ)

    def forward(weights_all, inputs):
        per_sequence = jax.checkpoint(lambda sample: one_sequence(weights_all, sample[0], sample[1]))
        return lax.map(per_sequence, (inputs, flat_segments))
    result, pullback = jax.vjp(forward, params, flat_tokens)
    gradients, token_grad = pullback(cotangent.astype(jnp.float32).reshape(-1, SEQ, D))
    layer_output = result.reshape(tokens.shape).astype(jnp.bfloat16)
    input_grad = token_grad.reshape(tokens.shape).astype(jnp.bfloat16)
    return (layer_output, input_grad, gradients[0], gradients[1], gradients[2], gradients[3], gradients[4], gradients[5], gradients[6], gradients[7], gradients[8], gradients[9], gradients[10], gradients[11], gradients[12])
```

```python
import functools
import math

import jax
import jax.numpy as jnp
from jax import lax
from jax.experimental import pallas as pl
from jax.experimental.pallas import tpu as pltpu
from jax.sharding import PartitionSpec as P

HEADS = 12
HEAD_DIM = 64
PAIR = 2 * HEAD_DIM
TILE = 128

epsilon = 1e-05
masked_score = -1e30
BF = jnp.bfloat16
F32 = jnp.float32
VMEM_LIMIT = 60 * 2**20


def dot_nn(a, b):
    return lax.dot_general(a, b, (((1,), (0,)), ((), ())), preferred_element_type=F32)


def dot_nt(a, b):
    return lax.dot_general(a, b, (((1,), (1,)), ((), ())), preferred_element_type=F32)


def dot_tn(a, b):
    return lax.dot_general(a, b, (((0,), (0,)), ((), ())), preferred_element_type=F32)


def head_rows(value):
    lane = lax.broadcasted_iota(jnp.int32, (1, PAIR), 1)
    first = jnp.where(lane < HEAD_DIM, value, 0.0).astype(BF)
    second = jnp.where(lane < HEAD_DIM, 0.0, value).astype(BF)
    return first, second


def stack_heads(block, rows):
    return jnp.concatenate([block * rows[0], block * rows[1]], axis=0)


def diagonal_back(transposed):
    kept = jnp.concatenate(
        [transposed[:HEAD_DIM, :TILE], transposed[HEAD_DIM:, TILE:]], axis=0
    )
    return kept.T


def for_windows(count, tiles, body):
    sizes = [t for t in range(1, tiles + 1) if t < 7 or t == tiles]
    below = 0
    for size in sizes:
        @pl.when((count > below) & (count <= size))
        def _(size=size):
            body(size)

        below = size


def attend_forward_kernel(pairs, tiles, low_ref, count_ref, q_ref, k_ref, v_ref, kseg_ref, qseg_ref, o_ref, lse_ref):
    place = pl.program_id(0) * tiles + pl.program_id(1)
    low = low_ref[place]
    count = count_ref[place]
    rows_of = head_rows(1.0 / math.sqrt(HEAD_DIM))

    def window(size):
        start = jnp.minimum(low, tiles - size) * TILE
        chunks = [pl.ds(pl.multiple_of(start + c * TILE, TILE), TILE) for c in range(size)]
        whole = pl.ds(pl.multiple_of(start, TILE), size * TILE)
        masks = [kseg_ref[c, :] == qseg_ref[0] for c in chunks]
        for p in range(pairs):
            lanes = slice(p * PAIR, (p + 1) * PAIR)
            queries = stack_heads(q_ref[:, lanes], rows_of)
            scores = []
            for c, mask in zip(chunks, masks):
                part = dot_nt(k_ref[c, lanes], queries)
                scores.append(
                    jnp.concatenate(
                        [
                            jnp.where(mask, part[:, :TILE], masked_score),
                            jnp.where(mask, part[:, TILE:], masked_score),
                        ],
                        axis=1,
                    )
                )
            top = functools.reduce(jnp.maximum, [jnp.max(s, axis=0, keepdims=True) for s in scores])
            exps = [jnp.exp(s - top) for s in scores]
            total = functools.reduce(jnp.add, [jnp.sum(e, axis=0, keepdims=True) for e in exps])
            weights = jnp.concatenate([e.astype(BF) for e in exps], axis=0)
            mixed = dot_tn(v_ref[whole, lanes], weights) / total
            o_ref[:, lanes] = diagonal_back(mixed).astype(BF)
            lse_ref[0, p : p + 1, :] = top + jnp.log(total)

    for_windows(count, tiles, window)


def attend_backward_kernel(
    pairs, tiles, low_ref, count_ref, q_ref, k_ref, v_ref, do_ref, o_ref, lse_ref, kseg_ref, qseg_ref,
    dq_ref, dk_ref, dv_ref, dk_acc, dv_acc,
):
    group = pl.program_id(1)
    block = pl.program_id(2)
    place = pl.program_id(0) * tiles + block
    low = low_ref[place]
    count = count_ref[place]
    scale = 1.0 / math.sqrt(HEAD_DIM)
    scaled_rows = head_rows(scale)
    plain_rows = head_rows(1.0)

    @pl.when(block == 0)
    def _():
        dk_acc[...] = jnp.zeros_like(dk_acc)
        dv_acc[...] = jnp.zeros_like(dv_acc)

    def window(size):
        start = jnp.minimum(low, tiles - size) * TILE
        chunks = [pl.ds(pl.multiple_of(start + c * TILE, TILE), TILE) for c in range(size)]
        whole = pl.ds(pl.multiple_of(start, TILE), size * TILE)
        masks = [kseg_ref[c, :] == qseg_ref[0] for c in chunks]
        for p in range(pairs):
            lanes = slice(p * PAIR, (p + 1) * PAIR)
            queries = stack_heads(q_ref[:, lanes], scaled_rows)
            grads = do_ref[:, lanes]
            stacked = stack_heads(grads, plain_rows)
            product = (grads.astype(F32) * o_ref[:, lanes].astype(F32)).T
            row_dot = jnp.concatenate(
                [
                    jnp.sum(product[:HEAD_DIM], axis=0, keepdims=True),
                    jnp.sum(product[HEAD_DIM:], axis=0, keepdims=True),
                ],
                axis=1,
            )
            lse = lse_ref[0, pl.ds(group * pairs + p, 1), :]
            kept = []
            for c, mask in zip(chunks, masks):
                part = dot_nt(k_ref[c, lanes], queries) - lse
                d_probs = dot_nt(v_ref[c, lanes], stacked)
                probs = jnp.exp(
                    jnp.concatenate(
                        [
                            jnp.where(mask, part[:, :TILE], masked_score),
                            jnp.where(mask, part[:, TILE:], masked_score),
                        ],
                        axis=1,
                    )
                )
                d_scores = (probs * (d_probs - row_dot)).astype(BF)
                kept.append(d_scores)
                dv_acc[c, lanes] += dot_nn(probs.astype(BF), stacked)
                dk_acc[c, lanes] += dot_nn(d_scores, queries)
            mixed = dot_tn(k_ref[whole, lanes], jnp.concatenate(kept, axis=0)) * scale
            dq_ref[:, lanes] = diagonal_back(mixed).astype(BF)

    for_windows(count, tiles, window)

    @pl.when(block == tiles - 1)
    def _():
        dk_ref[...] = dk_acc[...].astype(BF)
        dv_ref[...] = dv_acc[...].astype(BF)


def windows_of(segments):
    sequences, length = segments.shape
    tiles = length // TILE
    blocked = segments.reshape(sequences, tiles, TILE)
    first = blocked[:, :, 0]
    last = blocked[:, :, TILE - 1]
    starts = jnp.sum((segments[:, None, :] < first[:, :, None]).astype(jnp.int32), axis=-1)
    ends = jnp.sum((segments[:, None, :] <= last[:, :, None]).astype(jnp.int32), axis=-1)
    low = starts // TILE
    count = (ends + TILE - 1) // TILE - low
    key_ids = jnp.broadcast_to(segments.reshape(sequences * length, 1), (sequences * length, TILE))
    query_ids = blocked.reshape(sequences * tiles, 1, TILE)
    return low.reshape(-1), count.reshape(-1), key_ids, query_ids


def attend_forward(projected, windows, sequences):
    low, count, key_ids, query_ids = windows
    rows = projected.shape[0]
    width = projected.shape[1] // 3
    length = rows // sequences
    tiles = length // TILE
    pairs = width // PAIR
    return pl.pallas_call(
        functools.partial(attend_forward_kernel, pairs, tiles),
        grid_spec=pltpu.PrefetchScalarGridSpec(
            num_scalar_prefetch=2,
            grid=(sequences, tiles),
            in_specs=[
                pl.BlockSpec((TILE, width), lambda s, b, *_: (s * tiles + b, 0)),
                pl.BlockSpec((length, width), lambda s, b, *_: (s, 1)),
                pl.BlockSpec((length, width), lambda s, b, *_: (s, 2)),
                pl.BlockSpec((length, TILE), lambda s, b, *_: (s, 0)),
                pl.BlockSpec((1, 1, TILE), lambda s, b, *_: (s * tiles + b, 0, 0)),
            ],
            out_specs=[
                pl.BlockSpec((TILE, width), lambda s, b, *_: (s * tiles + b, 0)),
                pl.BlockSpec((1, 8, 2 * TILE), lambda s, b, *_: (s * tiles + b, 0, 0)),
            ],
        ),
        out_shape=[
            jax.ShapeDtypeStruct((rows, width), BF),
            jax.ShapeDtypeStruct((sequences * tiles, 8, 2 * TILE), F32),
        ],
        compiler_params=pltpu.CompilerParams(vmem_limit_bytes=VMEM_LIMIT),
        cost_estimate=pl.CostEstimate(flops=8 * 10**9, bytes_accessed=16 * 10**6, transcendentals=0),
        name="attend_forward",
    )(low, count, projected, projected, projected, key_ids, query_ids)


def attend_backward(projected, d_attended, attended, lse, windows, sequences, groups=2):
    low, count, key_ids, query_ids = windows
    rows = projected.shape[0]
    width = projected.shape[1] // 3
    length = rows // sequences
    tiles = length // TILE
    part = width // groups
    pairs = part // PAIR
    query_spec = pl.BlockSpec((TILE, part), lambda s, g, b, *_: (s * tiles + b, g))
    return pl.pallas_call(
        functools.partial(attend_backward_kernel, pairs, tiles),
        grid_spec=pltpu.PrefetchScalarGridSpec(
            num_scalar_prefetch=2,
            grid=(sequences, groups, tiles),
            in_specs=[
                query_spec,
                pl.BlockSpec((length, part), lambda s, g, b, *_: (s, groups + g)),
                pl.BlockSpec((length, part), lambda s, g, b, *_: (s, 2 * groups + g)),
                query_spec,
                query_spec,
                pl.BlockSpec((1, 8, 2 * TILE), lambda s, g, b, *_: (s * tiles + b, 0, 0)),
                pl.BlockSpec((length, TILE), lambda s, g, b, *_: (s, 0)),
                pl.BlockSpec((1, 1, TILE), lambda s, g, b, *_: (s * tiles + b, 0, 0)),
            ],
            out_specs=[
                query_spec,
                pl.BlockSpec((length, part), lambda s, g, b, *_: (s, g)),
                pl.BlockSpec((length, part), lambda s, g, b, *_: (s, g)),
            ],
            scratch_shapes=[pltpu.VMEM((length, part), F32), pltpu.VMEM((length, part), F32)],
        ),
        out_shape=[jax.ShapeDtypeStruct((rows, width), BF)] * 3,
        compiler_params=pltpu.CompilerParams(vmem_limit_bytes=VMEM_LIMIT),
        cost_estimate=pl.CostEstimate(flops=30 * 10**9, bytes_accessed=30 * 10**6, transcendentals=0),
        name="attend_backward",
    )(low, count, projected, projected, projected, d_attended, attended, lse, key_ids, query_ids)


def layer_norm(values, gain_vec, shift_vec):
    center = values - jnp.mean(values, axis=-1, keepdims=True)
    spread = jnp.mean(center * center, axis=-1, keepdims=True)
    rstd_rows = lax.rsqrt(spread + epsilon)
    scaled = center * rstd_rows
    return (scaled * gain_vec + shift_vec, scaled, rstd_rows)


def norm_backward(grad, scaled, rstd_rows, gain_vec):
    inner = grad * gain_vec
    d_input = rstd_rows * (
        inner
        - jnp.mean(inner, axis=-1, keepdims=True)
        - scaled * jnp.mean(inner * scaled, axis=-1, keepdims=True)
    )
    return (d_input, jnp.sum(grad * scaled, axis=0), jnp.sum(grad, axis=0))


def gelu_slope(values):
    return 0.5 * (1.0 + lax.erf(values * (1.0 / math.sqrt(2.0)))) + values * jnp.exp(
        -0.5 * values * values
    ) * (1.0 / math.sqrt(2.0 * math.pi))


def local(
    tokens,
    segment_ids,
    cotangent,
    w_qkv,
    b_query,
    b_value,
    w_out,
    b_out,
    gain_one,
    shift_one,
    w_in,
    b_in,
    w_ffo,
    b_ffo,
    gain_two,
    shift_two,
):
    micro, sequences, length, width = tokens.shape
    total = micro * sequences
    rows = total * length
    x = tokens.reshape(rows, width)
    seg = segment_ids.reshape(total, length)
    cot = cotangent.reshape(rows, width).astype(F32)

    def gather(a):
        return lax.all_gather(a, "shard", axis=0, tiled=True)

    full_qkv = gather(w_qkv)
    full_out = gather(w_out)
    full_in = gather(w_in)
    full_ffo = gather(w_ffo)
    small_shards = (b_query, b_value, b_out, gain_one, shift_one, b_ffo, gain_two, shift_two, b_in)
    part = b_query.shape[0]
    small = jnp.concatenate(small_shards).reshape(1, -1)
    small_full = gather(small).astype(F32)
    piece = [small_full[:, i * part : (i + 1) * part].reshape(-1) for i in range(8)]
    bq, bv, bo, g1, s1, bf, g2, s2 = piece
    bi = small_full[:, 8 * part :].reshape(-1)

    windows = windows_of(seg)
    bias_all = jnp.concatenate([bq, jnp.zeros_like(bq), bv])
    projected = (dot_nn(x, full_qkv) + bias_all).astype(BF)
    attended, lse = attend_forward(projected, windows, total)
    branch = dot_nn(attended, full_out) + bo
    normed_one, n_one, rstd_one = layer_norm(x.astype(F32) + branch, g1, s1)
    normed = normed_one.astype(BF)
    pre = dot_nn(normed, full_in) + bi
    hidden = jax.nn.gelu(pre, approximate=False).astype(BF)
    second = dot_nn(hidden, full_ffo) + bf
    output, n_two, rstd_two = layer_norm(normed.astype(F32) + second, g2, s2)
    output = output.astype(BF)

    d_res_two, d_gain_two, d_shift_two = norm_backward(cot, n_two, rstd_two, g2)
    d_second = d_res_two.astype(BF)
    d_ffo_bias = jnp.sum(d_second.astype(F32), axis=0)
    d_ffo = dot_tn(hidden, d_second)
    d_pre = (dot_nt(d_second, full_ffo) * gelu_slope(pre)).astype(BF)
    d_in_bias = jnp.sum(d_pre.astype(F32), axis=0)
    d_in = dot_tn(normed, d_pre)
    d_norm_one = d_res_two + dot_nt(d_pre, full_in)
    d_res_one, d_gain_one, d_shift_one = norm_backward(d_norm_one, n_one, rstd_one, g1)
    d_branch = d_res_one.astype(BF)
    d_out_bias = jnp.sum(d_branch.astype(F32), axis=0)
    d_out = dot_tn(attended, d_branch)
    d_attended = dot_nt(d_branch, full_out).astype(BF)
    dq, dk, dv = attend_backward(projected, d_attended, attended, lse, windows, total)
    d_projected = jnp.concatenate([dq, dk, dv], axis=1)
    d_query_bias = jnp.sum(dq.astype(F32), axis=0)
    d_value_bias = jnp.sum(dv.astype(F32), axis=0)
    d_qkv = dot_tn(x, d_projected)
    d_tokens = (d_res_one + dot_nt(d_projected, full_qkv)).astype(BF)

    def reduce(grad):
        owned = lax.psum_scatter(grad.astype(BF), "shard", scatter_dimension=0, tiled=True)
        return lax.psum(owned, "rep").astype(F32)

    smalls = (
        d_query_bias, d_value_bias, d_out_bias, d_gain_one, d_shift_one, d_ffo_bias, d_gain_two, d_shift_two,
        d_in_bias,
    )
    group = lax.axis_size("shard")
    packed = jnp.concatenate([s.reshape(group, -1) for s in smalls], axis=1)
    packed = lax.psum(packed, ("shard", "rep"))
    mine = lax.dynamic_index_in_dim(packed, lax.axis_index("shard"), 0, keepdims=False)
    sm = [mine[i * part : (i + 1) * part] for i in range(8)]
    gqb, gvb, gob, gg1, gs1, gfb, gg2, gs2 = sm
    gib = mine[8 * part :]
    return (
        output.reshape(tokens.shape),
        d_tokens.reshape(tokens.shape),
        reduce(d_qkv),
        gqb,
        gvb,
        reduce(d_out),
        gob,
        gg1,
        gs1,
        reduce(d_in),
        gib,
        reduce(d_ffo),
        gfb,
        gg2,
        gs2,
    )


def solution(mesh):
    data = P(None, ("shard", "rep"), None, None)
    matrix = P("shard", None)
    vector = P("shard")
    return jax.shard_map(
        local,
        mesh=mesh,
        in_specs=(
            data,
            P(None, ("shard", "rep"), None),
            data,
            matrix,
            vector,
            vector,
            matrix,
            vector,
            vector,
            vector,
            matrix,
            vector,
            matrix,
            vector,
            vector,
            vector,
        ),
        out_specs=(
            data,
            data,
            matrix,
            vector,
            vector,
            matrix,
            vector,
            vector,
            vector,
            matrix,
            vector,
            matrix,
            vector,
            vector,
            vector,
        ),
        check_vma=False,
    )
```

```python
import functools
import math

import jax
import jax.numpy as jnp
from jax import lax
from jax.experimental import pallas as pl
from jax.experimental.pallas import tpu as pltpu
from jax.sharding import PartitionSpec as P

HEADS = 12
HEAD_DIM = 64
PAIR = 2 * HEAD_DIM
TILE = 128

epsilon = 1e-05
masked_score = -1e30
BF = jnp.bfloat16
F32 = jnp.float32
VMEM_LIMIT = 60 * 2**20


def dot_nn(a, b):
    return lax.dot_general(a, b, (((1,), (0,)), ((), ())), preferred_element_type=F32)


def dot_nt(a, b):
    return lax.dot_general(a, b, (((1,), (1,)), ((), ())), preferred_element_type=F32)


def dot_tn(a, b):
    return lax.dot_general(a, b, (((0,), (0,)), ((), ())), preferred_element_type=F32)


def head_rows(value):
    lane = lax.broadcasted_iota(jnp.int32, (1, PAIR), 1)
    first = jnp.where(lane < HEAD_DIM, value, 0.0).astype(BF)
    second = jnp.where(lane < HEAD_DIM, 0.0, value).astype(BF)
    return first, second


def stack_heads(block, rows):
    return jnp.concatenate([block * rows[0], block * rows[1]], axis=0)


def diagonal_back(transposed):
    kept = jnp.concatenate(
        [transposed[:HEAD_DIM, :TILE], transposed[HEAD_DIM:, TILE:]], axis=0
    )
    return kept.T


def for_windows(count, tiles, body):
    sizes = [t for t in range(1, tiles + 1) if t < 7 or t == tiles]
    below = 0
    for size in sizes:
        @pl.when((count > below) & (count <= size))
        def _(size=size):
            body(size)

        below = size


def attend_forward_kernel(pairs, tiles, low_ref, count_ref, q_ref, k_ref, v_ref, kseg_ref, qseg_ref, o_ref, lse_ref):
    place = pl.program_id(0) * tiles + pl.program_id(1)
    low = low_ref[place]
    count = count_ref[place]
    rows_of = head_rows(1.0 / math.sqrt(HEAD_DIM))

    def window(size):
        start = jnp.minimum(low, tiles - size) * TILE
        chunks = [pl.ds(pl.multiple_of(start + c * TILE, TILE), TILE) for c in range(size)]
        whole = pl.ds(pl.multiple_of(start, TILE), size * TILE)
        masks = [kseg_ref[c, :] == qseg_ref[0] for c in chunks]
        for p in range(pairs):
            lanes = slice(p * PAIR, (p + 1) * PAIR)
            queries = stack_heads(q_ref[:, lanes], rows_of)
            scores = []
            for c, mask in zip(chunks, masks):
                part = dot_nt(k_ref[c, lanes], queries)
                scores.append(
                    jnp.concatenate(
                        [
                            jnp.where(mask, part[:, :TILE], masked_score),
                            jnp.where(mask, part[:, TILE:], masked_score),
                        ],
                        axis=1,
                    )
                )
            top = functools.reduce(jnp.maximum, [jnp.max(s, axis=0, keepdims=True) for s in scores])
            exps = [jnp.exp(s - top) for s in scores]
            total = functools.reduce(jnp.add, [jnp.sum(e, axis=0, keepdims=True) for e in exps])
            weights = jnp.concatenate([e.astype(BF) for e in exps], axis=0)
            mixed = dot_tn(v_ref[whole, lanes], weights) / total
            o_ref[:, lanes] = diagonal_back(mixed).astype(BF)
            lse_ref[0, p : p + 1, :] = top + jnp.log(total)

    for_windows(count, tiles, window)


def attend_backward_kernel(
    pairs, tiles, low_ref, count_ref, q_ref, k_ref, v_ref, do_ref, o_ref, lse_ref, kseg_ref, qseg_ref,
    dq_ref, dk_ref, dv_ref, dk_acc, dv_acc,
):
    group = pl.program_id(1)
    block = pl.program_id(2)
    place = pl.program_id(0) * tiles + block
    low = low_ref[place]
    count = count_ref[place]
    scale = 1.0 / math.sqrt(HEAD_DIM)
    scaled_rows = head_rows(scale)
    plain_rows = head_rows(1.0)

    @pl.when(block == 0)
    def _():
        dk_acc[...] = jnp.zeros_like(dk_acc)
        dv_acc[...] = jnp.zeros_like(dv_acc)

    def window(size):
        start = jnp.minimum(low, tiles - size) * TILE
        chunks = [pl.ds(pl.multiple_of(start + c * TILE, TILE), TILE) for c in range(size)]
        whole = pl.ds(pl.multiple_of(start, TILE), size * TILE)
        masks = [kseg_ref[c, :] == qseg_ref[0] for c in chunks]
        for p in range(pairs):
            lanes = slice(p * PAIR, (p + 1) * PAIR)
            queries = stack_heads(q_ref[:, lanes], scaled_rows)
            grads = do_ref[:, lanes]
            stacked = stack_heads(grads, plain_rows)
            product = (grads.astype(F32) * o_ref[:, lanes].astype(F32)).T
            row_dot = jnp.concatenate(
                [
                    jnp.sum(product[:HEAD_DIM], axis=0, keepdims=True),
                    jnp.sum(product[HEAD_DIM:], axis=0, keepdims=True),
                ],
                axis=1,
            )
            lse = lse_ref[0, pl.ds(group * pairs + p, 1), :]
            kept = []
            for c, mask in zip(chunks, masks):
                part = dot_nt(k_ref[c, lanes], queries) - lse
                d_probs = dot_nt(v_ref[c, lanes], stacked)
                probs = jnp.exp(
                    jnp.concatenate(
                        [
                            jnp.where(mask, part[:, :TILE], masked_score),
                            jnp.where(mask, part[:, TILE:], masked_score),
                        ],
                        axis=1,
                    )
                )
                d_scores = (probs * (d_probs - row_dot)).astype(BF)
                kept.append(d_scores)
                dv_acc[c, lanes] += dot_nn(probs.astype(BF), stacked)
                dk_acc[c, lanes] += dot_nn(d_scores, queries)
            mixed = dot_tn(k_ref[whole, lanes], jnp.concatenate(kept, axis=0)) * scale
            dq_ref[:, lanes] = diagonal_back(mixed).astype(BF)

    for_windows(count, tiles, window)

    @pl.when(block == tiles - 1)
    def _():
        dk_ref[...] = dk_acc[...].astype(BF)
        dv_ref[...] = dv_acc[...].astype(BF)


def windows_of(segments):
    sequences, length = segments.shape
    tiles = length // TILE
    blocked = segments.reshape(sequences, tiles, TILE)
    first = blocked[:, :, 0]
    last = blocked[:, :, TILE - 1]
    starts = jnp.sum((segments[:, None, :] < first[:, :, None]).astype(jnp.int32), axis=-1)
    ends = jnp.sum((segments[:, None, :] <= last[:, :, None]).astype(jnp.int32), axis=-1)
    low = starts // TILE
    count = (ends + TILE - 1) // TILE - low
    key_ids = jnp.broadcast_to(segments.reshape(sequences * length, 1), (sequences * length, TILE))
    query_ids = blocked.reshape(sequences * tiles, 1, TILE)
    return low.reshape(-1), count.reshape(-1), key_ids, query_ids


def attend_forward(projected, windows, sequences):
    low, count, key_ids, query_ids = windows
    rows = projected.shape[0]
    width = projected.shape[1] // 3
    length = rows // sequences
    tiles = length // TILE
    pairs = width // PAIR
    return pl.pallas_call(
        functools.partial(attend_forward_kernel, pairs, tiles),
        grid_spec=pltpu.PrefetchScalarGridSpec(
            num_scalar_prefetch=2,
            grid=(sequences, tiles),
            in_specs=[
                pl.BlockSpec((TILE, width), lambda s, b, *_: (s * tiles + b, 0)),
                pl.BlockSpec((length, width), lambda s, b, *_: (s, 1)),
                pl.BlockSpec((length, width), lambda s, b, *_: (s, 2)),
                pl.BlockSpec((length, TILE), lambda s, b, *_: (s, 0)),
                pl.BlockSpec((1, 1, TILE), lambda s, b, *_: (s * tiles + b, 0, 0)),
            ],
            out_specs=[
                pl.BlockSpec((TILE, width), lambda s, b, *_: (s * tiles + b, 0)),
                pl.BlockSpec((1, 8, 2 * TILE), lambda s, b, *_: (s * tiles + b, 0, 0)),
            ],
        ),
        out_shape=[
            jax.ShapeDtypeStruct((rows, width), BF),
            jax.ShapeDtypeStruct((sequences * tiles, 8, 2 * TILE), F32),
        ],
        compiler_params=pltpu.CompilerParams(vmem_limit_bytes=VMEM_LIMIT),
        cost_estimate=pl.CostEstimate(flops=8 * 10**9, bytes_accessed=16 * 10**6, transcendentals=0),
        name="attend_forward",
    )(low, count, projected, projected, projected, key_ids, query_ids)


def attend_backward(projected, d_attended, attended, lse, windows, sequences, groups=2):
    low, count, key_ids, query_ids = windows
    rows = projected.shape[0]
    width = projected.shape[1] // 3
    length = rows // sequences
    tiles = length // TILE
    part = width // groups
    pairs = part // PAIR
    query_spec = pl.BlockSpec((TILE, part), lambda s, g, b, *_: (s * tiles + b, g))
    return pl.pallas_call(
        functools.partial(attend_backward_kernel, pairs, tiles),
        grid_spec=pltpu.PrefetchScalarGridSpec(
            num_scalar_prefetch=2,
            grid=(sequences, groups, tiles),
            in_specs=[
                query_spec,
                pl.BlockSpec((length, part), lambda s, g, b, *_: (s, groups + g)),
                pl.BlockSpec((length, part), lambda s, g, b, *_: (s, 2 * groups + g)),
                query_spec,
                query_spec,
                pl.BlockSpec((1, 8, 2 * TILE), lambda s, g, b, *_: (s * tiles + b, 0, 0)),
                pl.BlockSpec((length, TILE), lambda s, g, b, *_: (s, 0)),
                pl.BlockSpec((1, 1, TILE), lambda s, g, b, *_: (s * tiles + b, 0, 0)),
            ],
            out_specs=[
                query_spec,
                pl.BlockSpec((length, part), lambda s, g, b, *_: (s, g)),
                pl.BlockSpec((length, part), lambda s, g, b, *_: (s, g)),
            ],
            scratch_shapes=[pltpu.VMEM((length, part), F32), pltpu.VMEM((length, part), F32)],
        ),
        out_shape=[jax.ShapeDtypeStruct((rows, width), BF)] * 3,
        compiler_params=pltpu.CompilerParams(vmem_limit_bytes=VMEM_LIMIT),
        cost_estimate=pl.CostEstimate(flops=30 * 10**9, bytes_accessed=30 * 10**6, transcendentals=0),
        name="attend_backward",
    )(low, count, projected, projected, projected, d_attended, attended, lse, key_ids, query_ids)


def row_mean(values):
    return jnp.mean(values, axis=-1, keepdims=True)


def fold_rows(values):
    rows, width = values.shape
    return jnp.sum(values.reshape(rows // 8, 8, width), axis=0)


def load_pieces(starts_ref, pieces, targets, sems):
    copies = []
    for n, (piece, target) in enumerate(zip(pieces, targets)):
        height = piece.shape[0]
        start = pl.multiple_of(starts_ref[n], math.gcd(height, 128))
        copies.append(pltpu.make_async_copy(piece, target.at[pl.ds(start, height)], sems.at[n]))
    for copy in copies:
        copy.start()
    for copy in copies:
        copy.wait()


def gelu_parts(values):
    bell = jnp.exp(values * values * -0.5)
    t = 1.0 / (1.0 + jnp.abs(values) * (0.3275911 / math.sqrt(2.0)))
    poly = t * (
        0.5 * 0.254829592
        + t * (0.5 * -0.284496736 + t * (0.5 * 1.421413741 + t * (0.5 * -1.453152027 + t * (0.5 * 1.061405429))))
    )
    tail = poly * bell
    phi = jnp.where(values >= 0.0, 1.0 - tail, tail)
    return values * phi, phi + values * bell * (1.0 / math.sqrt(2.0 * math.pi))


def project_kernel(count, starts_ref, x_ref, bias_ref, *refs):
    pieces = refs[:count]
    o_ref, weight, sems = refs[count:]

    @pl.when(pl.program_id(0) == 0)
    def _():
        load_pieces(starts_ref, pieces, [weight] * count, sems)

    o_ref[...] = (dot_nn(x_ref[...], weight[...]) + bias_ref[...]).astype(BF)


FFN_CHUNK = 512


def layer_forward_kernel(
    counts, starts_ref, x_ref, att_ref, cot_ref, vec_ref, bin_ref, *refs
):
    total = sum(counts)
    pieces = refs[:total]
    (
        out_ref, normed_ref, none_ref, rstd_ref, dsec_ref, hidden_ref, slope_ref, sums_ref,
        w_out, w_in, w_ffo, sems,
    ) = refs[total:]
    targets = [w_out] * counts[0] + [w_in] * counts[1] + [w_ffo] * counts[2]

    @pl.when(pl.program_id(0) == 0)
    def _():
        load_pieces(starts_ref, pieces, targets, sems)
        sums_ref[...] = jnp.zeros_like(sums_ref)

    b_out, gain_one, shift_one, b_ffo, gain_two, shift_two = [vec_ref[i : i + 1, :] for i in range(6)]
    res = x_ref[...].astype(F32) + (dot_nn(att_ref[...], w_out[...]) + b_out)
    center = res - row_mean(res)
    rstd = lax.rsqrt(row_mean(center * center) + epsilon)
    n_one = center * rstd
    normed = (n_one * gain_one + shift_one).astype(BF)
    normed_ref[...] = normed
    none_ref[...] = n_one.astype(BF)
    rstd_ref[...] = jnp.broadcast_to(rstd, rstd_ref.shape)
    hidden_width = w_in.shape[1]
    second = None
    pres = []
    for c in range(0, hidden_width, FFN_CHUNK):
        cols = slice(c, c + FFN_CHUNK)
        pre = dot_nn(normed, w_in[:, cols]) + bin_ref[:, cols]
        value, slope = gelu_parts(pre)
        value = value.astype(BF)
        hidden_ref[:, cols] = value
        slope_ref[:, cols] = slope.astype(BF)
        term = dot_nn(value, w_ffo[cols, :])
        second = term if second is None else second + term
    res = normed.astype(F32) + (second + b_ffo)
    center = res - row_mean(res)
    rstd = lax.rsqrt(row_mean(center * center) + epsilon)
    n_two = center * rstd
    out_ref[...] = (n_two * gain_two + shift_two).astype(BF)
    cot = cot_ref[...].astype(F32)
    inner = cot * gain_two
    d_second = (rstd * (inner - row_mean(inner) - n_two * row_mean(inner * n_two))).astype(BF)
    dsec_ref[...] = d_second
    sums_ref[0:8, :] += fold_rows(cot * n_two)
    sums_ref[8:16, :] += fold_rows(cot)
    sums_ref[16:24, :] += fold_rows(d_second.astype(F32))


def layer_backward_kernel(counts, starts_ref, dsec_ref, slope_ref, none_ref, rstd_ref, vec_ref, *refs):
    total = sum(counts)
    pieces = refs[:total]
    dpre_ref, dbranch_ref, datt_ref, sums_ref, bin_ref, w_out, w_in, w_ffo, sems = refs[total:]
    targets = [w_out] * counts[0] + [w_in] * counts[1] + [w_ffo] * counts[2]

    @pl.when(pl.program_id(0) == 0)
    def _():
        load_pieces(starts_ref, pieces, targets, sems)
        sums_ref[...] = jnp.zeros_like(sums_ref)
        bin_ref[...] = jnp.zeros_like(bin_ref)

    gain_one = vec_ref[1:2, :]
    d_second = dsec_ref[...]
    d_norm = d_second.astype(F32)
    for c in range(0, w_in.shape[1], FFN_CHUNK):
        cols = slice(c, c + FFN_CHUNK)
        d_pre = (dot_nt(d_second, w_ffo[cols, :]) * slope_ref[:, cols].astype(F32)).astype(BF)
        dpre_ref[:, cols] = d_pre
        bin_ref[:, cols] += fold_rows(d_pre.astype(F32))
        d_norm = d_norm + dot_nt(d_pre, w_in[:, cols])
    n_one = none_ref[...].astype(F32)
    inner = d_norm * gain_one
    d_res = rstd_ref[:, 0:1] * (inner - row_mean(inner) - n_one * row_mean(inner * n_one))
    d_branch = d_res.astype(BF)
    dbranch_ref[...] = d_branch
    datt_ref[...] = dot_nt(d_branch, w_out[...]).astype(BF)
    sums_ref[0:8, :] += fold_rows(d_norm * n_one)
    sums_ref[8:16, :] += fold_rows(d_norm)
    sums_ref[16:24, :] += fold_rows(d_branch.astype(F32))


def input_grad_kernel(count, starts_ref, dbranch_ref, dq_ref, dk_ref, dv_ref, *refs):
    pieces = refs[:count]
    o_ref, weight, sems = refs[count:]

    @pl.when(pl.program_id(0) == 0)
    def _():
        load_pieces(starts_ref, pieces, [weight] * count, sems)

    width = dq_ref.shape[1]
    total = dbranch_ref[...].astype(F32)
    for n, ref in enumerate((dq_ref, dk_ref, dv_ref)):
        total = total + dot_nt(ref[...], weight[:, n * width : (n + 1) * width])
    o_ref[...] = total.astype(BF)


def weight_grad_rows_kernel(owner_ref, a_ref, b_ref, keep_ref, pass_ref, send_ref):
    step = pl.program_id(0)
    part = dot_tn(a_ref[...], b_ref[...]).astype(BF)

    @pl.when(step < 2)
    def _():
        send_ref[...] = part

    @pl.when(step == 2)
    def _():
        pass_ref[...] = part

    @pl.when(step == 3)
    def _():
        keep_ref[...] = part


def weight_grad_cols_kernel(slots, owner_ref, a_ref, b_ref, keep_ref, pass_ref, send_ref, held):
    part = dot_tn(a_ref[...], b_ref[...]).astype(BF)
    height = keep_ref.shape[0]
    for owner in range(4):
        held[owner_ref[owner]] = part[owner * height : (owner + 1) * height]
    keep_ref[...] = held[0]
    pass_ref[...] = held[1]
    send_ref[0:height, :] = held[2]
    send_ref[height:, :] = held[3]


PARAMS = pltpu.CompilerParams(vmem_limit_bytes=VMEM_LIMIT)


def cost(flops, bytes_accessed):
    return pl.CostEstimate(flops=int(flops), bytes_accessed=int(bytes_accessed), transcendentals=0)


def whole_spec(array):
    zeros = (0,) * array.ndim
    return pl.BlockSpec(array.shape, lambda *_: zeros)


ANY = pl.BlockSpec(memory_space=pl.ANY)


def row_call(kernel, name, rows, block, scalars, blocked, fixed, pieces, outs, accs, scratch, flops):
    in_specs = (
        [pl.BlockSpec((block, a.shape[1]), lambda i, *_: (i, 0)) for a in blocked]
        + [whole_spec(a) for a in fixed]
        + [ANY] * len(pieces)
    )
    out_specs = [pl.BlockSpec((block, s.shape[1]), lambda i, *_: (i, 0)) for s in outs] + [
        whole_spec(s) for s in accs
    ]
    moved = sum(a.size * a.dtype.itemsize for a in list(blocked) + list(pieces) + list(outs))
    return pl.pallas_call(
        kernel,
        grid_spec=pltpu.PrefetchScalarGridSpec(
            num_scalar_prefetch=1,
            grid=(rows // block,),
            in_specs=in_specs,
            out_specs=out_specs,
            scratch_shapes=list(scratch) + [pltpu.SemaphoreType.DMA((len(pieces),))],
        ),
        out_shape=list(outs) + list(accs),
        compiler_params=PARAMS,
        cost_estimate=cost(flops, moved),
        name=name,
    )(scalars, *blocked, *fixed, *pieces)


def shaped(*shape, dtype=BF):
    return jax.ShapeDtypeStruct(shape, dtype)


def weight_grad(slots, a, b, name):
    rows, height = a.shape
    width = b.shape[1]
    part = height // 4
    flops = 2 * rows * height * width
    moved = 2 * (rows * height + rows * width + height * width)
    if part % 128 == 0:
        return pl.pallas_call(
            weight_grad_rows_kernel,
            grid_spec=pltpu.PrefetchScalarGridSpec(
                num_scalar_prefetch=1,
                grid=(4,),
                in_specs=[
                    pl.BlockSpec((rows, part), lambda t, s: (0, s[4 + t])),
                    pl.BlockSpec((rows, width), lambda t, s: (0, 0)),
                ],
                out_specs=[
                    pl.BlockSpec((part, width), lambda t, s: (0, 0)),
                    pl.BlockSpec((part, width), lambda t, s: (0, 0)),
                    pl.BlockSpec((part, width), lambda t, s: (jnp.minimum(t, 1), 0)),
                ],
            ),
            out_shape=[shaped(part, width), shaped(part, width), shaped(2 * part, width)],
            compiler_params=PARAMS,
            cost_estimate=cost(flops, moved),
            name=name,
        )(slots, a, b)
    block = min(width, 768)
    return pl.pallas_call(
        functools.partial(weight_grad_cols_kernel, 4),
        grid_spec=pltpu.PrefetchScalarGridSpec(
            num_scalar_prefetch=1,
            grid=(width // block,),
            in_specs=[
                pl.BlockSpec((rows, height), lambda t, s: (0, 0)),
                pl.BlockSpec((rows, block), lambda t, s: (0, t)),
            ],
            out_specs=[
                pl.BlockSpec((part, block), lambda t, s: (0, t)),
                pl.BlockSpec((part, block), lambda t, s: (0, t)),
                pl.BlockSpec((2 * part, block), lambda t, s: (0, t)),
            ],
            scratch_shapes=[pltpu.VMEM((4, part, block), BF)],
        ),
        out_shape=[shaped(part, width), shaped(part, width), shaped(2 * part, width)],
        compiler_params=PARAMS,
        cost_estimate=cost(flops, moved),
        name=name,
    )(slots, a, b)


def swap(array, axis, bit):
    size = lax.axis_size(axis)
    return lax.ppermute(array, axis, [(i, i ^ bit) for i in range(size)])


def gather_pieces(shard):
    height = shard.shape[0]
    if lax.axis_size("shard") != 4 or lax.axis_size("rep") % 2:
        return [(lax.all_gather(shard, "shard", axis=0, tiled=True), jnp.int32(0))]
    me = lax.axis_index("shard")
    side = lax.rem(lax.axis_index("rep"), 2)
    half = height // 2
    mine = lax.dynamic_slice_in_dim(shard, side * half, half, axis=0)
    direct = swap(mine, "shard", 2)
    relayed = swap(direct, "rep", 1)
    near = me * height
    core = (me ^ 1) * height
    far = (me ^ 2) * height
    cross = (me ^ 3) * height
    return [
        (shard, near),
        (swap(shard, "shard", 1), core),
        (direct, far + side * half),
        (relayed, far + (1 - side) * half),
        (swap(direct, "shard", 1), cross + side * half),
        (swap(relayed, "shard", 1), cross + (1 - side) * half),
    ]


def added(*terms):
    return functools.reduce(jnp.add, [t.astype(F32) for t in terms]).astype(BF)


def reduce_owned(parts):
    keep, passed, sent = parts
    height = keep.shape[0]
    come = swap(sent, "shard", 1)
    onward = swap(added(passed, come[height:]), "shard", 2)
    owned = added(keep, come[:height], onward)
    place = lax.axis_index("rep")
    half, quarter = height // 2, height // 4
    y = lax.rem(place, 2)
    z = lax.rem(place // 2, 2)
    away = lax.dynamic_slice_in_dim(owned, (1 - y) * half, half, axis=0)
    stay = lax.dynamic_slice_in_dim(owned, y * half, half, axis=0)
    stay = added(stay, swap(away, "rep", 1))
    away = lax.dynamic_slice_in_dim(stay, (1 - z) * quarter, quarter, axis=0)
    stay = lax.dynamic_slice_in_dim(stay, z * quarter, quarter, axis=0)
    stay = added(stay, swap(away, "rep", 2))
    stay = added(stay, swap(stay, "rep", 4))
    other = swap(stay, "rep", 2)
    pair = jnp.where(z == 0, jnp.stack([stay, other]), jnp.stack([other, stay])).reshape(half, -1)
    other = swap(pair, "rep", 1)
    both = jnp.where(y == 0, jnp.stack([pair, other]), jnp.stack([other, pair])).reshape(height, -1)
    return both.astype(F32)


def reduce_plain(a, b):
    grad = dot_tn(a, b).astype(BF)
    owned = lax.psum_scatter(grad, "shard", scatter_dimension=0, tiled=True)
    return lax.psum(owned, "rep").astype(F32)


def local(
    tokens,
    segment_ids,
    cotangent,
    w_qkv,
    b_query,
    b_value,
    w_out,
    b_out,
    gain_one,
    shift_one,
    w_in,
    b_in,
    w_ffo,
    b_ffo,
    gain_two,
    shift_two,
):
    micro, sequences, length, width = tokens.shape
    total = micro * sequences
    rows = total * length
    group = lax.axis_size("shard")
    hidden_width = w_in.shape[1]
    x = tokens.reshape(rows, width)
    seg = segment_ids.reshape(total, length)
    cot = cotangent.reshape(rows, width)
    me = lax.axis_index("shard")
    direct = group == 4 and lax.axis_size("rep") == 8

    part = b_query.shape[0]
    small_shards = (b_query, b_value, b_out, gain_one, shift_one, b_ffo, gain_two, shift_two, b_in)
    small = jnp.concatenate(small_shards).reshape(1, -1)
    if direct:
        near = swap(small, "shard", 1)
        pair = jnp.concatenate([small, near], axis=0)
        four = jnp.concatenate([pair, swap(pair, "shard", 2)], axis=0)
        order = [jnp.bitwise_xor(me, o) for o in range(4)]
        small_full = jnp.concatenate([lax.dynamic_slice_in_dim(four, o, 1, axis=0) for o in order], axis=0)
    else:
        small_full = lax.all_gather(small, "shard", axis=0, tiled=True)
    small_full = small_full.astype(F32)
    vectors = [small_full[:, i * part : (i + 1) * part].reshape(1, -1) for i in range(8)]
    bias_all = jnp.concatenate([vectors[0], jnp.zeros_like(vectors[0]), vectors[1]], axis=1)
    vec = jnp.concatenate(vectors[2:] + [jnp.zeros((2, width), F32)], axis=0)
    bias_in = small_full[:, 8 * part :].reshape(1, -1)

    qkv_pieces = gather_pieces(w_qkv)
    out_pieces = gather_pieces(w_out)
    in_pieces = gather_pieces(w_in)
    ffo_pieces = gather_pieces(w_ffo)

    def arrays(pieces):
        return [p[0] for p in pieces]

    def starts(pieces):
        return jnp.stack([jnp.asarray(p[1], jnp.int32) for p in pieces])

    windows = windows_of(seg)
    block = 256
    qkv_starts = starts(qkv_pieces)
    (projected,) = row_call(
        functools.partial(project_kernel, len(qkv_pieces)),
        "project",
        rows,
        block,
        qkv_starts,
        [x],
        [bias_all],
        arrays(qkv_pieces),
        [shaped(rows, 3 * width)],
        [],
        [pltpu.VMEM((width, 3 * width), BF)],
        6 * rows * width * width,
    )
    attended, lse = attend_forward(projected, windows, total)
    layer_pieces = out_pieces + in_pieces + ffo_pieces
    counts = (len(out_pieces), len(in_pieces), len(ffo_pieces))
    layer_starts = starts(layer_pieces)
    weights_scratch = [
        pltpu.VMEM((width, width), BF),
        pltpu.VMEM((width, hidden_width), BF),
        pltpu.VMEM((hidden_width, width), BF),
    ]
    layer_flops = 2 * rows * width * (width + 2 * hidden_width)
    output, normed, n_one, rstd_one, d_second, hidden, slope, sums_two = row_call(
        functools.partial(layer_forward_kernel, counts),
        "layer_forward",
        rows,
        block,
        layer_starts,
        [x, attended, cot],
        [vec, bias_in],
        arrays(layer_pieces),
        [
            shaped(rows, width),
            shaped(rows, width),
            shaped(rows, width),
            shaped(rows, 128, dtype=F32),
            shaped(rows, width),
            shaped(rows, hidden_width),
            shaped(rows, hidden_width),
        ],
        [shaped(24, width, dtype=F32)],
        weights_scratch,
        layer_flops,
    )

    place = [jnp.bitwise_xor(me, o) for o in range(4)]
    slots = jnp.stack(
        [(p % 2) * 2 + p // 2 for p in place] + [jnp.bitwise_xor(me, j) for j in (1, 3, 2, 0)]
    ).astype(jnp.int32)

    def weight_terms(a, b, name):
        if direct:
            return reduce_owned(weight_grad(slots, a, b, name))
        return reduce_plain(a, b)

    grad_ffo = weight_terms(hidden, d_second, "grad_ffo")
    d_pre, d_branch, d_attended, sums_one, sums_in = row_call(
        functools.partial(layer_backward_kernel, counts),
        "layer_backward",
        rows,
        block,
        layer_starts,
        [d_second, slope, n_one, rstd_one],
        [vec],
        arrays(layer_pieces),
        [shaped(rows, hidden_width), shaped(rows, width), shaped(rows, width)],
        [shaped(24, width, dtype=F32), shaped(8, hidden_width, dtype=F32)],
        weights_scratch,
        layer_flops,
    )
    grad_in = weight_terms(normed, d_pre, "grad_in")
    grad_out = weight_terms(attended, d_branch, "grad_out")
    dq, dk, dv = attend_backward(projected, d_attended, attended, lse, windows, total)
    grad_q = weight_terms(x, dq, "grad_q")
    grad_k = weight_terms(x, dk, "grad_k")
    grad_v = weight_terms(x, dv, "grad_v")
    (d_tokens,) = row_call(
        functools.partial(input_grad_kernel, len(qkv_pieces)),
        "input_grad",
        rows,
        block,
        qkv_starts,
        [d_branch, dq, dk, dv],
        [],
        arrays(qkv_pieces),
        [shaped(rows, width)],
        [],
        [pltpu.VMEM((width, 3 * width), BF)],
        6 * rows * width * width,
    )
    d_query_bias = jnp.sum(dq.astype(F32), axis=0)
    d_value_bias = jnp.sum(dv.astype(F32), axis=0)

    def folded(sums):
        return [jnp.sum(sums[i : i + 8], axis=0) for i in range(0, sums.shape[0], 8)]

    d_gain_two, d_shift_two, d_ffo_bias = folded(sums_two)
    d_gain_one, d_shift_one, d_out_bias = folded(sums_one)
    (d_in_bias,) = folded(sums_in)
    smalls = (
        d_query_bias, d_value_bias, d_out_bias, d_gain_one, d_shift_one, d_ffo_bias, d_gain_two, d_shift_two,
        d_in_bias,
    )
    packed = jnp.concatenate([s.reshape(group, -1) for s in smalls], axis=1)
    if direct:
        for axis, bit in (("shard", 1), ("shard", 2), ("rep", 1), ("rep", 2), ("rep", 4)):
            packed = packed + swap(packed, axis, bit)
    else:
        packed = lax.psum(packed, ("shard", "rep"))
    mine = lax.dynamic_index_in_dim(packed, me, 0, keepdims=False)
    sm = [mine[i * part : (i + 1) * part] for i in range(8)]
    gqb, gvb, gob, gg1, gs1, gfb, gg2, gs2 = sm
    gib = mine[8 * part :]
    return (
        output.reshape(tokens.shape),
        d_tokens.reshape(tokens.shape),
        jnp.concatenate([grad_q, grad_k, grad_v], axis=1),
        gqb,
        gvb,
        grad_out,
        gob,
        gg1,
        gs1,
        grad_in,
        gib,
        grad_ffo,
        gfb,
        gg2,
        gs2,
    )


def solution(mesh):
    data = P(None, ("shard", "rep"), None, None)
    matrix = P("shard", None)
    vector = P("shard")
    return jax.shard_map(
        local,
        mesh=mesh,
        in_specs=(
            data,
            P(None, ("shard", "rep"), None),
            data,
            matrix,
            vector,
            vector,
            matrix,
            vector,
            vector,
            vector,
            matrix,
            vector,
            matrix,
            vector,
            vector,
            vector,
        ),
        out_specs=(
            data,
            data,
            matrix,
            vector,
            vector,
            matrix,
            vector,
            vector,
            vector,
            matrix,
            vector,
            matrix,
            vector,
            vector,
            vector,
        ),
        check_vma=False,
    )
```

```python
import functools
import math

import jax
import jax.numpy as jnp
from jax import lax
from jax.experimental import pallas as pl
from jax.experimental.pallas import tpu as pltpu
from jax.sharding import PartitionSpec as P

HEADS = 12
HEAD_DIM = 64
PAIR = 2 * HEAD_DIM
TILE = 128

epsilon = 1e-05
masked_score = -1e30
BF = jnp.bfloat16
F32 = jnp.float32
VMEM_LIMIT = 60 * 2**20


def dot_nn(a, b):
    return lax.dot_general(a, b, (((1,), (0,)), ((), ())), preferred_element_type=F32)


def dot_nt(a, b):
    return lax.dot_general(a, b, (((1,), (1,)), ((), ())), preferred_element_type=F32)


def dot_tn(a, b):
    return lax.dot_general(a, b, (((0,), (0,)), ((), ())), preferred_element_type=F32)


def head_rows(value):
    lane = lax.broadcasted_iota(jnp.int32, (1, PAIR), 1)
    first = jnp.where(lane < HEAD_DIM, value, 0.0).astype(BF)
    second = jnp.where(lane < HEAD_DIM, 0.0, value).astype(BF)
    return first, second


def stack_heads(block, rows):
    return jnp.concatenate([block * rows[0], block * rows[1]], axis=0)


def diagonal_back(transposed):
    kept = jnp.concatenate(
        [transposed[:HEAD_DIM, :TILE], transposed[HEAD_DIM:, TILE:]], axis=0
    )
    return kept.T


def for_windows(count, tiles, body):
    sizes = [t for t in range(1, tiles + 1) if t < 7 or t == tiles]
    below = 0
    for size in sizes:
        @pl.when((count > below) & (count <= size))
        def _(size=size):
            body(size)

        below = size


def attend_forward_kernel(pairs, tiles, low_ref, count_ref, q_ref, k_ref, v_ref, kseg_ref, qseg_ref, o_ref, lse_ref):
    place = pl.program_id(0) * tiles + pl.program_id(1)
    low = low_ref[place]
    count = count_ref[place]
    rows_of = head_rows(1.0 / math.sqrt(HEAD_DIM))

    def window(size):
        start = jnp.minimum(low, tiles - size) * TILE
        chunks = [pl.ds(pl.multiple_of(start + c * TILE, TILE), TILE) for c in range(size)]
        whole = pl.ds(pl.multiple_of(start, TILE), size * TILE)
        masks = [kseg_ref[c, :] == qseg_ref[0] for c in chunks]
        for p in range(pairs):
            lanes = slice(p * PAIR, (p + 1) * PAIR)
            queries = stack_heads(q_ref[:, lanes], rows_of)
            scores = []
            for c, mask in zip(chunks, masks):
                part = dot_nt(k_ref[c, lanes], queries)
                scores.append(
                    jnp.concatenate(
                        [
                            jnp.where(mask, part[:, :TILE], masked_score),
                            jnp.where(mask, part[:, TILE:], masked_score),
                        ],
                        axis=1,
                    )
                )
            top = functools.reduce(jnp.maximum, [jnp.max(s, axis=0, keepdims=True) for s in scores])
            exps = [jnp.exp(s - top) for s in scores]
            total = functools.reduce(jnp.add, [jnp.sum(e, axis=0, keepdims=True) for e in exps])
            weights = jnp.concatenate([e.astype(BF) for e in exps], axis=0)
            mixed = dot_tn(v_ref[whole, lanes], weights) / total
            o_ref[:, lanes] = diagonal_back(mixed).astype(BF)
            lse_ref[0, p : p + 1, :] = top + jnp.log(total)

    for_windows(count, tiles, window)


def attend_backward_kernel(
    pairs, tiles, low_ref, count_ref, q_ref, k_ref, v_ref, do_ref, o_ref, lse_ref, kseg_ref, qseg_ref,
    out_ref, dk_acc, dv_acc, *, first_pair,
):
    block = pl.program_id(1)
    place = pl.program_id(0) * tiles + block
    low = low_ref[place]
    count = count_ref[place]
    part = pairs * PAIR
    scale = 1.0 / math.sqrt(HEAD_DIM)
    scaled_rows = head_rows(scale)
    plain_rows = head_rows(1.0)

    @pl.when(block == 0)
    def _():
        dk_acc[...] = jnp.zeros_like(dk_acc)
        dv_acc[...] = jnp.zeros_like(dv_acc)

    def window(size):
        start = jnp.minimum(low, tiles - size) * TILE
        chunks = [pl.ds(pl.multiple_of(start + c * TILE, TILE), TILE) for c in range(size)]
        whole = pl.ds(pl.multiple_of(start, TILE), size * TILE)
        masks = [kseg_ref[c, :] == qseg_ref[0] for c in chunks]
        mine = pl.ds(pl.multiple_of(block * TILE, TILE), TILE)
        for p in range(pairs):
            lanes = slice(p * PAIR, (p + 1) * PAIR)
            queries = stack_heads(q_ref[:, lanes], scaled_rows)
            grads = do_ref[:, lanes]
            stacked = stack_heads(grads, plain_rows)
            product = (grads.astype(F32) * o_ref[:, lanes].astype(F32)).T
            row_dot = jnp.concatenate(
                [
                    jnp.sum(product[:HEAD_DIM], axis=0, keepdims=True),
                    jnp.sum(product[HEAD_DIM:], axis=0, keepdims=True),
                ],
                axis=1,
            )
            lse = lse_ref[0, first_pair + p : first_pair + p + 1, :]
            kept = []
            for c, mask in zip(chunks, masks):
                part_scores = dot_nt(k_ref[c, lanes], queries) - lse
                d_probs = dot_nt(v_ref[c, lanes], stacked)
                probs = jnp.exp(
                    jnp.concatenate(
                        [
                            jnp.where(mask, part_scores[:, :TILE], masked_score),
                            jnp.where(mask, part_scores[:, TILE:], masked_score),
                        ],
                        axis=1,
                    )
                )
                d_scores = (probs * (d_probs - row_dot)).astype(BF)
                kept.append(d_scores)
                dv_acc[c, lanes] += dot_nn(probs.astype(BF), stacked)
                dk_acc[c, lanes] += dot_nn(d_scores, queries)
            mixed = dot_tn(k_ref[whole, lanes], jnp.concatenate(kept, axis=0)) * scale
            out_ref[mine, lanes] = diagonal_back(mixed).astype(BF)

    for_windows(count, tiles, window)

    @pl.when(block == tiles - 1)
    def _():
        out_ref[:, part : 2 * part] = dk_acc[...].astype(BF)
        out_ref[:, 2 * part :] = dv_acc[...].astype(BF)


def windows_of(segments):
    sequences, length = segments.shape
    tiles = length // TILE
    blocked = segments.reshape(sequences, tiles, TILE)
    first = blocked[:, :, 0]
    last = blocked[:, :, TILE - 1]
    starts = jnp.sum((segments[:, None, :] < first[:, :, None]).astype(jnp.int32), axis=-1)
    ends = jnp.sum((segments[:, None, :] <= last[:, :, None]).astype(jnp.int32), axis=-1)
    bits = TILE.bit_length() - 1
    low = lax.shift_right_logical(starts, bits)
    count = lax.shift_right_logical(ends + TILE - 1, bits) - low
    key_ids = jnp.broadcast_to(segments.reshape(sequences * length, 1), (sequences * length, TILE))
    query_ids = blocked.reshape(sequences * tiles, 1, TILE)
    return low.reshape(-1), count.reshape(-1), key_ids, query_ids


def attend_forward(projected, windows, sequences):
    low, count, key_ids, query_ids = windows
    rows = projected.shape[0]
    width = projected.shape[1] // 3
    length = rows // sequences
    tiles = length // TILE
    pairs = width // PAIR
    return pl.pallas_call(
        functools.partial(attend_forward_kernel, pairs, tiles),
        grid_spec=pltpu.PrefetchScalarGridSpec(
            num_scalar_prefetch=2,
            grid=(sequences, tiles),
            in_specs=[
                pl.BlockSpec((TILE, width), lambda s, b, *_: (s * tiles + b, 0)),
                pl.BlockSpec((length, width), lambda s, b, *_: (s, 1)),
                pl.BlockSpec((length, width), lambda s, b, *_: (s, 2)),
                pl.BlockSpec((length, TILE), lambda s, b, *_: (s, 0)),
                pl.BlockSpec((1, 1, TILE), lambda s, b, *_: (s * tiles + b, 0, 0)),
            ],
            out_specs=[
                pl.BlockSpec((TILE, width), lambda s, b, *_: (s * tiles + b, 0)),
                pl.BlockSpec((1, 8, 2 * TILE), lambda s, b, *_: (s * tiles + b, 0, 0)),
            ],
        ),
        out_shape=[
            jax.ShapeDtypeStruct((rows, width), BF),
            jax.ShapeDtypeStruct((sequences * tiles, 8, 2 * TILE), F32),
        ],
        compiler_params=pltpu.CompilerParams(vmem_limit_bytes=VMEM_LIMIT),
        cost_estimate=cost(8 * 10**9, 16 * 10**6),
        name="attend_forward",
    )(low, count, projected, projected, projected, key_ids, query_ids)


def attend_backward(projected, d_attended, attended, lse, windows, sequences, group, groups):
    low, count, key_ids, query_ids = windows
    rows = projected.shape[0]
    width = projected.shape[1] // 3
    length = rows // sequences
    tiles = length // TILE
    part = width // groups
    pairs = part // PAIR
    query_spec = pl.BlockSpec((TILE, part), lambda s, b, *_: (s * tiles + b, group))
    return pl.pallas_call(
        functools.partial(attend_backward_kernel, pairs, tiles, first_pair=group * pairs),
        grid_spec=pltpu.PrefetchScalarGridSpec(
            num_scalar_prefetch=2,
            grid=(sequences, tiles),
            in_specs=[
                query_spec,
                pl.BlockSpec((length, part), lambda s, b, *_: (s, groups + group)),
                pl.BlockSpec((length, part), lambda s, b, *_: (s, 2 * groups + group)),
                query_spec,
                query_spec,
                pl.BlockSpec((1, 8, 2 * TILE), lambda s, b, *_: (s * tiles + b, 0, 0)),
                pl.BlockSpec((length, TILE), lambda s, b, *_: (s, 0)),
                pl.BlockSpec((1, 1, TILE), lambda s, b, *_: (s * tiles + b, 0, 0)),
            ],
            out_specs=pl.BlockSpec((length, 3 * part), lambda s, b, *_: (s, 0)),
            scratch_shapes=[pltpu.VMEM((length, part), F32), pltpu.VMEM((length, part), F32)],
        ),
        out_shape=jax.ShapeDtypeStruct((rows, 3 * part), BF),
        compiler_params=pltpu.CompilerParams(vmem_limit_bytes=VMEM_LIMIT),
        cost_estimate=cost(30 * 10**9 // groups, 30 * 10**6 // groups),
        name="attend_backward",
    )(low, count, projected, projected, projected, d_attended, attended, lse, key_ids, query_ids)


def row_mean(values):
    return jnp.mean(values, axis=-1, keepdims=True)


def fold_rows(values):
    rows, width = values.shape
    return jnp.sum(values.reshape(rows // 8, 8, width), axis=0)


def load_pieces(starts_ref, pieces, targets, sems):
    copies = []
    for n, (piece, target) in enumerate(zip(pieces, targets)):
        height = piece.shape[0]
        start = pl.multiple_of(starts_ref[n], math.gcd(height, 128))
        copies.append(pltpu.make_async_copy(piece, target.at[pl.ds(start, height)], sems.at[n]))
    for copy in copies:
        copy.start()
    for copy in copies:
        copy.wait()


def gelu_parts(values):
    bell = jnp.exp(values * values * -0.5)
    t = 1.0 / (1.0 + jnp.abs(values) * (0.3275911 / math.sqrt(2.0)))
    poly = t * (
        0.5 * 0.254829592
        + t * (0.5 * -0.284496736 + t * (0.5 * 1.421413741 + t * (0.5 * -1.453152027 + t * (0.5 * 1.061405429))))
    )
    tail = poly * bell
    phi = jnp.where(values >= 0.0, 1.0 - tail, tail)
    return values * phi, phi + values * bell * (1.0 / math.sqrt(2.0 * math.pi))


def project_kernel(count, starts_ref, x_ref, bias_ref, *refs):
    pieces = refs[:count]
    o_ref, weight, sems = refs[count:]

    @pl.when(pl.program_id(0) == 0)
    def _():
        load_pieces(starts_ref, pieces, [weight] * count, sems)

    o_ref[...] = (dot_nn(x_ref[...], weight[...]) + bias_ref[...]).astype(BF)


FFN_CHUNK = 512


def layer_forward_kernel(
    counts, starts_ref, x_ref, att_ref, cot_ref, vec_ref, bin_ref, *refs
):
    total = sum(counts)
    pieces = refs[:total]
    (
        out_ref, normed_ref, none_ref, rstd_ref, dsec_ref, hidden_ref, slope_ref, sums_ref,
        w_out, w_in, w_ffo, sems,
    ) = refs[total:]
    targets = [w_out] * counts[0] + [w_in] * counts[1] + [w_ffo] * counts[2]

    @pl.when(pl.program_id(0) == 0)
    def _():
        load_pieces(starts_ref, pieces, targets, sems)
        sums_ref[...] = jnp.zeros_like(sums_ref)

    b_out, gain_one, shift_one, b_ffo, gain_two, shift_two = [vec_ref[i : i + 1, :] for i in range(6)]
    res = x_ref[...].astype(F32) + (dot_nn(att_ref[...], w_out[...]) + b_out)
    center = res - row_mean(res)
    rstd = lax.rsqrt(row_mean(center * center) + epsilon)
    n_one = center * rstd
    normed = (n_one * gain_one + shift_one).astype(BF)
    normed_ref[...] = normed
    none_ref[...] = n_one.astype(BF)
    rstd_ref[...] = jnp.broadcast_to(rstd, rstd_ref.shape)
    hidden_width = w_in.shape[1]
    second = None
    pres = []
    for c in range(0, hidden_width, FFN_CHUNK):
        cols = slice(c, c + FFN_CHUNK)
        pre = dot_nn(normed, w_in[:, cols]) + bin_ref[:, cols]
        value, slope = gelu_parts(pre)
        value = value.astype(BF)
        hidden_ref[:, cols] = value
        slope_ref[:, cols] = slope.astype(BF)
        term = dot_nn(value, w_ffo[cols, :])
        second = term if second is None else second + term
    res = normed.astype(F32) + (second + b_ffo)
    center = res - row_mean(res)
    rstd = lax.rsqrt(row_mean(center * center) + epsilon)
    n_two = center * rstd
    out_ref[...] = (n_two * gain_two + shift_two).astype(BF)
    cot = cot_ref[...].astype(F32)
    inner = cot * gain_two
    d_second = (rstd * (inner - row_mean(inner) - n_two * row_mean(inner * n_two))).astype(BF)
    dsec_ref[...] = d_second
    sums_ref[0:8, :] += fold_rows(cot * n_two)
    sums_ref[8:16, :] += fold_rows(cot)
    sums_ref[16:24, :] += fold_rows(d_second.astype(F32))


def layer_backward_kernel(counts, starts_ref, dsec_ref, slope_ref, none_ref, rstd_ref, vec_ref, *refs):
    total = sum(counts)
    pieces = refs[:total]
    dpre_ref, dbranch_ref, datt_ref, sums_ref, bin_ref, w_out, w_in, w_ffo, sems = refs[total:]
    targets = [w_out] * counts[0] + [w_in] * counts[1] + [w_ffo] * counts[2]

    @pl.when(pl.program_id(0) == 0)
    def _():
        load_pieces(starts_ref, pieces, targets, sems)
        sums_ref[...] = jnp.zeros_like(sums_ref)
        bin_ref[...] = jnp.zeros_like(bin_ref)

    gain_one = vec_ref[1:2, :]
    d_second = dsec_ref[...]
    d_norm = d_second.astype(F32)
    for c in range(0, w_in.shape[1], FFN_CHUNK):
        cols = slice(c, c + FFN_CHUNK)
        d_pre = (dot_nt(d_second, w_ffo[cols, :]) * slope_ref[:, cols].astype(F32)).astype(BF)
        dpre_ref[:, cols] = d_pre
        bin_ref[:, cols] += fold_rows(d_pre.astype(F32))
        d_norm = d_norm + dot_nt(d_pre, w_in[:, cols])
    n_one = none_ref[...].astype(F32)
    inner = d_norm * gain_one
    d_res = rstd_ref[:, 0:1] * (inner - row_mean(inner) - n_one * row_mean(inner * n_one))
    d_branch = d_res.astype(BF)
    dbranch_ref[...] = d_branch
    datt_ref[...] = dot_nt(d_branch, w_out[...]).astype(BF)
    sums_ref[0:8, :] += fold_rows(d_norm * n_one)
    sums_ref[8:16, :] += fold_rows(d_norm)
    sums_ref[16:24, :] += fold_rows(d_branch.astype(F32))


def input_grad_kernel(count, groups, starts_ref, dbranch_ref, *refs):
    grads = refs[:groups]
    pieces = refs[groups : groups + count]
    o_ref, weight, sems = refs[groups + count :]

    @pl.when(pl.program_id(0) == 0)
    def _():
        load_pieces(starts_ref, pieces, [weight] * count, sems)

    width = dbranch_ref.shape[1]
    part = width // groups
    total = dbranch_ref[...].astype(F32)
    for g, ref in enumerate(grads):
        for n in range(3):
            first = n * width + g * part
            total = total + dot_nt(ref[:, n * part : (n + 1) * part], weight[:, first : first + part])
    o_ref[...] = total.astype(BF)


def weight_grad_rows_kernel(owner_ref, a_ref, b_ref, keep_ref, pass_ref, send_ref):
    step = pl.program_id(0)
    part = dot_tn(a_ref[...], b_ref[...]).astype(BF)

    @pl.when(step < 2)
    def _():
        send_ref[...] = part

    @pl.when(step == 2)
    def _():
        pass_ref[...] = part

    @pl.when(step == 3)
    def _():
        keep_ref[...] = part


def weight_grad_cols_kernel(slots, owner_ref, a_ref, b_ref, keep_ref, pass_ref, send_ref, sums_ref, held):
    terms = b_ref[...]
    sums_ref[...] = fold_rows(terms.astype(F32))
    part = dot_tn(a_ref[...], terms).astype(BF)
    height = keep_ref.shape[0]
    for owner in range(4):
        held[owner_ref[owner]] = part[owner * height : (owner + 1) * height]
    keep_ref[...] = held[0]
    pass_ref[...] = held[1]
    send_ref[0:height, :] = held[2]
    send_ref[height:, :] = held[3]


PARAMS = pltpu.CompilerParams(vmem_limit_bytes=VMEM_LIMIT)


def cost(flops, bytes_accessed):
    return pl.CostEstimate(flops=int(flops) // 16, bytes_accessed=int(bytes_accessed) // 16, transcendentals=0)


def whole_spec(array):
    zeros = (0,) * array.ndim
    return pl.BlockSpec(array.shape, lambda *_: zeros)


ANY = pl.BlockSpec(memory_space=pl.ANY)


def row_call(kernel, name, rows, block, scalars, blocked, fixed, pieces, outs, accs, scratch, flops):
    in_specs = (
        [pl.BlockSpec((block, a.shape[1]), lambda i, *_: (i, 0)) for a in blocked]
        + [whole_spec(a) for a in fixed]
        + [ANY] * len(pieces)
    )
    out_specs = [pl.BlockSpec((block, s.shape[1]), lambda i, *_: (i, 0)) for s in outs] + [
        whole_spec(s) for s in accs
    ]
    moved = sum(a.size * a.dtype.itemsize for a in list(blocked) + list(pieces) + list(outs))
    return pl.pallas_call(
        kernel,
        grid_spec=pltpu.PrefetchScalarGridSpec(
            num_scalar_prefetch=1,
            grid=(rows // block,),
            in_specs=in_specs,
            out_specs=out_specs,
            scratch_shapes=list(scratch) + [pltpu.SemaphoreType.DMA((len(pieces),))],
        ),
        out_shape=list(outs) + list(accs),
        compiler_params=PARAMS,
        cost_estimate=cost(flops, moved),
        name=name,
    )(scalars, *blocked, *fixed, *pieces)


def shaped(*shape, dtype=BF):
    return jax.ShapeDtypeStruct(shape, dtype)


def weight_grad(slots, a, b, name):
    rows, height = a.shape
    width = b.shape[1]
    part = height // 4
    flops = 2 * rows * height * width
    moved = 2 * (rows * height + rows * width + height * width)
    if part % 128 == 0:
        return pl.pallas_call(
            weight_grad_rows_kernel,
            grid_spec=pltpu.PrefetchScalarGridSpec(
                num_scalar_prefetch=1,
                grid=(4,),
                in_specs=[
                    pl.BlockSpec((rows, part), lambda t, s: (0, s[4 + t])),
                    pl.BlockSpec((rows, width), lambda t, s: (0, 0)),
                ],
                out_specs=[
                    pl.BlockSpec((part, width), lambda t, s: (0, 0)),
                    pl.BlockSpec((part, width), lambda t, s: (0, 0)),
                    pl.BlockSpec((part, width), lambda t, s: (jnp.minimum(t, 1), 0)),
                ],
            ),
            out_shape=[shaped(part, width), shaped(part, width), shaped(2 * part, width)],
            compiler_params=PARAMS,
            cost_estimate=cost(flops, moved),
            name=name,
        )(slots, a, b)
    block = min(width, 768)
    return pl.pallas_call(
        functools.partial(weight_grad_cols_kernel, 4),
        grid_spec=pltpu.PrefetchScalarGridSpec(
            num_scalar_prefetch=1,
            grid=(width // block,),
            in_specs=[
                pl.BlockSpec((rows, height), lambda t, s: (0, 0)),
                pl.BlockSpec((rows, block), lambda t, s: (0, t)),
            ],
            out_specs=[
                pl.BlockSpec((part, block), lambda t, s: (0, t)),
                pl.BlockSpec((part, block), lambda t, s: (0, t)),
                pl.BlockSpec((2 * part, block), lambda t, s: (0, t)),
                pl.BlockSpec((8, block), lambda t, s: (0, t)),
            ],
            scratch_shapes=[pltpu.VMEM((4, part, block), BF)],
        ),
        out_shape=[
            shaped(part, width),
            shaped(part, width),
            shaped(2 * part, width),
            shaped(8, width, dtype=F32),
        ],
        compiler_params=PARAMS,
        cost_estimate=cost(flops, moved),
        name=name,
    )(slots, a, b)


def swap(array, axis, bit):
    size = lax.axis_size(axis)
    return lax.ppermute(array, axis, [(i, i ^ bit) for i in range(size)])


def gather_hops(shards):
    side = lax.axis_index("rep") & 1
    halves = [s.shape[0] // 2 for s in shards]
    mine = [lax.dynamic_slice_in_dim(s, side * h, h, axis=0) for s, h in zip(shards, halves)]
    direct, core = yield [swap(m, "shard", 2) for m in mine], [swap(s, "shard", 1) for s in shards]
    relayed, cross = yield [swap(d, "rep", 1) for d in direct], [swap(d, "shard", 1) for d in direct]
    cross_relayed = yield [swap(r, "shard", 1) for r in relayed]
    return [list(p) for p in zip(shards, core, direct, relayed, cross, cross_relayed)]


def piece_starts(shard):
    height = shard.shape[0]
    me = lax.axis_index("shard")
    side = lax.axis_index("rep") & 1
    half = height // 2
    near, core, far, cross = [(me ^ o) * height for o in range(4)]
    return [near, core, far + side * half, far + (1 - side) * half, cross + side * half, cross + (1 - side) * half]


def added(*terms):
    return functools.reduce(jnp.add, [t.astype(F32) for t in terms]).astype(BF)


def reduce_hops(parts):
    keep, passed, sent = parts
    height = keep.shape[0]
    come = yield swap(sent, "shard", 1)
    onward = yield swap(added(passed, come[height:]), "shard", 2)
    owned = added(keep, come[:height], onward)
    place = lax.axis_index("rep")
    half, quarter = height // 2, height // 4
    y = place & 1
    z = lax.shift_right_logical(place, 1) & 1
    away = lax.dynamic_slice_in_dim(owned, (1 - y) * half, half, axis=0)
    stay = lax.dynamic_slice_in_dim(owned, y * half, half, axis=0)
    stay = added(stay, (yield swap(away, "rep", 1)))
    away = lax.dynamic_slice_in_dim(stay, (1 - z) * quarter, quarter, axis=0)
    stay = lax.dynamic_slice_in_dim(stay, z * quarter, quarter, axis=0)
    stay = added(stay, (yield swap(away, "rep", 2)))
    stay = added(stay, (yield swap(stay, "rep", 4)))
    other = yield swap(stay, "rep", 2)
    pair = jnp.where(z == 0, jnp.stack([stay, other]), jnp.stack([other, stay])).reshape(half, -1)
    other = yield swap(pair, "rep", 1)
    both = jnp.where(y == 0, jnp.stack([pair, other]), jnp.stack([other, pair])).reshape(height, -1)
    return both.astype(F32)


def reduce_small(packed):
    for axis, bit in (("shard", 1), ("shard", 2), ("rep", 1), ("rep", 2), ("rep", 4)):
        packed = packed + (yield swap(packed, axis, bit))
    return packed


class Flow:
    def __init__(self, hops):
        self.hops = hops
        self.result = None
        self.flying = next(hops)

    def land(self, arrived):
        try:
            self.flying = self.hops.send(arrived)
        except StopIteration as stop:
            self.flying, self.result = None, stop.value


class Line:
    def __init__(self):
        self.flows = []
        self.recent = []

    def step(self, arrays, flows=None):
        moving = [f for f in (self.flows if flows is None else flows) if f.flying is not None]
        held = self.recent
        arrays, arrived, held = lax.optimization_barrier((arrays, [f.flying for f in moving], held))
        for flow, value in zip(moving, arrived):
            flow.land(value)
        self.recent = []
        return arrays

    def start(self, hops):
        flow = Flow(hops)
        self.flows.append(flow)
        return flow


def reduce_plain(a, b):
    grad = dot_tn(a, b).astype(BF)
    owned = lax.psum_scatter(grad, "shard", scatter_dimension=0, tiled=True)
    return lax.psum(owned, "rep").astype(F32)


def local(
    tokens,
    segment_ids,
    cotangent,
    w_qkv,
    b_query,
    b_value,
    w_out,
    b_out,
    gain_one,
    shift_one,
    w_in,
    b_in,
    w_ffo,
    b_ffo,
    gain_two,
    shift_two,
):
    micro, sequences, length, width = tokens.shape
    total = micro * sequences
    rows = total * length
    group = lax.axis_size("shard")
    hidden_width = w_in.shape[1]
    x = tokens.reshape(rows, width)
    seg = segment_ids.reshape(total, length)
    cot = cotangent.reshape(rows, width)
    me = lax.axis_index("shard")
    direct = group == 4 and lax.axis_size("rep") == 8

    part = b_query.shape[0]
    line = Line()
    small_shards = (b_query, b_value, b_out, gain_one, shift_one, b_ffo, gain_two, shift_two, b_in)
    small = jnp.concatenate(small_shards).reshape(1, -1)
    if direct:
        qkv_flow = Flow(gather_hops([w_qkv]))
        near = swap(small, "shard", 1)
        pair = jnp.concatenate([small, near], axis=0)
        four = jnp.concatenate([pair, swap(pair, "shard", 2)], axis=0)
        order = [jnp.bitwise_xor(me, o) for o in range(4)]
        small_full = jnp.concatenate([lax.dynamic_slice_in_dim(four, o, 1, axis=0) for o in order], axis=0)
        later = line.step([w_out, w_in, w_ffo], [qkv_flow])
        later_flow = Flow(gather_hops(later))
        seg = line.step(seg, [qkv_flow])
        x_first = line.step(x, [qkv_flow])
        (qkv_pieces,) = qkv_flow.result
        qkv_starts = jnp.stack(piece_starts(w_qkv)).astype(jnp.int32)
        layer_starts = jnp.stack(sum([piece_starts(w) for w in (w_out, w_in, w_ffo)], [])).astype(jnp.int32)
        counts = (6, 6, 6)
    else:
        small_full = lax.all_gather(small, "shard", axis=0, tiled=True)
        qkv_pieces, *layer_lists = [
            [lax.all_gather(w, "shard", axis=0, tiled=True)] for w in (w_qkv, w_out, w_in, w_ffo)
        ]
        x_first = x
        qkv_starts = jnp.zeros((1,), jnp.int32)
        layer_starts = jnp.zeros((3,), jnp.int32)
        counts = (1, 1, 1)
    small_full = small_full.astype(F32)
    vectors = [small_full[:, i * part : (i + 1) * part].reshape(1, -1) for i in range(8)]
    bias_all = jnp.concatenate([vectors[0], jnp.zeros_like(vectors[0]), vectors[1]], axis=1)
    vec = jnp.concatenate(vectors[2:] + [jnp.zeros((2, width), F32)], axis=0)
    bias_in = small_full[:, 8 * part :].reshape(1, -1)

    windows = windows_of(seg)
    block = 256
    (projected,) = row_call(
        functools.partial(project_kernel, len(qkv_pieces)),
        "project",
        rows,
        block,
        qkv_starts,
        [x_first],
        [bias_all],
        qkv_pieces,
        [shaped(rows, 3 * width)],
        [],
        [pltpu.VMEM((width, 3 * width), BF)],
        6 * rows * width * width,
    )
    if direct:
        projected = line.step(projected, [later_flow])
    attended, lse = attend_forward(projected, windows, total)
    if direct:
        attended = line.step(attended, [later_flow])
        attended = line.step(attended, [later_flow])
        layer_lists = later_flow.result
    layer_pieces = sum(layer_lists, [])
    weights_scratch = [
        pltpu.VMEM((width, width), BF),
        pltpu.VMEM((width, hidden_width), BF),
        pltpu.VMEM((hidden_width, width), BF),
    ]
    layer_flops = 2 * rows * width * (width + 2 * hidden_width)
    output, normed, n_one, rstd_one, d_second, hidden, slope, sums_two = row_call(
        functools.partial(layer_forward_kernel, counts),
        "layer_forward",
        rows,
        block,
        layer_starts,
        [x, attended, cot],
        [vec, bias_in],
        layer_pieces,
        [
            shaped(rows, width),
            shaped(rows, width),
            shaped(rows, width),
            shaped(rows, 128, dtype=F32),
            shaped(rows, width),
            shaped(rows, hidden_width),
            shaped(rows, hidden_width),
        ],
        [shaped(24, width, dtype=F32)],
        weights_scratch,
        layer_flops,
    )

    place = [jnp.bitwise_xor(me, o) for o in range(4)]
    slots = jnp.stack(
        [(p & 1) * 2 + lax.shift_right_logical(p, 1) for p in place] + [jnp.bitwise_xor(me, j) for j in (1, 3, 2, 0)]
    ).astype(jnp.int32)

    def weight_terms(a, b, name):
        if direct:
            terms = weight_grad(slots, a, b, name)
            line.recent.append(terms[0])
            return line.start(reduce_hops(terms[:3])), terms[3:]
        return reduce_plain(a, b), [fold_rows(b.astype(F32))]

    flow_ffo, _ = weight_terms(hidden, d_second, "grad_ffo")
    if direct:
        d_second, layer_pieces = line.step((d_second, layer_pieces), [])
    d_pre, d_branch, d_attended, sums_one, sums_in = row_call(
        functools.partial(layer_backward_kernel, counts),
        "layer_backward",
        rows,
        block,
        layer_starts,
        [d_second, slope, n_one, rstd_one],
        [vec],
        layer_pieces,
        [shaped(rows, hidden_width), shaped(rows, width), shaped(rows, width)],
        [shaped(24, width, dtype=F32), shaped(8, hidden_width, dtype=F32)],
        weights_scratch,
        layer_flops,
    )
    if direct:
        d_pre, d_branch, d_attended = line.step((d_pre, d_branch, d_attended))
    flow_in, _ = weight_terms(normed, d_pre, "grad_in")
    if direct:
        d_branch, d_attended = line.step((d_branch, d_attended), [])
    flow_out, _ = weight_terms(attended, d_branch, "grad_out")
    groups = 3
    d_heads, flows, head_sums = [], [], []
    for g in range(groups):
        if direct:
            d_attended = line.step(d_attended)
        d_head = attend_backward(projected, d_attended, attended, lse, windows, total, g, groups)
        if direct:
            d_head = line.step(d_head)
        flow, sums = weight_terms(x, d_head, "grad_qkv")
        d_heads.append(d_head)
        flows.append(flow)
        head_sums.append(sums[0])

    def folded(sums):
        return [jnp.sum(sums[i : i + 8], axis=0) for i in range(0, sums.shape[0], 8)]

    d_gain_two, d_shift_two, d_ffo_bias = folded(sums_two)
    d_gain_one, d_shift_one, d_out_bias = folded(sums_one)
    (d_in_bias,) = folded(sums_in)
    cut = width // groups
    head_sums = [jnp.sum(s, axis=0) for s in head_sums]
    d_query_bias = jnp.concatenate([s[:cut] for s in head_sums])
    d_value_bias = jnp.concatenate([s[2 * cut :] for s in head_sums])
    smalls = (
        d_query_bias, d_value_bias, d_out_bias, d_gain_one, d_shift_one, d_ffo_bias, d_gain_two, d_shift_two,
        d_in_bias,
    )
    packed = jnp.concatenate([s.reshape(group, -1) for s in smalls], axis=1)
    if direct:
        flow_small = line.start(reduce_small(packed))
        d_branch = line.step(d_branch, [])
    (d_tokens,) = row_call(
        functools.partial(input_grad_kernel, len(qkv_pieces), groups),
        "input_grad",
        rows,
        block,
        qkv_starts,
        [d_branch, *d_heads],
        [],
        qkv_pieces,
        [shaped(rows, width)],
        [],
        [pltpu.VMEM((width, 3 * width), BF)],
        6 * rows * width * width,
    )
    if direct:
        while any(f.flying is not None for f in line.flows):
            d_tokens = line.step(d_tokens)
        packed = flow_small.result
        grad_ffo, grad_in, grad_out, *grads = [f.result for f in (flow_ffo, flow_in, flow_out, *flows)]
    else:
        packed = lax.psum(packed, ("shard", "rep"))
        grad_ffo, grad_in, grad_out, grads = flow_ffo, flow_in, flow_out, flows
    grad_qkv = jnp.concatenate([g[:, n * cut : (n + 1) * cut] for n in range(3) for g in grads], axis=1)
    mine = lax.dynamic_index_in_dim(packed, me, 0, keepdims=False)
    sm = [mine[i * part : (i + 1) * part] for i in range(8)]
    gqb, gvb, gob, gg1, gs1, gfb, gg2, gs2 = sm
    gib = mine[8 * part :]
    return (
        output.reshape(tokens.shape),
        d_tokens.reshape(tokens.shape),
        grad_qkv,
        gqb,
        gvb,
        grad_out,
        gob,
        gg1,
        gs1,
        grad_in,
        gib,
        grad_ffo,
        gfb,
        gg2,
        gs2,
    )


def solution(mesh):
    data = P(None, ("shard", "rep"), None, None)
    matrix = P("shard", None)
    vector = P("shard")
    return jax.shard_map(
        local,
        mesh=mesh,
        in_specs=(
            data,
            P(None, ("shard", "rep"), None),
            data,
            matrix,
            vector,
            vector,
            matrix,
            vector,
            vector,
            vector,
            matrix,
            vector,
            matrix,
            vector,
            vector,
            vector,
        ),
        out_specs=(
            data,
            data,
            matrix,
            vector,
            vector,
            matrix,
            vector,
            vector,
            vector,
            matrix,
            vector,
            matrix,
            vector,
            vector,
            vector,
        ),
        check_vma=False,
    )
```

```python
import functools
import math

import jax
import jax.numpy as jnp
from jax import lax
from jax.experimental import pallas as pl
from jax.experimental.pallas import tpu as pltpu
from jax.sharding import PartitionSpec as P

HEADS = 12
HEAD_DIM = 64
PAIR = 2 * HEAD_DIM
TILE = 128

epsilon = 1e-05
masked_score = -1e30
BF = jnp.bfloat16
F32 = jnp.float32
VMEM_LIMIT = 60 * 2**20


def dot_nn(a, b):
    return lax.dot_general(a, b, (((1,), (0,)), ((), ())), preferred_element_type=F32)


def dot_nt(a, b):
    return lax.dot_general(a, b, (((1,), (1,)), ((), ())), preferred_element_type=F32)


def dot_tn(a, b):
    return lax.dot_general(a, b, (((0,), (0,)), ((), ())), preferred_element_type=F32)


def head_rows(value):
    lane = lax.broadcasted_iota(jnp.int32, (1, PAIR), 1)
    first = jnp.where(lane < HEAD_DIM, value, 0.0).astype(BF)
    second = jnp.where(lane < HEAD_DIM, 0.0, value).astype(BF)
    return first, second


def stack_heads(block, rows):
    return jnp.concatenate([block * rows[0], block * rows[1]], axis=0)


def diagonal_back(transposed):
    kept = jnp.concatenate(
        [transposed[:HEAD_DIM, :TILE], transposed[HEAD_DIM:, TILE:]], axis=0
    )
    return kept.T


def for_windows(count, tiles, body):
    sizes = [t for t in range(1, tiles + 1) if t < 7 or t == tiles]
    below = 0
    for size in sizes:
        @pl.when((count > below) & (count <= size))
        def _(size=size):
            body(size)

        below = size


def attend_forward_kernel(pairs, tiles, low_ref, count_ref, q_ref, k_ref, v_ref, kseg_ref, qseg_ref, o_ref, lse_ref):
    place = pl.program_id(0) * tiles + pl.program_id(1)
    low = low_ref[place]
    count = count_ref[place]
    rows_of = head_rows(1.0 / math.sqrt(HEAD_DIM))

    def window(size):
        start = jnp.minimum(low, tiles - size) * TILE
        chunks = [pl.ds(pl.multiple_of(start + c * TILE, TILE), TILE) for c in range(size)]
        whole = pl.ds(pl.multiple_of(start, TILE), size * TILE)
        masks = [kseg_ref[c, :] == qseg_ref[0] for c in chunks]
        def first(p):
            lanes = slice(p * PAIR, (p + 1) * PAIR)
            queries = stack_heads(q_ref[:, lanes], rows_of)
            scores = []
            for c, mask in zip(chunks, masks):
                part = dot_nt(k_ref[c, lanes], queries)
                scores.append(
                    jnp.concatenate(
                        [
                            jnp.where(mask, part[:, :TILE], masked_score),
                            jnp.where(mask, part[:, TILE:], masked_score),
                        ],
                        axis=1,
                    )
                )
            return scores

        def second(p, scores):
            lanes = slice(p * PAIR, (p + 1) * PAIR)
            top = functools.reduce(jnp.maximum, [jnp.max(s, axis=0, keepdims=True) for s in scores])
            exps = [jnp.exp(s - top) for s in scores]
            total = functools.reduce(jnp.add, [jnp.sum(e, axis=0, keepdims=True) for e in exps])
            weights = jnp.concatenate([e.astype(BF) for e in exps], axis=0)
            mixed = dot_tn(v_ref[whole, lanes], weights) / total
            o_ref[:, lanes] = diagonal_back(mixed).astype(BF)
            lse_ref[0, p : p + 1, :] = top + jnp.log(total)

        ready = first(0)
        for p in range(pairs):
            after = first(p + 1) if p + 1 < pairs else None
            second(p, ready)
            ready = after

    for_windows(count, tiles, window)


def attend_backward_kernel(
    pairs, tiles, low_ref, count_ref, q_ref, k_ref, v_ref, do_ref, o_ref, lse_ref, kseg_ref, qseg_ref,
    out_ref, dk_acc, dv_acc, *, first_pair,
):
    block = pl.program_id(1)
    place = pl.program_id(0) * tiles + block
    low = low_ref[place]
    count = count_ref[place]
    part = pairs * PAIR
    scale = 1.0 / math.sqrt(HEAD_DIM)
    scaled_rows = head_rows(scale)
    plain_rows = head_rows(1.0)

    @pl.when(block == 0)
    def _():
        dk_acc[...] = jnp.zeros_like(dk_acc)
        dv_acc[...] = jnp.zeros_like(dv_acc)

    def window(size):
        start = jnp.minimum(low, tiles - size) * TILE
        chunks = [pl.ds(pl.multiple_of(start + c * TILE, TILE), TILE) for c in range(size)]
        whole = pl.ds(pl.multiple_of(start, TILE), size * TILE)
        masks = [kseg_ref[c, :] == qseg_ref[0] for c in chunks]
        mine = pl.ds(pl.multiple_of(block * TILE, TILE), TILE)
        for p in range(pairs):
            lanes = slice(p * PAIR, (p + 1) * PAIR)
            queries = stack_heads(q_ref[:, lanes], scaled_rows)
            grads = do_ref[:, lanes]
            stacked = stack_heads(grads, plain_rows)
            product = (grads.astype(F32) * o_ref[:, lanes].astype(F32)).T
            row_dot = jnp.concatenate(
                [
                    jnp.sum(product[:HEAD_DIM], axis=0, keepdims=True),
                    jnp.sum(product[HEAD_DIM:], axis=0, keepdims=True),
                ],
                axis=1,
            )
            lse = lse_ref[0, first_pair + p : first_pair + p + 1, :]
            kept = []
            weights = []
            all_scores = dot_nt(k_ref[whole, lanes], queries)
            all_d_probs = dot_nt(v_ref[whole, lanes], stacked)
            for n, mask in enumerate(masks):
                rows_n = slice(n * TILE, (n + 1) * TILE)
                part_scores = all_scores[rows_n] - lse
                d_probs = all_d_probs[rows_n]
                probs = jnp.exp(
                    jnp.concatenate(
                        [
                            jnp.where(mask, part_scores[:, :TILE], masked_score),
                            jnp.where(mask, part_scores[:, TILE:], masked_score),
                        ],
                        axis=1,
                    )
                )
                kept.append((probs * (d_probs - row_dot)).astype(BF))
                weights.append(probs.astype(BF))
            kept = jnp.concatenate(kept, axis=0)
            weights = jnp.concatenate(weights, axis=0)
            dv_acc[whole, lanes] += dot_nn(weights, stacked)
            dk_acc[whole, lanes] += dot_nn(kept, queries)
            mixed = dot_tn(k_ref[whole, lanes], kept) * scale
            out_ref[mine, lanes] = diagonal_back(mixed).astype(BF)

    for_windows(count, tiles, window)

    @pl.when(block == tiles - 1)
    def _():
        out_ref[:, part : 2 * part] = dk_acc[...].astype(BF)
        out_ref[:, 2 * part :] = dv_acc[...].astype(BF)


def windows_of(segments):
    sequences, length = segments.shape
    tiles = length // TILE
    blocked = segments.reshape(sequences, tiles, TILE)
    first = blocked[:, :, 0]
    last = blocked[:, :, TILE - 1]
    starts = jnp.sum((segments[:, None, :] < first[:, :, None]).astype(jnp.int32), axis=-1)
    ends = jnp.sum((segments[:, None, :] <= last[:, :, None]).astype(jnp.int32), axis=-1)
    bits = TILE.bit_length() - 1
    low = lax.shift_right_logical(starts, bits)
    count = lax.shift_right_logical(ends + TILE - 1, bits) - low
    key_ids = jnp.broadcast_to(segments.reshape(sequences * length, 1), (sequences * length, TILE))
    query_ids = blocked.reshape(sequences * tiles, 1, TILE)
    return low.reshape(-1), count.reshape(-1), key_ids, query_ids


def attend_forward(projected, windows, sequences):
    low, count, key_ids, query_ids = windows
    rows = projected.shape[0]
    width = projected.shape[1] // 3
    length = rows // sequences
    tiles = length // TILE
    pairs = width // PAIR
    return pl.pallas_call(
        functools.partial(attend_forward_kernel, pairs, tiles),
        grid_spec=pltpu.PrefetchScalarGridSpec(
            num_scalar_prefetch=2,
            grid=(sequences, tiles),
            in_specs=[
                pl.BlockSpec((TILE, width), lambda s, b, *_: (s * tiles + b, 0)),
                pl.BlockSpec((length, width), lambda s, b, *_: (s, 1)),
                pl.BlockSpec((length, width), lambda s, b, *_: (s, 2)),
                pl.BlockSpec((length, TILE), lambda s, b, *_: (s, 0)),
                pl.BlockSpec((1, 1, TILE), lambda s, b, *_: (s * tiles + b, 0, 0)),
            ],
            out_specs=[
                pl.BlockSpec((TILE, width), lambda s, b, *_: (s * tiles + b, 0)),
                pl.BlockSpec((1, 8, 2 * TILE), lambda s, b, *_: (s * tiles + b, 0, 0)),
            ],
        ),
        out_shape=[
            jax.ShapeDtypeStruct((rows, width), BF),
            jax.ShapeDtypeStruct((sequences * tiles, 8, 2 * TILE), F32),
        ],
        compiler_params=pltpu.CompilerParams(vmem_limit_bytes=VMEM_LIMIT),
        cost_estimate=cost(8 * 10**9, 16 * 10**6),
        name="attend_forward",
    )(low, count, projected, projected, projected, key_ids, query_ids)


def attend_backward(projected, d_attended, attended, lse, windows, sequences, group, groups):
    low, count, key_ids, query_ids = windows
    rows = projected.shape[0]
    width = projected.shape[1] // 3
    length = rows // sequences
    tiles = length // TILE
    part = width // groups
    pairs = part // PAIR
    query_spec = pl.BlockSpec((TILE, part), lambda s, b, *_: (s * tiles + b, group))
    return pl.pallas_call(
        functools.partial(attend_backward_kernel, pairs, tiles, first_pair=group * pairs),
        grid_spec=pltpu.PrefetchScalarGridSpec(
            num_scalar_prefetch=2,
            grid=(sequences, tiles),
            in_specs=[
                query_spec,
                pl.BlockSpec((length, part), lambda s, b, *_: (s, groups + group)),
                pl.BlockSpec((length, part), lambda s, b, *_: (s, 2 * groups + group)),
                query_spec,
                query_spec,
                pl.BlockSpec((1, 8, 2 * TILE), lambda s, b, *_: (s * tiles + b, 0, 0)),
                pl.BlockSpec((length, TILE), lambda s, b, *_: (s, 0)),
                pl.BlockSpec((1, 1, TILE), lambda s, b, *_: (s * tiles + b, 0, 0)),
            ],
            out_specs=pl.BlockSpec((length, 3 * part), lambda s, b, *_: (s, 0)),
            scratch_shapes=[pltpu.VMEM((length, part), F32), pltpu.VMEM((length, part), F32)],
        ),
        out_shape=jax.ShapeDtypeStruct((rows, 3 * part), BF),
        compiler_params=pltpu.CompilerParams(vmem_limit_bytes=VMEM_LIMIT),
        cost_estimate=cost(30 * 10**9 // groups, 30 * 10**6 // groups),
        name="attend_backward",
    )(low, count, projected, projected, projected, d_attended, attended, lse, key_ids, query_ids)


def row_mean(values):
    return jnp.mean(values, axis=-1, keepdims=True)


def fold_rows(values):
    rows, width = values.shape
    return jnp.sum(values.reshape(rows // 8, 8, width), axis=0)


def load_pieces(starts_ref, pieces, targets, sems):
    copies = []
    for n, (piece, target) in enumerate(zip(pieces, targets)):
        height = piece.shape[0]
        start = pl.multiple_of(starts_ref[n], math.gcd(height, 128))
        copies.append(pltpu.make_async_copy(piece, target.at[pl.ds(start, height)], sems.at[n]))
    for copy in copies:
        copy.start()
    for copy in copies:
        copy.wait()


def gelu_parts(values):
    bell = jnp.exp(values * values * -0.5)
    t = 1.0 / (1.0 + jnp.abs(values) * (0.3275911 / math.sqrt(2.0)))
    poly = t * (
        0.5 * 0.254829592
        + t * (0.5 * -0.284496736 + t * (0.5 * 1.421413741 + t * (0.5 * -1.453152027 + t * (0.5 * 1.061405429))))
    )
    tail = poly * bell
    phi = jnp.where(values >= 0.0, 1.0 - tail, tail)
    return values * phi, phi + values * bell * (1.0 / math.sqrt(2.0 * math.pi))


def project_kernel(count, starts_ref, x_ref, bias_ref, *refs):
    pieces = refs[:count]
    o_ref, weight, sems = refs[count:]

    @pl.when(pl.program_id(0) == 0)
    def _():
        load_pieces(starts_ref, pieces, [weight] * count, sems)

    o_ref[...] = (dot_nn(x_ref[...], weight[...]) + bias_ref[...]).astype(BF)


FFN_CHUNK = 512


def layer_forward_kernel(
    counts, starts_ref, x_ref, att_ref, cot_ref, vec_ref, bin_ref, *refs
):
    total = sum(counts)
    pieces = refs[:total]
    (
        out_ref, normed_ref, none_ref, rstd_ref, dsec_ref, hidden_ref, slope_ref, sums_ref,
        w_out, w_in, w_ffo, sems,
    ) = refs[total:]
    targets = [w_out] * counts[0] + [w_in] * counts[1] + [w_ffo] * counts[2]

    @pl.when(pl.program_id(0) == 0)
    def _():
        load_pieces(starts_ref, pieces, targets, sems)
        sums_ref[...] = jnp.zeros_like(sums_ref)

    b_out, gain_one, shift_one, b_ffo, gain_two, shift_two = [vec_ref[i : i + 1, :] for i in range(6)]
    res = x_ref[...].astype(F32) + (dot_nn(att_ref[...], w_out[...]) + b_out)
    center = res - row_mean(res)
    rstd = lax.rsqrt(row_mean(center * center) + epsilon)
    n_one = center * rstd
    normed = (n_one * gain_one + shift_one).astype(BF)
    normed_ref[...] = normed
    none_ref[...] = n_one.astype(BF)
    rstd_ref[...] = jnp.broadcast_to(rstd, rstd_ref.shape)
    hidden_width = w_in.shape[1]
    second = None
    pres = []
    for c in range(0, hidden_width, FFN_CHUNK):
        cols = slice(c, c + FFN_CHUNK)
        pre = dot_nn(normed, w_in[:, cols]) + bin_ref[:, cols]
        value, slope = gelu_parts(pre)
        value = value.astype(BF)
        hidden_ref[:, cols] = value
        slope_ref[:, cols] = slope.astype(BF)
        term = dot_nn(value, w_ffo[cols, :])
        second = term if second is None else second + term
    res = normed.astype(F32) + (second + b_ffo)
    center = res - row_mean(res)
    rstd = lax.rsqrt(row_mean(center * center) + epsilon)
    n_two = center * rstd
    out_ref[...] = (n_two * gain_two + shift_two).astype(BF)
    cot = cot_ref[...].astype(F32)
    inner = cot * gain_two
    d_second = (rstd * (inner - row_mean(inner) - n_two * row_mean(inner * n_two))).astype(BF)
    dsec_ref[...] = d_second
    sums_ref[0:8, :] += fold_rows(cot * n_two)
    sums_ref[8:16, :] += fold_rows(cot)
    sums_ref[16:24, :] += fold_rows(d_second.astype(F32))


def layer_backward_kernel(counts, starts_ref, dsec_ref, slope_ref, none_ref, rstd_ref, vec_ref, *refs):
    total = sum(counts)
    pieces = refs[:total]
    dpre_ref, dbranch_ref, datt_ref, sums_ref, bin_ref, w_out, w_in, w_ffo, sems = refs[total:]
    targets = [w_out] * counts[0] + [w_in] * counts[1] + [w_ffo] * counts[2]

    @pl.when(pl.program_id(0) == 0)
    def _():
        load_pieces(starts_ref, pieces, targets, sems)
        sums_ref[...] = jnp.zeros_like(sums_ref)
        bin_ref[...] = jnp.zeros_like(bin_ref)

    gain_one = vec_ref[1:2, :]
    d_second = dsec_ref[...]
    d_norm = d_second.astype(F32)
    for c in range(0, w_in.shape[1], FFN_CHUNK):
        cols = slice(c, c + FFN_CHUNK)
        d_pre = (dot_nt(d_second, w_ffo[cols, :]) * slope_ref[:, cols].astype(F32)).astype(BF)
        dpre_ref[:, cols] = d_pre
        bin_ref[:, cols] += fold_rows(d_pre.astype(F32))
        d_norm = d_norm + dot_nt(d_pre, w_in[:, cols])
    n_one = none_ref[...].astype(F32)
    inner = d_norm * gain_one
    d_res = rstd_ref[:, 0:1] * (inner - row_mean(inner) - n_one * row_mean(inner * n_one))
    d_branch = d_res.astype(BF)
    dbranch_ref[...] = d_branch
    datt_ref[...] = dot_nt(d_branch, w_out[...]).astype(BF)
    sums_ref[0:8, :] += fold_rows(d_norm * n_one)
    sums_ref[8:16, :] += fold_rows(d_norm)
    sums_ref[16:24, :] += fold_rows(d_branch.astype(F32))


def input_grad_kernel(count, groups, starts_ref, dbranch_ref, *refs):
    grads = refs[:groups]
    pieces = refs[groups : groups + count]
    o_ref, weight, sems = refs[groups + count :]

    @pl.when(pl.program_id(0) == 0)
    def _():
        load_pieces(starts_ref, pieces, [weight] * count, sems)

    width = dbranch_ref.shape[1]
    part = width // groups
    total = dbranch_ref[...].astype(F32)
    for g, ref in enumerate(grads):
        for n in range(3):
            first = n * width + g * part
            total = total + dot_nt(ref[:, n * part : (n + 1) * part], weight[:, first : first + part])
    o_ref[...] = total.astype(BF)


def weight_grad_rows_kernel(owner_ref, a_ref, b_ref, keep_ref, pass_ref, send_ref):
    step = pl.program_id(0)
    part = dot_tn(a_ref[...], b_ref[...]).astype(BF)

    @pl.when(step < 2)
    def _():
        send_ref[...] = part

    @pl.when(step == 2)
    def _():
        pass_ref[...] = part

    @pl.when(step == 3)
    def _():
        keep_ref[...] = part


def weight_grad_cols_kernel(slots, owner_ref, a_ref, b_ref, keep_ref, pass_ref, send_ref, sums_ref, held):
    terms = b_ref[...]
    sums_ref[...] = fold_rows(terms.astype(F32))
    part = dot_tn(a_ref[...], terms).astype(BF)
    height = keep_ref.shape[0]
    for owner in range(4):
        held[owner_ref[owner]] = part[owner * height : (owner + 1) * height]
    keep_ref[...] = held[0]
    pass_ref[...] = held[1]
    send_ref[0:height, :] = held[2]
    send_ref[height:, :] = held[3]


PARAMS = pltpu.CompilerParams(vmem_limit_bytes=VMEM_LIMIT)


def cost(flops, bytes_accessed):
    return pl.CostEstimate(flops=int(flops) // 16, bytes_accessed=int(bytes_accessed) // 16, transcendentals=0)


def whole_spec(array):
    zeros = (0,) * array.ndim
    return pl.BlockSpec(array.shape, lambda *_: zeros)


ANY = pl.BlockSpec(memory_space=pl.ANY)


def row_call(kernel, name, rows, block, scalars, blocked, fixed, pieces, outs, accs, scratch, flops):
    in_specs = (
        [pl.BlockSpec((block, a.shape[1]), lambda i, *_: (i, 0)) for a in blocked]
        + [whole_spec(a) for a in fixed]
        + [ANY] * len(pieces)
    )
    out_specs = [pl.BlockSpec((block, s.shape[1]), lambda i, *_: (i, 0)) for s in outs] + [
        whole_spec(s) for s in accs
    ]
    moved = sum(a.size * a.dtype.itemsize for a in list(blocked) + list(pieces) + list(outs))
    return pl.pallas_call(
        kernel,
        grid_spec=pltpu.PrefetchScalarGridSpec(
            num_scalar_prefetch=1,
            grid=(rows // block,),
            in_specs=in_specs,
            out_specs=out_specs,
            scratch_shapes=list(scratch) + [pltpu.SemaphoreType.DMA((len(pieces),))],
        ),
        out_shape=list(outs) + list(accs),
        compiler_params=PARAMS,
        cost_estimate=cost(flops, moved),
        name=name,
    )(scalars, *blocked, *fixed, *pieces)


def shaped(*shape, dtype=BF):
    return jax.ShapeDtypeStruct(shape, dtype)


def weight_grad(slots, a, b, name):
    rows, height = a.shape
    width = b.shape[1]
    part = height // 4
    flops = 2 * rows * height * width
    moved = 2 * (rows * height + rows * width + height * width)
    if part % 128 == 0:
        return pl.pallas_call(
            weight_grad_rows_kernel,
            grid_spec=pltpu.PrefetchScalarGridSpec(
                num_scalar_prefetch=1,
                grid=(4,),
                in_specs=[
                    pl.BlockSpec((rows, part), lambda t, s: (0, s[4 + t])),
                    pl.BlockSpec((rows, width), lambda t, s: (0, 0)),
                ],
                out_specs=[
                    pl.BlockSpec((part, width), lambda t, s: (0, 0)),
                    pl.BlockSpec((part, width), lambda t, s: (0, 0)),
                    pl.BlockSpec((part, width), lambda t, s: (jnp.minimum(t, 1), 0)),
                ],
            ),
            out_shape=[shaped(part, width), shaped(part, width), shaped(2 * part, width)],
            compiler_params=PARAMS,
            cost_estimate=cost(flops, moved),
            name=name,
        )(slots, a, b)
    block = min(width, 768)
    return pl.pallas_call(
        functools.partial(weight_grad_cols_kernel, 4),
        grid_spec=pltpu.PrefetchScalarGridSpec(
            num_scalar_prefetch=1,
            grid=(width // block,),
            in_specs=[
                pl.BlockSpec((rows, height), lambda t, s: (0, 0)),
                pl.BlockSpec((rows, block), lambda t, s: (0, t)),
            ],
            out_specs=[
                pl.BlockSpec((part, block), lambda t, s: (0, t)),
                pl.BlockSpec((part, block), lambda t, s: (0, t)),
                pl.BlockSpec((2 * part, block), lambda t, s: (0, t)),
                pl.BlockSpec((8, block), lambda t, s: (0, t)),
            ],
            scratch_shapes=[pltpu.VMEM((4, part, block), BF)],
        ),
        out_shape=[
            shaped(part, width),
            shaped(part, width),
            shaped(2 * part, width),
            shaped(8, width, dtype=F32),
        ],
        compiler_params=PARAMS,
        cost_estimate=cost(flops, moved),
        name=name,
    )(slots, a, b)


def swap(array, axis, bit):
    size = lax.axis_size(axis)
    return lax.ppermute(array, axis, [(i, i ^ bit) for i in range(size)])


def gather_hops(shards):
    side = lax.axis_index("rep") & 1
    halves = [s.shape[0] // 2 for s in shards]
    mine = [lax.dynamic_slice_in_dim(s, side * h, h, axis=0) for s, h in zip(shards, halves)]
    direct, core = yield [swap(m, "shard", 2) for m in mine], [swap(s, "shard", 1) for s in shards]
    relayed, cross = yield [swap(d, "rep", 1) for d in direct], [swap(d, "shard", 1) for d in direct]
    cross_relayed = yield [swap(r, "shard", 1) for r in relayed]
    return [list(p) for p in zip(shards, core, direct, relayed, cross, cross_relayed)]


def piece_starts(shard):
    height = shard.shape[0]
    me = lax.axis_index("shard")
    side = lax.axis_index("rep") & 1
    half = height // 2
    near, core, far, cross = [(me ^ o) * height for o in range(4)]
    return [near, core, far + side * half, far + (1 - side) * half, cross + side * half, cross + (1 - side) * half]


def added(*terms):
    return functools.reduce(jnp.add, [t.astype(F32) for t in terms]).astype(BF)


def reduce_hops(parts):
    keep, passed, sent = parts
    height = keep.shape[0]
    come = yield swap(sent, "shard", 1)
    onward = yield swap(added(passed, come[height:]), "shard", 2)
    owned = added(keep, come[:height], onward)
    place = lax.axis_index("rep")
    half, quarter = height // 2, height // 4
    y = place & 1
    z = lax.shift_right_logical(place, 1) & 1
    away = lax.dynamic_slice_in_dim(owned, (1 - y) * half, half, axis=0)
    stay = lax.dynamic_slice_in_dim(owned, y * half, half, axis=0)
    stay = added(stay, (yield swap(away, "rep", 1)))
    away = lax.dynamic_slice_in_dim(stay, (1 - z) * quarter, quarter, axis=0)
    stay = lax.dynamic_slice_in_dim(stay, z * quarter, quarter, axis=0)
    stay = added(stay, (yield swap(away, "rep", 2)))
    stay = added(stay, (yield swap(stay, "rep", 4)))
    other = yield swap(stay, "rep", 2)
    pair = jnp.where(z == 0, jnp.stack([stay, other]), jnp.stack([other, stay])).reshape(half, -1)
    other = yield swap(pair, "rep", 1)
    both = jnp.where(y == 0, jnp.stack([pair, other]), jnp.stack([other, pair])).reshape(height, -1)
    return both.astype(F32)


def reduce_small(packed):
    for axis, bit in (("shard", 1), ("shard", 2), ("rep", 1), ("rep", 2), ("rep", 4)):
        packed = packed + (yield swap(packed, axis, bit))
    return packed


class Flow:
    def __init__(self, hops):
        self.hops = hops
        self.result = None
        self.flying = next(hops)

    def land(self, arrived):
        try:
            self.flying = self.hops.send(arrived)
        except StopIteration as stop:
            self.flying, self.result = None, stop.value


class Line:
    def __init__(self):
        self.flows = []
        self.recent = []

    def step(self, arrays, flows=None):
        moving = [f for f in (self.flows if flows is None else flows) if f.flying is not None]
        held = self.recent
        arrays, arrived, held = lax.optimization_barrier((arrays, [f.flying for f in moving], held))
        for flow, value in zip(moving, arrived):
            flow.land(value)
        self.recent = []
        return arrays

    def start(self, hops):
        flow = Flow(hops)
        self.flows.append(flow)
        return flow


def reduce_plain(a, b):
    grad = dot_tn(a, b).astype(BF)
    owned = lax.psum_scatter(grad, "shard", scatter_dimension=0, tiled=True)
    return lax.psum(owned, "rep").astype(F32)


def local(
    tokens,
    segment_ids,
    cotangent,
    w_qkv,
    b_query,
    b_value,
    w_out,
    b_out,
    gain_one,
    shift_one,
    w_in,
    b_in,
    w_ffo,
    b_ffo,
    gain_two,
    shift_two,
):
    micro, sequences, length, width = tokens.shape
    total = micro * sequences
    rows = total * length
    group = lax.axis_size("shard")
    hidden_width = w_in.shape[1]
    x = tokens.reshape(rows, width)
    seg = segment_ids.reshape(total, length)
    cot = cotangent.reshape(rows, width)
    me = lax.axis_index("shard")
    direct = group == 4 and lax.axis_size("rep") == 8

    part = b_query.shape[0]
    line = Line()
    small_shards = (b_query, b_value, b_out, gain_one, shift_one, b_ffo, gain_two, shift_two, b_in)
    small = jnp.concatenate(small_shards).reshape(1, -1)
    if direct:
        qkv_flow = Flow(gather_hops([w_qkv]))
        near = swap(small, "shard", 1)
        pair = jnp.concatenate([small, near], axis=0)
        four = jnp.concatenate([pair, swap(pair, "shard", 2)], axis=0)
        order = [jnp.bitwise_xor(me, o) for o in range(4)]
        small_full = jnp.concatenate([lax.dynamic_slice_in_dim(four, o, 1, axis=0) for o in order], axis=0)
        later = line.step([w_out, w_in, w_ffo], [qkv_flow])
        later_flow = Flow(gather_hops(later))
        seg = line.step(seg, [qkv_flow])
        x_first = line.step(x, [qkv_flow])
        (qkv_pieces,) = qkv_flow.result
        qkv_starts = jnp.stack(piece_starts(w_qkv)).astype(jnp.int32)
        layer_starts = jnp.stack(sum([piece_starts(w) for w in (w_out, w_in, w_ffo)], [])).astype(jnp.int32)
        counts = (6, 6, 6)
    else:
        small_full = lax.all_gather(small, "shard", axis=0, tiled=True)
        qkv_pieces, *layer_lists = [
            [lax.all_gather(w, "shard", axis=0, tiled=True)] for w in (w_qkv, w_out, w_in, w_ffo)
        ]
        x_first = x
        qkv_starts = jnp.zeros((1,), jnp.int32)
        layer_starts = jnp.zeros((3,), jnp.int32)
        counts = (1, 1, 1)
    small_full = small_full.astype(F32)
    vectors = [small_full[:, i * part : (i + 1) * part].reshape(1, -1) for i in range(8)]
    bias_all = jnp.concatenate([vectors[0], jnp.zeros_like(vectors[0]), vectors[1]], axis=1)
    vec = jnp.concatenate(vectors[2:] + [jnp.zeros((2, width), F32)], axis=0)
    bias_in = small_full[:, 8 * part :].reshape(1, -1)

    windows = windows_of(seg)
    block = 256
    (projected,) = row_call(
        functools.partial(project_kernel, len(qkv_pieces)),
        "project",
        rows,
        block,
        qkv_starts,
        [x_first],
        [bias_all],
        qkv_pieces,
        [shaped(rows, 3 * width)],
        [],
        [pltpu.VMEM((width, 3 * width), BF)],
        6 * rows * width * width,
    )
    if direct:
        projected = line.step(projected, [later_flow])
    attended, lse = attend_forward(projected, windows, total)
    if direct:
        attended = line.step(attended, [later_flow])
        attended = line.step(attended, [later_flow])
        layer_lists = later_flow.result
    layer_pieces = sum(layer_lists, [])
    weights_scratch = [
        pltpu.VMEM((width, width), BF),
        pltpu.VMEM((width, hidden_width), BF),
        pltpu.VMEM((hidden_width, width), BF),
    ]
    layer_flops = 2 * rows * width * (width + 2 * hidden_width)
    output, normed, n_one, rstd_one, d_second, hidden, slope, sums_two = row_call(
        functools.partial(layer_forward_kernel, counts),
        "layer_forward",
        rows,
        block,
        layer_starts,
        [x, attended, cot],
        [vec, bias_in],
        layer_pieces,
        [
            shaped(rows, width),
            shaped(rows, width),
            shaped(rows, width),
            shaped(rows, 128, dtype=F32),
            shaped(rows, width),
            shaped(rows, hidden_width),
            shaped(rows, hidden_width),
        ],
        [shaped(24, width, dtype=F32)],
        weights_scratch,
        layer_flops,
    )

    place = [jnp.bitwise_xor(me, o) for o in range(4)]
    slots = jnp.stack(
        [(p & 1) * 2 + lax.shift_right_logical(p, 1) for p in place] + [jnp.bitwise_xor(me, j) for j in (1, 3, 2, 0)]
    ).astype(jnp.int32)

    def weight_terms(a, b, name):
        if direct:
            terms = weight_grad(slots, a, b, name)
            line.recent.append(terms[0])
            return line.start(reduce_hops(terms[:3])), terms[3:]
        return reduce_plain(a, b), [fold_rows(b.astype(F32))]

    flow_ffo, _ = weight_terms(hidden, d_second, "grad_ffo")
    if direct:
        d_second, layer_pieces = line.step((d_second, layer_pieces), [])
    d_pre, d_branch, d_attended, sums_one, sums_in = row_call(
        functools.partial(layer_backward_kernel, counts),
        "layer_backward",
        rows,
        block,
        layer_starts,
        [d_second, slope, n_one, rstd_one],
        [vec],
        layer_pieces,
        [shaped(rows, hidden_width), shaped(rows, width), shaped(rows, width)],
        [shaped(24, width, dtype=F32), shaped(8, hidden_width, dtype=F32)],
        weights_scratch,
        layer_flops,
    )
    if direct:
        d_pre, d_branch, d_attended = line.step((d_pre, d_branch, d_attended))
    flow_in, _ = weight_terms(normed, d_pre, "grad_in")
    if direct:
        d_branch, d_attended = line.step((d_branch, d_attended), [])
    flow_out, _ = weight_terms(attended, d_branch, "grad_out")
    groups = 3
    d_heads, flows, head_sums = [], [], []
    for g in range(groups):
        if direct:
            d_attended = line.step(d_attended)
        d_head = attend_backward(projected, d_attended, attended, lse, windows, total, g, groups)
        if direct:
            d_head = line.step(d_head)
        flow, sums = weight_terms(x, d_head, "grad_qkv")
        d_heads.append(d_head)
        flows.append(flow)
        head_sums.append(sums[0])

    def folded(sums):
        return [jnp.sum(sums[i : i + 8], axis=0) for i in range(0, sums.shape[0], 8)]

    d_gain_two, d_shift_two, d_ffo_bias = folded(sums_two)
    d_gain_one, d_shift_one, d_out_bias = folded(sums_one)
    (d_in_bias,) = folded(sums_in)
    cut = width // groups
    head_sums = [jnp.sum(s, axis=0) for s in head_sums]
    d_query_bias = jnp.concatenate([s[:cut] for s in head_sums])
    d_value_bias = jnp.concatenate([s[2 * cut :] for s in head_sums])
    smalls = (
        d_query_bias, d_value_bias, d_out_bias, d_gain_one, d_shift_one, d_ffo_bias, d_gain_two, d_shift_two,
        d_in_bias,
    )
    packed = jnp.concatenate([s.reshape(group, -1) for s in smalls], axis=1)
    if direct:
        flow_small = line.start(reduce_small(packed))
        d_branch = line.step(d_branch, [])
    (d_tokens,) = row_call(
        functools.partial(input_grad_kernel, len(qkv_pieces), groups),
        "input_grad",
        rows,
        block,
        qkv_starts,
        [d_branch, *d_heads],
        [],
        qkv_pieces,
        [shaped(rows, width)],
        [],
        [pltpu.VMEM((width, 3 * width), BF)],
        6 * rows * width * width,
    )
    if direct:
        while any(f.flying is not None for f in line.flows):
            d_tokens = line.step(d_tokens)
        packed = flow_small.result
        grad_ffo, grad_in, grad_out, *grads = [f.result for f in (flow_ffo, flow_in, flow_out, *flows)]
    else:
        packed = lax.psum(packed, ("shard", "rep"))
        grad_ffo, grad_in, grad_out, grads = flow_ffo, flow_in, flow_out, flows
    grad_qkv = jnp.concatenate([g[:, n * cut : (n + 1) * cut] for n in range(3) for g in grads], axis=1)
    mine = lax.dynamic_index_in_dim(packed, me, 0, keepdims=False)
    sm = [mine[i * part : (i + 1) * part] for i in range(8)]
    gqb, gvb, gob, gg1, gs1, gfb, gg2, gs2 = sm
    gib = mine[8 * part :]
    return (
        output.reshape(tokens.shape),
        d_tokens.reshape(tokens.shape),
        grad_qkv,
        gqb,
        gvb,
        grad_out,
        gob,
        gg1,
        gs1,
        grad_in,
        gib,
        grad_ffo,
        gfb,
        gg2,
        gs2,
    )


def solution(mesh):
    data = P(None, ("shard", "rep"), None, None)
    matrix = P("shard", None)
    vector = P("shard")
    return jax.shard_map(
        local,
        mesh=mesh,
        in_specs=(
            data,
            P(None, ("shard", "rep"), None),
            data,
            matrix,
            vector,
            vector,
            matrix,
            vector,
            vector,
            vector,
            matrix,
            vector,
            matrix,
            vector,
            vector,
            vector,
        ),
        out_specs=(
            data,
            data,
            matrix,
            vector,
            vector,
            matrix,
            vector,
            vector,
            vector,
            matrix,
            vector,
            matrix,
            vector,
            vector,
            vector,
        ),
        check_vma=False,
    )
```

```python
import functools
import math

import jax
import jax.numpy as jnp
from jax import lax
from jax.experimental import pallas as pl
from jax.experimental.pallas import tpu as pltpu
from jax.sharding import PartitionSpec as P

HEADS = 12
HEAD_DIM = 64
PAIR = 2 * HEAD_DIM
TILE = 128

epsilon = 1e-05
masked_score = -1e30
BF = jnp.bfloat16
F32 = jnp.float32
VMEM_LIMIT = 60 * 2**20


def dot_nn(a, b):
    return lax.dot_general(a, b, (((1,), (0,)), ((), ())), preferred_element_type=F32)


def dot_nt(a, b):
    return lax.dot_general(a, b, (((1,), (1,)), ((), ())), preferred_element_type=F32)


def dot_tn(a, b):
    return lax.dot_general(a, b, (((0,), (0,)), ((), ())), preferred_element_type=F32)


def head_rows(value):
    lane = lax.broadcasted_iota(jnp.int32, (1, PAIR), 1)
    first = jnp.where(lane < HEAD_DIM, value, 0.0).astype(BF)
    second = jnp.where(lane < HEAD_DIM, 0.0, value).astype(BF)
    return first, second


def stack_heads(block, rows):
    return jnp.concatenate([block * rows[0], block * rows[1]], axis=0)


def diagonal_back(transposed):
    kept = jnp.concatenate(
        [transposed[:HEAD_DIM, :TILE], transposed[HEAD_DIM:, TILE:]], axis=0
    )
    return kept.T


def for_windows(count, tiles, body):
    sizes = [t for t in range(1, tiles + 1) if t < 7 or t == tiles]
    below = 0
    for size in sizes:
        @pl.when((count > below) & (count <= size))
        def _(size=size):
            body(size)

        below = size


def attend_forward_kernel(pairs, tiles, low_ref, count_ref, q_ref, k_ref, v_ref, kseg_ref, qseg_ref, o_ref, lse_ref):
    place = pl.program_id(0) * tiles + pl.program_id(1)
    low = low_ref[place]
    count = count_ref[place]
    rows_of = head_rows(1.0 / math.sqrt(HEAD_DIM))

    def window(size):
        start = jnp.minimum(low, tiles - size) * TILE
        chunks = [pl.ds(pl.multiple_of(start + c * TILE, TILE), TILE) for c in range(size)]
        whole = pl.ds(pl.multiple_of(start, TILE), size * TILE)
        masks = [kseg_ref[c, :] == qseg_ref[0] for c in chunks]
        def first(p):
            lanes = slice(p * PAIR, (p + 1) * PAIR)
            queries = stack_heads(q_ref[:, lanes], rows_of)
            scores = []
            for c, mask in zip(chunks, masks):
                part = dot_nt(k_ref[c, lanes], queries)
                scores.append(
                    jnp.concatenate(
                        [
                            jnp.where(mask, part[:, :TILE], masked_score),
                            jnp.where(mask, part[:, TILE:], masked_score),
                        ],
                        axis=1,
                    )
                )
            return scores

        def second(p, scores):
            lanes = slice(p * PAIR, (p + 1) * PAIR)
            top = functools.reduce(jnp.maximum, [jnp.max(s, axis=0, keepdims=True) for s in scores])
            exps = [jnp.exp(s - top) for s in scores]
            total = functools.reduce(jnp.add, [jnp.sum(e, axis=0, keepdims=True) for e in exps])
            weights = jnp.concatenate([e.astype(BF) for e in exps], axis=0)
            mixed = dot_tn(v_ref[whole, lanes], weights) / total
            o_ref[:, lanes] = diagonal_back(mixed).astype(BF)
            lse_ref[0, p : p + 1, :] = top + jnp.log(total)

        ready = first(0)
        for p in range(pairs):
            after = first(p + 1) if p + 1 < pairs else None
            second(p, ready)
            ready = after

    for_windows(count, tiles, window)


def attend_backward_kernel(
    pairs, tiles, low_ref, count_ref, q_ref, k_ref, v_ref, do_ref, o_ref, lse_ref, kseg_ref, qseg_ref,
    out_ref, dk_acc, dv_acc, *, first_pair,
):
    block = pl.program_id(1)
    place = pl.program_id(0) * tiles + block
    low = low_ref[place]
    count = count_ref[place]
    part = pairs * PAIR
    scale = 1.0 / math.sqrt(HEAD_DIM)
    scaled_rows = head_rows(scale)
    plain_rows = head_rows(1.0)

    @pl.when(block == 0)
    def _():
        dk_acc[...] = jnp.zeros_like(dk_acc)
        dv_acc[...] = jnp.zeros_like(dv_acc)

    def window(size):
        start = jnp.minimum(low, tiles - size) * TILE
        chunks = [pl.ds(pl.multiple_of(start + c * TILE, TILE), TILE) for c in range(size)]
        whole = pl.ds(pl.multiple_of(start, TILE), size * TILE)
        masks = [kseg_ref[c, :] == qseg_ref[0] for c in chunks]
        mine = pl.ds(pl.multiple_of(block * TILE, TILE), TILE)
        for p in range(pairs):
            lanes = slice(p * PAIR, (p + 1) * PAIR)
            queries = stack_heads(q_ref[:, lanes], scaled_rows)
            grads = do_ref[:, lanes]
            stacked = stack_heads(grads, plain_rows)
            product = (grads.astype(F32) * o_ref[:, lanes].astype(F32)).T
            row_dot = jnp.concatenate(
                [
                    jnp.sum(product[:HEAD_DIM], axis=0, keepdims=True),
                    jnp.sum(product[HEAD_DIM:], axis=0, keepdims=True),
                ],
                axis=1,
            )
            lse = lse_ref[0, first_pair + p : first_pair + p + 1, :]
            kept = []
            weights = []
            all_scores = dot_nt(k_ref[whole, lanes], queries)
            all_d_probs = dot_nt(v_ref[whole, lanes], stacked)
            for n, mask in enumerate(masks):
                rows_n = slice(n * TILE, (n + 1) * TILE)
                part_scores = all_scores[rows_n] - lse
                d_probs = all_d_probs[rows_n]
                probs = jnp.exp(
                    jnp.concatenate(
                        [
                            jnp.where(mask, part_scores[:, :TILE], masked_score),
                            jnp.where(mask, part_scores[:, TILE:], masked_score),
                        ],
                        axis=1,
                    )
                )
                kept.append((probs * (d_probs - row_dot)).astype(BF))
                weights.append(probs.astype(BF))
            kept = jnp.concatenate(kept, axis=0)
            weights = jnp.concatenate(weights, axis=0)
            dv_acc[whole, lanes] += dot_nn(weights, stacked)
            dk_acc[whole, lanes] += dot_nn(kept, queries)
            mixed = dot_tn(k_ref[whole, lanes], kept) * scale
            out_ref[mine, lanes] = diagonal_back(mixed).astype(BF)

    for_windows(count, tiles, window)

    @pl.when(block == tiles - 1)
    def _():
        out_ref[:, part : 2 * part] = dk_acc[...].astype(BF)
        out_ref[:, 2 * part :] = dv_acc[...].astype(BF)


def windows_of(segments):
    sequences, length = segments.shape
    tiles = length // TILE
    blocked = segments.reshape(sequences, tiles, TILE)
    first = blocked[:, :, 0]
    last = blocked[:, :, TILE - 1]
    starts = jnp.sum((segments[:, None, :] < first[:, :, None]).astype(jnp.int32), axis=-1)
    ends = jnp.sum((segments[:, None, :] <= last[:, :, None]).astype(jnp.int32), axis=-1)
    bits = TILE.bit_length() - 1
    low = lax.shift_right_logical(starts, bits)
    count = lax.shift_right_logical(ends + TILE - 1, bits) - low
    key_ids = jnp.broadcast_to(segments.reshape(sequences * length, 1), (sequences * length, TILE))
    query_ids = blocked.reshape(sequences * tiles, 1, TILE)
    return low.reshape(-1), count.reshape(-1), key_ids, query_ids


def attend_forward(projected, windows, sequences):
    low, count, key_ids, query_ids = windows
    rows = projected.shape[0]
    width = projected.shape[1] // 3
    length = rows // sequences
    tiles = length // TILE
    pairs = width // PAIR
    return pl.pallas_call(
        functools.partial(attend_forward_kernel, pairs, tiles),
        grid_spec=pltpu.PrefetchScalarGridSpec(
            num_scalar_prefetch=2,
            grid=(sequences, tiles),
            in_specs=[
                pl.BlockSpec((TILE, width), lambda s, b, *_: (s * tiles + b, 0)),
                pl.BlockSpec((length, width), lambda s, b, *_: (s, 1)),
                pl.BlockSpec((length, width), lambda s, b, *_: (s, 2)),
                pl.BlockSpec((length, TILE), lambda s, b, *_: (s, 0)),
                pl.BlockSpec((1, 1, TILE), lambda s, b, *_: (s * tiles + b, 0, 0)),
            ],
            out_specs=[
                pl.BlockSpec((TILE, width), lambda s, b, *_: (s * tiles + b, 0)),
                pl.BlockSpec((1, 8, 2 * TILE), lambda s, b, *_: (s * tiles + b, 0, 0)),
            ],
        ),
        out_shape=[
            jax.ShapeDtypeStruct((rows, width), BF),
            jax.ShapeDtypeStruct((sequences * tiles, 8, 2 * TILE), F32),
        ],
        compiler_params=pltpu.CompilerParams(vmem_limit_bytes=VMEM_LIMIT),
        cost_estimate=cost(8 * 10**9, 16 * 10**6),
        name="attend_forward",
    )(low, count, projected, projected, projected, key_ids, query_ids)


def attend_backward(projected, d_attended, attended, lse, windows, sequences, group, groups):
    low, count, key_ids, query_ids = windows
    rows = projected.shape[0]
    width = projected.shape[1] // 3
    length = rows // sequences
    tiles = length // TILE
    part = width // groups
    pairs = part // PAIR
    query_spec = pl.BlockSpec((TILE, part), lambda s, b, *_: (s * tiles + b, group))
    return pl.pallas_call(
        functools.partial(attend_backward_kernel, pairs, tiles, first_pair=group * pairs),
        grid_spec=pltpu.PrefetchScalarGridSpec(
            num_scalar_prefetch=2,
            grid=(sequences, tiles),
            in_specs=[
                query_spec,
                pl.BlockSpec((length, part), lambda s, b, *_: (s, groups + group)),
                pl.BlockSpec((length, part), lambda s, b, *_: (s, 2 * groups + group)),
                query_spec,
                query_spec,
                pl.BlockSpec((1, 8, 2 * TILE), lambda s, b, *_: (s * tiles + b, 0, 0)),
                pl.BlockSpec((length, TILE), lambda s, b, *_: (s, 0)),
                pl.BlockSpec((1, 1, TILE), lambda s, b, *_: (s * tiles + b, 0, 0)),
            ],
            out_specs=pl.BlockSpec((length, 3 * part), lambda s, b, *_: (s, 0)),
            scratch_shapes=[pltpu.VMEM((length, part), F32), pltpu.VMEM((length, part), F32)],
        ),
        out_shape=jax.ShapeDtypeStruct((rows, 3 * part), BF),
        compiler_params=pltpu.CompilerParams(vmem_limit_bytes=VMEM_LIMIT),
        cost_estimate=cost(30 * 10**9 // groups, 30 * 10**6 // groups),
        name="attend_backward",
    )(low, count, projected, projected, projected, d_attended, attended, lse, key_ids, query_ids)


def row_mean(values):
    return jnp.mean(values, axis=-1, keepdims=True)


def fold_rows(values):
    rows, width = values.shape
    return jnp.sum(values.reshape(rows // 8, 8, width), axis=0)


def load_pieces(starts_ref, pieces, targets, sems):
    copies = []
    for n, (piece, target) in enumerate(zip(pieces, targets)):
        height = piece.shape[0]
        start = pl.multiple_of(starts_ref[n], math.gcd(height, 128))
        copies.append(pltpu.make_async_copy(piece, target.at[pl.ds(start, height)], sems.at[n]))
    for copy in copies:
        copy.start()
    for copy in copies:
        copy.wait()


def gelu_parts(values):
    bell = jnp.exp(values * values * -0.5)
    t = 1.0 / (1.0 + jnp.abs(values) * (0.3275911 / math.sqrt(2.0)))
    poly = t * (
        0.5 * 0.254829592
        + t * (0.5 * -0.284496736 + t * (0.5 * 1.421413741 + t * (0.5 * -1.453152027 + t * (0.5 * 1.061405429))))
    )
    tail = poly * bell
    phi = jnp.where(values >= 0.0, 1.0 - tail, tail)
    return values * phi, phi + values * bell * (1.0 / math.sqrt(2.0 * math.pi))


def project_kernel(count, starts_ref, x_ref, bias_ref, *refs):
    pieces = refs[:count]
    o_ref, weight, sems = refs[count:]

    @pl.when(pl.program_id(0) == 0)
    def _():
        load_pieces(starts_ref, pieces, [weight] * count, sems)

    o_ref[...] = (dot_nn(x_ref[...], weight[...]) + bias_ref[...]).astype(BF)


FFN_CHUNK = 512


def layer_forward_kernel(
    counts, starts_ref, x_ref, att_ref, cot_ref, vec_ref, bin_ref, *refs
):
    total = sum(counts)
    pieces = refs[:total]
    (
        out_ref, normed_ref, none_ref, rstd_ref, dsec_ref, hidden_ref, slope_ref, sums_ref,
        w_out, w_in, w_ffo, sems,
    ) = refs[total:]
    targets = [w_out] * counts[0] + [w_in] * counts[1] + [w_ffo] * counts[2]

    @pl.when(pl.program_id(0) == 0)
    def _():
        load_pieces(starts_ref, pieces, targets, sems)
        sums_ref[...] = jnp.zeros_like(sums_ref)

    b_out, gain_one, shift_one, b_ffo, gain_two, shift_two = [vec_ref[i : i + 1, :] for i in range(6)]
    res = x_ref[...].astype(F32) + (dot_nn(att_ref[...], w_out[...]) + b_out)
    center = res - row_mean(res)
    rstd = lax.rsqrt(row_mean(center * center) + epsilon)
    n_one = center * rstd
    normed = (n_one * gain_one + shift_one).astype(BF)
    normed_ref[...] = normed
    none_ref[...] = n_one.astype(BF)
    rstd_ref[...] = jnp.broadcast_to(rstd, rstd_ref.shape)
    hidden_width = w_in.shape[1]
    second = None
    pres = []
    for c in range(0, hidden_width, FFN_CHUNK):
        cols = slice(c, c + FFN_CHUNK)
        pre = dot_nn(normed, w_in[:, cols]) + bin_ref[:, cols]
        value, slope = gelu_parts(pre)
        value = value.astype(BF)
        hidden_ref[:, cols] = value
        slope_ref[:, cols] = slope.astype(BF)
        term = dot_nn(value, w_ffo[cols, :])
        second = term if second is None else second + term
    res = normed.astype(F32) + (second + b_ffo)
    center = res - row_mean(res)
    rstd = lax.rsqrt(row_mean(center * center) + epsilon)
    n_two = center * rstd
    out_ref[...] = (n_two * gain_two + shift_two).astype(BF)
    cot = cot_ref[...].astype(F32)
    inner = cot * gain_two
    d_second = (rstd * (inner - row_mean(inner) - n_two * row_mean(inner * n_two))).astype(BF)
    dsec_ref[...] = d_second
    sums_ref[0:8, :] += fold_rows(cot * n_two)
    sums_ref[8:16, :] += fold_rows(cot)
    sums_ref[16:24, :] += fold_rows(d_second.astype(F32))


def layer_backward_kernel(counts, starts_ref, dsec_ref, slope_ref, none_ref, rstd_ref, vec_ref, *refs):
    total = sum(counts)
    pieces = refs[:total]
    dpre_ref, dbranch_ref, datt_ref, sums_ref, bin_ref, w_out, w_in, w_ffo, sems = refs[total:]
    targets = [w_out] * counts[0] + [w_in] * counts[1] + [w_ffo] * counts[2]

    @pl.when(pl.program_id(0) == 0)
    def _():
        load_pieces(starts_ref, pieces, targets, sems)
        sums_ref[...] = jnp.zeros_like(sums_ref)
        bin_ref[...] = jnp.zeros_like(bin_ref)

    gain_one = vec_ref[1:2, :]
    d_second = dsec_ref[...]
    d_norm = d_second.astype(F32)
    for c in range(0, w_in.shape[1], FFN_CHUNK):
        cols = slice(c, c + FFN_CHUNK)
        d_pre = (dot_nt(d_second, w_ffo[cols, :]) * slope_ref[:, cols].astype(F32)).astype(BF)
        dpre_ref[:, cols] = d_pre
        bin_ref[:, cols] += fold_rows(d_pre.astype(F32))
        d_norm = d_norm + dot_nt(d_pre, w_in[:, cols])
    n_one = none_ref[...].astype(F32)
    inner = d_norm * gain_one
    d_res = rstd_ref[:, 0:1] * (inner - row_mean(inner) - n_one * row_mean(inner * n_one))
    d_branch = d_res.astype(BF)
    dbranch_ref[...] = d_branch
    datt_ref[...] = dot_nt(d_branch, w_out[...]).astype(BF)
    sums_ref[0:8, :] += fold_rows(d_norm * n_one)
    sums_ref[8:16, :] += fold_rows(d_norm)
    sums_ref[16:24, :] += fold_rows(d_branch.astype(F32))


def input_grad_kernel(count, groups, starts_ref, dbranch_ref, *refs):
    grads = refs[:groups]
    pieces = refs[groups : groups + count]
    o_ref, weight, sems = refs[groups + count :]

    @pl.when(pl.program_id(0) == 0)
    def _():
        load_pieces(starts_ref, pieces, [weight] * count, sems)

    width = dbranch_ref.shape[1]
    part = width // groups
    total = dbranch_ref[...].astype(F32)
    for g, ref in enumerate(grads):
        for n in range(3):
            first = n * width + g * part
            total = total + dot_nt(ref[:, n * part : (n + 1) * part], weight[:, first : first + part])
    o_ref[...] = total.astype(BF)


def weight_grad_rows_kernel(owner_ref, a_ref, b_ref, keep_ref, pass_ref, send_ref):
    step = pl.program_id(0)
    part = dot_tn(a_ref[...], b_ref[...]).astype(BF)

    @pl.when(step < 2)
    def _():
        send_ref[...] = part

    @pl.when(step == 2)
    def _():
        pass_ref[...] = part

    @pl.when(step == 3)
    def _():
        keep_ref[...] = part


def weight_grad_cols_kernel(slots, owner_ref, a_ref, b_ref, keep_ref, pass_ref, send_ref, sums_ref, held):
    terms = b_ref[...]
    sums_ref[...] = fold_rows(terms.astype(F32))
    part = dot_tn(a_ref[...], terms).astype(BF)
    height = keep_ref.shape[0]
    for owner in range(4):
        held[owner_ref[owner]] = part[owner * height : (owner + 1) * height]
    keep_ref[...] = held[0]
    pass_ref[...] = held[1]
    send_ref[0:height, :] = held[2]
    send_ref[height:, :] = held[3]


PARAMS = pltpu.CompilerParams(vmem_limit_bytes=VMEM_LIMIT)


def cost(flops, bytes_accessed):
    return pl.CostEstimate(flops=int(flops) // 16, bytes_accessed=int(bytes_accessed) // 16, transcendentals=0)


def whole_spec(array):
    zeros = (0,) * array.ndim
    return pl.BlockSpec(array.shape, lambda *_: zeros)


ANY = pl.BlockSpec(memory_space=pl.ANY)


def row_call(kernel, name, rows, block, scalars, blocked, fixed, pieces, outs, accs, scratch, flops):
    in_specs = (
        [pl.BlockSpec((block, a.shape[1]), lambda i, *_: (i, 0)) for a in blocked]
        + [whole_spec(a) for a in fixed]
        + [ANY] * len(pieces)
    )
    out_specs = [pl.BlockSpec((block, s.shape[1]), lambda i, *_: (i, 0)) for s in outs] + [
        whole_spec(s) for s in accs
    ]
    moved = sum(a.size * a.dtype.itemsize for a in list(blocked) + list(pieces) + list(outs))
    return pl.pallas_call(
        kernel,
        grid_spec=pltpu.PrefetchScalarGridSpec(
            num_scalar_prefetch=1,
            grid=(rows // block,),
            in_specs=in_specs,
            out_specs=out_specs,
            scratch_shapes=list(scratch) + [pltpu.SemaphoreType.DMA((len(pieces),))],
        ),
        out_shape=list(outs) + list(accs),
        compiler_params=PARAMS,
        cost_estimate=cost(flops, moved),
        name=name,
    )(scalars, *blocked, *fixed, *pieces)


def shaped(*shape, dtype=BF):
    return jax.ShapeDtypeStruct(shape, dtype)


def weight_grad(slots, a, b, name):
    rows, height = a.shape
    width = b.shape[1]
    part = height // 4
    flops = 2 * rows * height * width
    moved = 2 * (rows * height + rows * width + height * width)
    if part % 128 == 0:
        return pl.pallas_call(
            weight_grad_rows_kernel,
            grid_spec=pltpu.PrefetchScalarGridSpec(
                num_scalar_prefetch=1,
                grid=(4,),
                in_specs=[
                    pl.BlockSpec((rows, part), lambda t, s: (0, s[4 + t])),
                    pl.BlockSpec((rows, width), lambda t, s: (0, 0)),
                ],
                out_specs=[
                    pl.BlockSpec((part, width), lambda t, s: (0, 0)),
                    pl.BlockSpec((part, width), lambda t, s: (0, 0)),
                    pl.BlockSpec((part, width), lambda t, s: (jnp.minimum(t, 1), 0)),
                ],
            ),
            out_shape=[shaped(part, width), shaped(part, width), shaped(2 * part, width)],
            compiler_params=PARAMS,
            cost_estimate=cost(flops, moved),
            name=name,
        )(slots, a, b)
    block = min(width, 768)
    return pl.pallas_call(
        functools.partial(weight_grad_cols_kernel, 4),
        grid_spec=pltpu.PrefetchScalarGridSpec(
            num_scalar_prefetch=1,
            grid=(width // block,),
            in_specs=[
                pl.BlockSpec((rows, height), lambda t, s: (0, 0)),
                pl.BlockSpec((rows, block), lambda t, s: (0, t)),
            ],
            out_specs=[
                pl.BlockSpec((part, block), lambda t, s: (0, t)),
                pl.BlockSpec((part, block), lambda t, s: (0, t)),
                pl.BlockSpec((2 * part, block), lambda t, s: (0, t)),
                pl.BlockSpec((8, block), lambda t, s: (0, t)),
            ],
            scratch_shapes=[pltpu.VMEM((4, part, block), BF)],
        ),
        out_shape=[
            shaped(part, width),
            shaped(part, width),
            shaped(2 * part, width),
            shaped(8, width, dtype=F32),
        ],
        compiler_params=PARAMS,
        cost_estimate=cost(flops, moved),
        name=name,
    )(slots, a, b)


def plain_grad_kernel(a_ref, b_ref, o_ref):
    o_ref[...] = dot_tn(a_ref[...], b_ref[...]).astype(BF)


def plain_grad(a, b, name):
    rows, height = a.shape
    width = b.shape[1]
    block = 768
    tall = height > width
    steps = (height if tall else width) // block
    specs = [
        pl.BlockSpec((rows, block if tall else height), (lambda t: (0, t)) if tall else (lambda t: (0, 0))),
        pl.BlockSpec((rows, width if tall else block), (lambda t: (0, 0)) if tall else (lambda t: (0, t))),
    ]
    out = (
        pl.BlockSpec((block, width), lambda t: (t, 0)) if tall else pl.BlockSpec((height, block), lambda t: (0, t))
    )
    return pl.pallas_call(
        plain_grad_kernel,
        grid=(steps,),
        in_specs=specs,
        out_specs=out,
        out_shape=shaped(height, width),
        compiler_params=PARAMS,
        cost_estimate=cost(2 * rows * height * width, 2 * (rows * (height + width) + height * width)),
        name=name,
    )(a, b)


REDUCE_COLS = 384


def reduce_kernel(flows, *refs):
    parts = [refs[3 * f : 3 * f + 3] for f in range(flows)]
    small_ref = refs[3 * flows]
    out_ref, total_ref = refs[3 * flows + 1 : 3 * flows + 3]
    come, onward, across, owned, half_in, quarter_in, quarter, far_in, small_in, small_sum = refs[
        3 * flows + 3 : 3 * flows + 13
    ]
    sent, got, small_sent, small_got = refs[3 * flows + 13 :]
    me = lax.axis_index("shard")
    place = lax.axis_index("rep")
    y = lax.rem(place, 2)
    z = lax.rem(lax.div(place, 2), 2)
    peers = [
        {"shard": me + 1 - 2 * lax.rem(me, 2)},
        {"shard": lax.rem(me + 2, 4)},
        {"rep": place + 1 - 2 * y},
        {"rep": place + 2 - 4 * z},
        {"rep": lax.rem(place + 4, 8)},
    ]
    barrier = pltpu.get_barrier_semaphore()
    for peer in peers:
        pl.semaphore_signal(barrier, inc=1, device_id=peer, device_id_type=pl.DeviceIdType.MESH)
    pl.semaphore_wait(barrier, len(peers))

    height = owned.shape[1]
    half, fourth = height // 2, height // 4
    width = owned.shape[2]
    chunks = [(f, c) for f in range(flows) for c in range(0, width, REDUCE_COLS)]
    started = []

    def rows(start, size):
        return pl.ds(pl.multiple_of(start, 16), size)

    def send(hop, n, source, target, peer):
        copy = pltpu.make_async_remote_copy(
            src_ref=source,
            dst_ref=target,
            send_sem=sent.at[hop, n],
            recv_sem=got.at[hop, n],
            device_id=peers[peer],
            device_id_type=pl.DeviceIdType.MESH,
        )
        copy.start()
        started.append(copy)
        return copy

    def small_send(hop, source):
        copy = pltpu.make_async_remote_copy(
            src_ref=source,
            dst_ref=small_in.at[hop],
            send_sem=small_sent.at[hop],
            recv_sem=small_got.at[hop],
            device_id=peers[hop],
            device_id_type=pl.DeviceIdType.MESH,
        )
        copy.start()
        started.append(copy)
        return copy

    def plus(*terms):
        return functools.reduce(jnp.add, [t.astype(F32) for t in terms])

    mine_half = y * half
    mine_fourth = y * half + z * fourth
    copies = {}
    for n, (f, c) in enumerate(chunks):
        cols = pl.ds(c, REDUCE_COLS)
        copies[0, n] = send(0, n, parts[f][2].at[:, cols], come.at[f, :, cols], 0)
    flying = small_send(0, small_ref)
    for n, (f, c) in enumerate(chunks):
        cols = pl.ds(c, REDUCE_COLS)
        copies[0, n].wait_recv()
        onward[f, :, cols] = plus(parts[f][1][:, cols], come[f, pl.ds(height, height), cols]).astype(BF)
        copies[1, n] = send(1, n, onward.at[f, :, cols], across.at[f, :, cols], 1)

    def small_step(hop):
        flying.wait_recv()
        total = plus(small_ref[...] if hop == 0 else small_sum[hop - 1], small_in[hop])
        if hop == 4:
            total_ref[...] = total
            return None
        small_sum[hop] = total
        return small_send(hop + 1, small_sum.at[hop])

    def step(stage, n):
        f, c = chunks[n]
        cols = pl.ds(c, REDUCE_COLS)
        copies[stage, n].wait_recv()
        if stage == 1:
            owned[f, :, cols] = plus(
                parts[f][0][:, cols], come[f, pl.ds(0, height), cols], across[f, :, cols]
            ).astype(BF)
            away = owned.at[f, rows((1 - y) * half, half), cols]
            copies[2, n] = send(2, n, away, half_in.at[f, :, cols], 2)
        elif stage == 2:
            owned[f, rows(mine_half, half), cols] = plus(
                owned[f, rows(mine_half, half), cols], half_in[f, :, cols]
            ).astype(BF)
            away = owned.at[f, rows(mine_half + (1 - z) * fourth, fourth), cols]
            copies[3, n] = send(3, n, away, quarter_in.at[f, :, cols], 3)
        elif stage == 3:
            quarter[f, :, cols] = plus(owned[f, rows(mine_fourth, fourth), cols], quarter_in[f, :, cols]).astype(BF)
            copies[4, n] = send(4, n, quarter.at[f, :, cols], far_in.at[f, :, cols], 4)
        elif stage == 4:
            out_ref[f, rows(mine_fourth, fourth), cols] = plus(quarter[f, :, cols], far_in[f, :, cols]).astype(BF)
            done = out_ref.at[f, rows(mine_fourth, fourth), cols]
            copies[5, n] = send(5, n, done, done, 3)
        elif stage == 5:
            done = out_ref.at[f, rows(mine_half, half), cols]
            copies[6, n] = send(6, n, done, done, 2)

    for wave in range(len(chunks) + 5):
        for stage in range(6, 0, -1):
            n = wave - (stage - 1)
            if 0 <= n < len(chunks):
                step(stage, n)
        if wave < 5:
            flying = small_step(wave)
    for copy in started:
        copy.wait_send()


def reduce_call(terms, packed):
    flows = len(terms)
    height, width = terms[0][0].shape
    chunks = flows * (width // REDUCE_COLS)
    vmem = pl.BlockSpec(memory_space=pltpu.VMEM)
    total = flows * height * width
    return pl.pallas_call(
        functools.partial(reduce_kernel, flows),
        in_specs=[vmem] * (3 * flows + 1),
        out_specs=[vmem, vmem],
        out_shape=[shaped(flows, height, width), jax.ShapeDtypeStruct(packed.shape, F32)],
        scratch_shapes=[
            pltpu.VMEM((flows, 2 * height, width), BF),
            pltpu.VMEM((flows, height, width), BF),
            pltpu.VMEM((flows, height, width), BF),
            pltpu.VMEM((flows, height, width), BF),
            pltpu.VMEM((flows, height // 2, width), BF),
            pltpu.VMEM((flows, height // 4, width), BF),
            pltpu.VMEM((flows, height // 4, width), BF),
            pltpu.VMEM((flows, height // 4, width), BF),
            pltpu.VMEM((5,) + packed.shape, F32),
            pltpu.VMEM((4,) + packed.shape, F32),
            pltpu.SemaphoreType.DMA((7, chunks)),
            pltpu.SemaphoreType.DMA((7, chunks)),
            pltpu.SemaphoreType.DMA((5,)),
            pltpu.SemaphoreType.DMA((5,)),
        ],
        compiler_params=pltpu.CompilerParams(
            collective_id=0, has_side_effects=True, vmem_limit_bytes=40 * 2**20
        ),
        cost_estimate=cost(total, 20 * total),
        name="reduce_grads",
    )(*[t for three in terms for t in three], packed)


def swap(array, axis, bit):
    size = lax.axis_size(axis)
    return lax.ppermute(array, axis, [(i, i ^ bit) for i in range(size)])


def gather_hops(shards):
    side = lax.axis_index("rep") & 1
    halves = [s.shape[0] // 2 for s in shards]
    mine = [lax.dynamic_slice_in_dim(s, side * h, h, axis=0) for s, h in zip(shards, halves)]
    direct, core = yield [swap(m, "shard", 2) for m in mine], [swap(s, "shard", 1) for s in shards]
    relayed, cross = yield [swap(d, "rep", 1) for d in direct], [swap(d, "shard", 1) for d in direct]
    cross_relayed = yield [swap(r, "shard", 1) for r in relayed]
    return [list(p) for p in zip(shards, core, direct, relayed, cross, cross_relayed)]


def piece_starts(shard):
    height = shard.shape[0]
    me = lax.axis_index("shard")
    side = lax.axis_index("rep") & 1
    half = height // 2
    near, core, far, cross = [(me ^ o) * height for o in range(4)]
    return [near, core, far + side * half, far + (1 - side) * half, cross + side * half, cross + (1 - side) * half]


def added(*terms):
    return functools.reduce(jnp.add, [t.astype(F32) for t in terms]).astype(BF)


class Flow:
    def __init__(self, hops):
        self.hops = hops
        self.result = None
        self.flying = next(hops)

    def land(self, arrived):
        try:
            self.flying = self.hops.send(arrived)
        except StopIteration as stop:
            self.flying, self.result = None, stop.value


class Line:
    def __init__(self):
        self.flows = []
        self.recent = []

    def step(self, arrays, flows=None):
        moving = [f for f in (self.flows if flows is None else flows) if f.flying is not None]
        held = self.recent
        arrays, arrived, held = lax.optimization_barrier((arrays, [f.flying for f in moving], held))
        for flow, value in zip(moving, arrived):
            flow.land(value)
        self.recent = []
        return arrays

    def start(self, hops):
        flow = Flow(hops)
        self.flows.append(flow)
        return flow


def group_sum(a, b, name):
    return lax.psum_scatter(plain_grad(a, b, name), "shard", scatter_dimension=0, tiled=True)


def replica_sum(owned):
    return lax.psum(owned, "rep").astype(F32)


def reduce_plain(a, b, name):
    return replica_sum(group_sum(a, b, name))


def local(
    tokens,
    segment_ids,
    cotangent,
    w_qkv,
    b_query,
    b_value,
    w_out,
    b_out,
    gain_one,
    shift_one,
    w_in,
    b_in,
    w_ffo,
    b_ffo,
    gain_two,
    shift_two,
):
    micro, sequences, length, width = tokens.shape
    total = micro * sequences
    rows = total * length
    group = lax.axis_size("shard")
    hidden_width = w_in.shape[1]
    x = tokens.reshape(rows, width)
    seg = segment_ids.reshape(total, length)
    cot = cotangent.reshape(rows, width)
    me = lax.axis_index("shard")
    direct = group == 4 and lax.axis_size("rep") == 8

    part = b_query.shape[0]
    line = Line()
    small_shards = (b_query, b_value, b_out, gain_one, shift_one, b_ffo, gain_two, shift_two, b_in)
    small = jnp.concatenate(small_shards).reshape(1, -1)
    if direct:
        qkv_flow = Flow(gather_hops([w_qkv]))
        near = swap(small, "shard", 1)
        pair = jnp.concatenate([small, near], axis=0)
        four = jnp.concatenate([pair, swap(pair, "shard", 2)], axis=0)
        order = [jnp.bitwise_xor(me, o) for o in range(4)]
        small_full = jnp.concatenate([lax.dynamic_slice_in_dim(four, o, 1, axis=0) for o in order], axis=0)
        (later,) = line.step([w_ffo], [qkv_flow])
        later_flow = Flow(gather_hops([later]))
        seg = line.step(seg, [qkv_flow])
        x_first = line.step(x, [qkv_flow])
        (qkv_pieces,) = qkv_flow.result
        qkv_starts = jnp.stack(piece_starts(w_qkv)).astype(jnp.int32)
        layer_lists = [[lax.all_gather(w, "shard", axis=0, tiled=True)] for w in (w_out, w_in)]
        layer_starts = jnp.stack([jnp.int32(0)] * 2 + piece_starts(w_ffo)).astype(jnp.int32)
        counts = (1, 1, 6)
    else:
        small_full = lax.all_gather(small, "shard", axis=0, tiled=True)
        qkv_pieces, *layer_lists = [
            [lax.all_gather(w, "shard", axis=0, tiled=True)] for w in (w_qkv, w_out, w_in, w_ffo)
        ]
        x_first = x
        qkv_starts = jnp.zeros((1,), jnp.int32)
        layer_starts = jnp.zeros((3,), jnp.int32)
        counts = (1, 1, 1)
    small_full = small_full.astype(F32)
    vectors = [small_full[:, i * part : (i + 1) * part].reshape(1, -1) for i in range(8)]
    bias_all = jnp.concatenate([vectors[0], jnp.zeros_like(vectors[0]), vectors[1]], axis=1)
    vec = jnp.concatenate(vectors[2:] + [jnp.zeros((2, width), F32)], axis=0)
    bias_in = small_full[:, 8 * part :].reshape(1, -1)

    windows = windows_of(seg)
    block = 256
    (projected,) = row_call(
        functools.partial(project_kernel, len(qkv_pieces)),
        "project",
        rows,
        block,
        qkv_starts,
        [x_first],
        [bias_all],
        qkv_pieces,
        [shaped(rows, 3 * width)],
        [],
        [pltpu.VMEM((width, 3 * width), BF)],
        6 * rows * width * width,
    )
    if direct:
        projected = line.step(projected, [later_flow])
    attended, lse = attend_forward(projected, windows, total)
    if direct:
        attended = line.step(attended, [later_flow])
        attended = line.step(attended, [later_flow])
        layer_lists = layer_lists + later_flow.result
    layer_pieces = sum(layer_lists, [])
    weights_scratch = [
        pltpu.VMEM((width, width), BF),
        pltpu.VMEM((width, hidden_width), BF),
        pltpu.VMEM((hidden_width, width), BF),
    ]
    layer_flops = 2 * rows * width * (width + 2 * hidden_width)
    output, normed, n_one, rstd_one, d_second, hidden, slope, sums_two = row_call(
        functools.partial(layer_forward_kernel, counts),
        "layer_forward",
        rows,
        block,
        layer_starts,
        [x, attended, cot],
        [vec, bias_in],
        layer_pieces,
        [
            shaped(rows, width),
            shaped(rows, width),
            shaped(rows, width),
            shaped(rows, 128, dtype=F32),
            shaped(rows, width),
            shaped(rows, hidden_width),
            shaped(rows, hidden_width),
        ],
        [shaped(24, width, dtype=F32)],
        weights_scratch,
        layer_flops,
    )

    place = [jnp.bitwise_xor(me, o) for o in range(4)]
    slots = jnp.stack(
        [(p & 1) * 2 + lax.shift_right_logical(p, 1) for p in place] + [jnp.bitwise_xor(me, j) for j in (1, 3, 2, 0)]
    ).astype(jnp.int32)

    def weight_terms(a, b, name):
        if direct:
            *terms, sums = weight_grad(slots, a, b, name)
            return terms, sums
        return reduce_plain(a, b, name), fold_rows(b.astype(F32))

    owned_ffo = group_sum(hidden, d_second, "grad_ffo")
    d_pre, d_branch, d_attended, sums_one, sums_in = row_call(
        functools.partial(layer_backward_kernel, counts),
        "layer_backward",
        rows,
        block,
        layer_starts,
        [d_second, slope, n_one, rstd_one],
        [vec],
        layer_pieces,
        [shaped(rows, hidden_width), shaped(rows, width), shaped(rows, width)],
        [shaped(24, width, dtype=F32), shaped(8, hidden_width, dtype=F32)],
        weights_scratch,
        layer_flops,
    )
    owned_in = group_sum(normed, d_pre, "grad_in")
    grad_out, _ = weight_terms(attended, d_branch, "grad_out")
    groups = 3
    d_heads, grads, head_sums = [], [], []
    for g in range(groups):
        if g == 0:
            d_attended, owned_ffo = lax.optimization_barrier((d_attended, owned_ffo))
            grad_ffo = replica_sum(owned_ffo)
        elif direct:
            d_attended, _ = lax.optimization_barrier((d_attended, d_heads[-1]))
        d_head = attend_backward(projected, d_attended, attended, lse, windows, total, g, groups)
        terms, sums = weight_terms(x, d_head, "grad_qkv")
        d_heads.append(d_head)
        grads.append(terms)
        head_sums.append(sums)

    def folded(sums):
        return [jnp.sum(sums[i : i + 8], axis=0) for i in range(0, sums.shape[0], 8)]

    d_gain_two, d_shift_two, d_ffo_bias = folded(sums_two)
    d_gain_one, d_shift_one, d_out_bias = folded(sums_one)
    (d_in_bias,) = folded(sums_in)
    cut = width // groups
    head_sums = [jnp.sum(s, axis=0) for s in head_sums]
    d_query_bias = jnp.concatenate([s[:cut] for s in head_sums])
    d_value_bias = jnp.concatenate([s[2 * cut :] for s in head_sums])
    smalls = (
        d_query_bias, d_value_bias, d_out_bias, d_gain_one, d_shift_one, d_ffo_bias, d_gain_two, d_shift_two,
        d_in_bias,
    )
    packed = jnp.concatenate([s.reshape(group, -1) for s in smalls], axis=1)
    (d_tokens,) = row_call(
        functools.partial(input_grad_kernel, len(qkv_pieces), groups),
        "input_grad",
        rows,
        block,
        qkv_starts,
        [d_branch, *d_heads],
        [],
        qkv_pieces,
        [shaped(rows, width)],
        [],
        [pltpu.VMEM((width, 3 * width), BF)],
        6 * rows * width * width,
    )
    packed, grad_ffo, owned_in = lax.optimization_barrier((packed, grad_ffo, owned_in))
    grad_in = replica_sum(owned_in)
    if direct:
        reduced, packed = reduce_call([grad_out, *grads], packed)
        grad_out, *grads = [r.astype(F32) for r in reduced]
    else:
        packed = lax.psum(packed, ("shard", "rep"))
    grad_qkv = jnp.concatenate([g[:, n * cut : (n + 1) * cut] for n in range(3) for g in grads], axis=1)
    mine = lax.dynamic_index_in_dim(packed, me, 0, keepdims=False)
    sm = [mine[i * part : (i + 1) * part] for i in range(8)]
    gqb, gvb, gob, gg1, gs1, gfb, gg2, gs2 = sm
    gib = mine[8 * part :]
    return (
        output.reshape(tokens.shape),
        d_tokens.reshape(tokens.shape),
        grad_qkv,
        gqb,
        gvb,
        grad_out,
        gob,
        gg1,
        gs1,
        grad_in,
        gib,
        grad_ffo,
        gfb,
        gg2,
        gs2,
    )


def solution(mesh):
    data = P(None, ("shard", "rep"), None, None)
    matrix = P("shard", None)
    vector = P("shard")
    return jax.shard_map(
        local,
        mesh=mesh,
        in_specs=(
            data,
            P(None, ("shard", "rep"), None),
            data,
            matrix,
            vector,
            vector,
            matrix,
            vector,
            vector,
            vector,
            matrix,
            vector,
            matrix,
            vector,
            vector,
            vector,
        ),
        out_specs=(
            data,
            data,
            matrix,
            vector,
            vector,
            matrix,
            vector,
            vector,
            vector,
            matrix,
            vector,
            matrix,
            vector,
            vector,
            vector,
        ),
        check_vma=False,
    )
```

```python
import functools
import math

import jax
import jax.numpy as jnp
from jax import lax
from jax.experimental import pallas as pl
from jax.experimental.pallas import tpu as pltpu
from jax.sharding import PartitionSpec as P

HEADS = 12
HEAD_DIM = 64
PAIR = 2 * HEAD_DIM
TILE = 128

epsilon = 1e-05
masked_score = -1e30
BF = jnp.bfloat16
F32 = jnp.float32
VMEM_LIMIT = 60 * 2**20


def dot_nn(a, b):
    return lax.dot_general(a, b, (((1,), (0,)), ((), ())), preferred_element_type=F32)


def dot_nt(a, b):
    return lax.dot_general(a, b, (((1,), (1,)), ((), ())), preferred_element_type=F32)


def dot_tn(a, b):
    return lax.dot_general(a, b, (((0,), (0,)), ((), ())), preferred_element_type=F32)


def head_rows(value):
    lane = lax.broadcasted_iota(jnp.int32, (1, PAIR), 1)
    first = jnp.where(lane < HEAD_DIM, value, 0.0).astype(BF)
    second = jnp.where(lane < HEAD_DIM, 0.0, value).astype(BF)
    return first, second


def stack_heads(block, rows):
    return jnp.concatenate([block * rows[0], block * rows[1]], axis=0)


def diagonal_back(transposed):
    kept = jnp.concatenate(
        [transposed[:HEAD_DIM, :TILE], transposed[HEAD_DIM:, TILE:]], axis=0
    )
    return kept.T


def for_windows(count, tiles, body):
    sizes = [t for t in range(1, tiles + 1) if t < 7 or t == tiles]
    below = 0
    for size in sizes:
        @pl.when((count > below) & (count <= size))
        def _(size=size):
            body(size)

        below = size


def attend_forward_kernel(pairs, tiles, low_ref, count_ref, q_ref, k_ref, v_ref, kseg_ref, qseg_ref, o_ref, lse_ref):
    place = pl.program_id(0) * tiles + pl.program_id(1)
    low = low_ref[place]
    count = count_ref[place]
    rows_of = head_rows(1.0 / math.sqrt(HEAD_DIM))

    def window(size):
        start = jnp.minimum(low, tiles - size) * TILE
        chunks = [pl.ds(pl.multiple_of(start + c * TILE, TILE), TILE) for c in range(size)]
        whole = pl.ds(pl.multiple_of(start, TILE), size * TILE)
        masks = [kseg_ref[c, :] == qseg_ref[0] for c in chunks]
        def first(p):
            lanes = slice(p * PAIR, (p + 1) * PAIR)
            queries = stack_heads(q_ref[:, lanes], rows_of)
            scores = []
            for c, mask in zip(chunks, masks):
                part = dot_nt(k_ref[c, lanes], queries)
                scores.append(
                    jnp.concatenate(
                        [
                            jnp.where(mask, part[:, :TILE], masked_score),
                            jnp.where(mask, part[:, TILE:], masked_score),
                        ],
                        axis=1,
                    )
                )
            return scores

        def second(p, scores):
            lanes = slice(p * PAIR, (p + 1) * PAIR)
            top = functools.reduce(jnp.maximum, [jnp.max(s, axis=0, keepdims=True) for s in scores])
            exps = [jnp.exp(s - top) for s in scores]
            total = functools.reduce(jnp.add, [jnp.sum(e, axis=0, keepdims=True) for e in exps])
            weights = jnp.concatenate([e.astype(BF) for e in exps], axis=0)
            mixed = dot_tn(v_ref[whole, lanes], weights) / total
            o_ref[:, lanes] = diagonal_back(mixed).astype(BF)
            lse_ref[0, p : p + 1, :] = top + jnp.log(total)

        ready = first(0)
        for p in range(pairs):
            after = first(p + 1) if p + 1 < pairs else None
            second(p, ready)
            ready = after

    for_windows(count, tiles, window)


def attend_backward_kernel(
    pairs, tiles, low_ref, count_ref, q_ref, k_ref, v_ref, do_ref, o_ref, lse_ref, kseg_ref, qseg_ref,
    out_ref, dk_acc, dv_acc,
):
    block = pl.program_id(2)
    first_pair = pl.program_id(1) * pairs
    place = pl.program_id(0) * tiles + block
    low = low_ref[place]
    count = count_ref[place]
    part = pairs * PAIR
    scale = 1.0 / math.sqrt(HEAD_DIM)
    scaled_rows = head_rows(scale)
    plain_rows = head_rows(1.0)

    @pl.when(block == 0)
    def _():
        dk_acc[...] = jnp.zeros_like(dk_acc)
        dv_acc[...] = jnp.zeros_like(dv_acc)

    def window(size):
        start = jnp.minimum(low, tiles - size) * TILE
        chunks = [pl.ds(pl.multiple_of(start + c * TILE, TILE), TILE) for c in range(size)]
        whole = pl.ds(pl.multiple_of(start, TILE), size * TILE)
        masks = [kseg_ref[c, :] == qseg_ref[0] for c in chunks]
        mine = pl.ds(pl.multiple_of(block * TILE, TILE), TILE)
        for p in range(pairs):
            lanes = slice(p * PAIR, (p + 1) * PAIR)
            queries = stack_heads(q_ref[:, lanes], scaled_rows)
            grads = do_ref[:, lanes]
            stacked = stack_heads(grads, plain_rows)
            product = (grads.astype(F32) * o_ref[:, lanes].astype(F32)).T
            row_dot = jnp.concatenate(
                [
                    jnp.sum(product[:HEAD_DIM], axis=0, keepdims=True),
                    jnp.sum(product[HEAD_DIM:], axis=0, keepdims=True),
                ],
                axis=1,
            )
            lse = lse_ref[0, pl.ds(first_pair + p, 1), :]
            kept = []
            weights = []
            all_scores = dot_nt(k_ref[whole, lanes], queries)
            all_d_probs = dot_nt(v_ref[whole, lanes], stacked)
            for n, mask in enumerate(masks):
                rows_n = slice(n * TILE, (n + 1) * TILE)
                part_scores = all_scores[rows_n] - lse
                d_probs = all_d_probs[rows_n]
                probs = jnp.exp(
                    jnp.concatenate(
                        [
                            jnp.where(mask, part_scores[:, :TILE], masked_score),
                            jnp.where(mask, part_scores[:, TILE:], masked_score),
                        ],
                        axis=1,
                    )
                )
                kept.append((probs * (d_probs - row_dot)).astype(BF))
                weights.append(probs.astype(BF))
            kept = jnp.concatenate(kept, axis=0)
            weights = jnp.concatenate(weights, axis=0)
            dv_acc[whole, lanes] += dot_nn(weights, stacked)
            dk_acc[whole, lanes] += dot_nn(kept, queries)
            mixed = dot_tn(k_ref[whole, lanes], kept) * scale
            out_ref[mine, lanes] = diagonal_back(mixed).astype(BF)

    for_windows(count, tiles, window)

    @pl.when(block == tiles - 1)
    def _():
        out_ref[:, part : 2 * part] = dk_acc[...].astype(BF)
        out_ref[:, 2 * part :] = dv_acc[...].astype(BF)


def windows_of(segments):
    sequences, length = segments.shape
    tiles = length // TILE
    blocked = segments.reshape(sequences, tiles, TILE)
    first = blocked[:, :, 0]
    last = blocked[:, :, TILE - 1]
    starts = jnp.sum((segments[:, None, :] < first[:, :, None]).astype(jnp.int32), axis=-1)
    ends = jnp.sum((segments[:, None, :] <= last[:, :, None]).astype(jnp.int32), axis=-1)
    bits = TILE.bit_length() - 1
    low = lax.shift_right_logical(starts, bits)
    count = lax.shift_right_logical(ends + TILE - 1, bits) - low
    key_ids = jnp.broadcast_to(segments.reshape(sequences * length, 1), (sequences * length, TILE))
    query_ids = blocked.reshape(sequences * tiles, 1, TILE)
    return low.reshape(-1), count.reshape(-1), key_ids, query_ids


def attend_forward(projected, windows, sequences):
    low, count, key_ids, query_ids = windows
    rows = projected.shape[0]
    width = projected.shape[1] // 3
    length = rows // sequences
    tiles = length // TILE
    pairs = width // PAIR
    return pl.pallas_call(
        functools.partial(attend_forward_kernel, pairs, tiles),
        grid_spec=pltpu.PrefetchScalarGridSpec(
            num_scalar_prefetch=2,
            grid=(sequences, tiles),
            in_specs=[
                pl.BlockSpec((TILE, width), lambda s, b, *_: (s * tiles + b, 0)),
                pl.BlockSpec((length, width), lambda s, b, *_: (s, 1)),
                pl.BlockSpec((length, width), lambda s, b, *_: (s, 2)),
                pl.BlockSpec((length, TILE), lambda s, b, *_: (s, 0)),
                pl.BlockSpec((1, 1, TILE), lambda s, b, *_: (s * tiles + b, 0, 0)),
            ],
            out_specs=[
                pl.BlockSpec((TILE, width), lambda s, b, *_: (s * tiles + b, 0)),
                pl.BlockSpec((1, 8, 2 * TILE), lambda s, b, *_: (s * tiles + b, 0, 0)),
            ],
        ),
        out_shape=[
            jax.ShapeDtypeStruct((rows, width), BF),
            jax.ShapeDtypeStruct((sequences * tiles, 8, 2 * TILE), F32),
        ],
        compiler_params=pltpu.CompilerParams(vmem_limit_bytes=VMEM_LIMIT),
        cost_estimate=cost(8 * 10**9, 16 * 10**6),
        name="attend_forward",
    )(low, count, projected, projected, projected, key_ids, query_ids)


def attend_backward(projected, d_attended, attended, lse, windows, sequences, groups):
    low, count, key_ids, query_ids = windows
    rows = projected.shape[0]
    width = projected.shape[1] // 3
    length = rows // sequences
    tiles = length // TILE
    part = width // groups
    pairs = part // PAIR
    query_spec = pl.BlockSpec((TILE, part), lambda s, g, b, *_: (s * tiles + b, g))
    return pl.pallas_call(
        functools.partial(attend_backward_kernel, pairs, tiles),
        grid_spec=pltpu.PrefetchScalarGridSpec(
            num_scalar_prefetch=2,
            grid=(sequences, groups, tiles),
            in_specs=[
                query_spec,
                pl.BlockSpec((length, part), lambda s, g, b, *_: (s, groups + g)),
                pl.BlockSpec((length, part), lambda s, g, b, *_: (s, 2 * groups + g)),
                query_spec,
                query_spec,
                pl.BlockSpec((1, 8, 2 * TILE), lambda s, g, b, *_: (s * tiles + b, 0, 0)),
                pl.BlockSpec((length, TILE), lambda s, g, b, *_: (s, 0)),
                pl.BlockSpec((1, 1, TILE), lambda s, g, b, *_: (s * tiles + b, 0, 0)),
            ],
            out_specs=pl.BlockSpec((length, 3 * part), lambda s, g, b, *_: (s, g)),
            scratch_shapes=[pltpu.VMEM((length, part), F32), pltpu.VMEM((length, part), F32)],
        ),
        out_shape=jax.ShapeDtypeStruct((rows, 3 * width), BF),
        compiler_params=pltpu.CompilerParams(vmem_limit_bytes=VMEM_LIMIT),
        cost_estimate=cost(30 * 10**9, 30 * 10**6),
        name="attend_backward",
    )(low, count, projected, projected, projected, d_attended, attended, lse, key_ids, query_ids)


def row_mean(values):
    return jnp.mean(values, axis=-1, keepdims=True)


def fold_rows(values):
    rows, width = values.shape
    return jnp.sum(values.reshape(rows // 8, 8, width), axis=0)


def load_pieces(starts_ref, pieces, targets, sems):
    copies = []
    for n, (piece, target) in enumerate(zip(pieces, targets)):
        height = piece.shape[0]
        start = pl.multiple_of(starts_ref[n], math.gcd(height, 128))
        copies.append(pltpu.make_async_copy(piece, target.at[pl.ds(start, height)], sems.at[n]))
    for copy in copies:
        copy.start()
    for copy in copies:
        copy.wait()


def gelu_parts(values):
    bell = jnp.exp2(values * values * (-0.5 * math.log2(math.e)))
    below = 1.0 + jnp.abs(values) * (0.3275911 / math.sqrt(2.0))
    t = pl.reciprocal(below, approx=True)
    t = t * (2.0 - below * t)
    t = t * (2.0 - below * t)
    poly = t * (
        0.5 * 0.254829592
        + t * (0.5 * -0.284496736 + t * (0.5 * 1.421413741 + t * (0.5 * -1.453152027 + t * (0.5 * 1.061405429))))
    )
    tail = poly * bell
    phi = jnp.where(values >= 0.0, 1.0 - tail, tail)
    return values * phi, phi + values * bell * (1.0 / math.sqrt(2.0 * math.pi))


def project_kernel(count, starts_ref, x_ref, bias_ref, *refs):
    pieces = refs[:count]
    o_ref, weight, sems = refs[count:]

    @pl.when(pl.program_id(0) == 0)
    def _():
        load_pieces(starts_ref, pieces, [weight] * count, sems)

    o_ref[...] = (dot_nn(x_ref[...], weight[...]) + bias_ref[...]).astype(BF)


FFN_CHUNK = 512


def layer_forward_kernel(
    counts, starts_ref, x_ref, att_ref, cot_ref, vec_ref, bin_ref, *refs
):
    total = sum(counts)
    pieces = refs[:total]
    (
        out_ref, normed_ref, none_ref, rstd_ref, dsec_ref, hidden_ref, slope_ref, sums_ref,
        w_out, w_in, w_ffo, sems,
    ) = refs[total:]
    targets = [w_out] * counts[0] + [w_in] * counts[1] + [w_ffo] * counts[2]

    @pl.when(pl.program_id(0) == 0)
    def _():
        load_pieces(starts_ref, pieces, targets, sems)
        sums_ref[...] = jnp.zeros_like(sums_ref)

    b_out, gain_one, shift_one, b_ffo, gain_two, shift_two = [vec_ref[i : i + 1, :] for i in range(6)]
    res = x_ref[...].astype(F32) + (dot_nn(att_ref[...], w_out[...]) + b_out)
    center = res - row_mean(res)
    rstd = lax.rsqrt(row_mean(center * center) + epsilon)
    n_one = center * rstd
    normed = (n_one * gain_one + shift_one).astype(BF)
    normed_ref[...] = normed
    none_ref[...] = n_one.astype(BF)
    rstd_ref[...] = jnp.broadcast_to(rstd, rstd_ref.shape)
    hidden_width = w_in.shape[1]
    second = None
    pres = []
    for c in range(0, hidden_width, FFN_CHUNK):
        cols = slice(c, c + FFN_CHUNK)
        pre = dot_nn(normed, w_in[:, cols]) + bin_ref[:, cols]
        value, slope = gelu_parts(pre)
        value = value.astype(BF)
        hidden_ref[:, cols] = value
        slope_ref[:, cols] = slope.astype(BF)
        term = dot_nn(value, w_ffo[cols, :])
        second = term if second is None else second + term
    res = normed.astype(F32) + (second + b_ffo)
    center = res - row_mean(res)
    rstd = lax.rsqrt(row_mean(center * center) + epsilon)
    n_two = center * rstd
    out_ref[...] = (n_two * gain_two + shift_two).astype(BF)
    cot = cot_ref[...].astype(F32)
    inner = cot * gain_two
    d_second = (rstd * (inner - row_mean(inner) - n_two * row_mean(inner * n_two))).astype(BF)
    dsec_ref[...] = d_second
    sums_ref[0:8, :] += fold_rows(cot * n_two)
    sums_ref[8:16, :] += fold_rows(cot)
    sums_ref[16:24, :] += fold_rows(d_second.astype(F32))


def layer_backward_kernel(counts, starts_ref, dsec_ref, slope_ref, none_ref, rstd_ref, vec_ref, *refs):
    total = sum(counts)
    pieces = refs[:total]
    dpre_ref, dbranch_ref, datt_ref, sums_ref, bin_ref, w_out, w_in, w_ffo, sems = refs[total:]
    targets = [w_out] * counts[0] + [w_in] * counts[1] + [w_ffo] * counts[2]

    @pl.when(pl.program_id(0) == 0)
    def _():
        load_pieces(starts_ref, pieces, targets, sems)
        sums_ref[...] = jnp.zeros_like(sums_ref)
        bin_ref[...] = jnp.zeros_like(bin_ref)

    gain_one = vec_ref[1:2, :]
    d_second = dsec_ref[...]
    d_norm = d_second.astype(F32)
    for c in range(0, w_in.shape[1], FFN_CHUNK):
        cols = slice(c, c + FFN_CHUNK)
        d_pre = (dot_nt(d_second, w_ffo[cols, :]) * slope_ref[:, cols].astype(F32)).astype(BF)
        dpre_ref[:, cols] = d_pre
        bin_ref[:, cols] += fold_rows(d_pre.astype(F32))
        d_norm = d_norm + dot_nt(d_pre, w_in[:, cols])
    n_one = none_ref[...].astype(F32)
    inner = d_norm * gain_one
    d_res = rstd_ref[:, 0:1] * (inner - row_mean(inner) - n_one * row_mean(inner * n_one))
    d_branch = d_res.astype(BF)
    dbranch_ref[...] = d_branch
    datt_ref[...] = dot_nt(d_branch, w_out[...]).astype(BF)
    sums_ref[0:8, :] += fold_rows(d_norm * n_one)
    sums_ref[8:16, :] += fold_rows(d_norm)
    sums_ref[16:24, :] += fold_rows(d_branch.astype(F32))


def input_grad_kernel(count, groups, starts_ref, dbranch_ref, *refs):
    grads = refs[0]
    pieces = refs[1 : 1 + count]
    o_ref, weight, sems = refs[1 + count :]

    @pl.when(pl.program_id(0) == 0)
    def _():
        load_pieces(starts_ref, pieces, [weight] * count, sems)

    width = dbranch_ref.shape[1]
    part = width // groups
    total = dbranch_ref[...].astype(F32)
    for g in range(groups):
        for n in range(3):
            here = (3 * g + n) * part
            first = n * width + g * part
            total = total + dot_nt(grads[:, here : here + part], weight[:, first : first + part])
    o_ref[...] = total.astype(BF)


def weight_grad_cols_kernel(slots, owner_ref, a_ref, b_ref, keep_ref, pass_ref, send_ref, sums_ref, held):
    terms = b_ref[...]
    sums_ref[...] = fold_rows(terms.astype(F32))
    part = dot_tn(a_ref[...], terms).astype(BF)
    height = keep_ref.shape[0]
    for owner in range(4):
        held[owner_ref[owner]] = part[owner * height : (owner + 1) * height]
    keep_ref[...] = held[0]
    pass_ref[...] = held[1]
    send_ref[0:height, :] = held[2]
    send_ref[height:, :] = held[3]


PARAMS = pltpu.CompilerParams(vmem_limit_bytes=VMEM_LIMIT)


def cost(flops, bytes_accessed):
    return pl.CostEstimate(flops=int(flops) // 16, bytes_accessed=int(bytes_accessed) // 16, transcendentals=0)


def whole_spec(array):
    zeros = (0,) * array.ndim
    return pl.BlockSpec(array.shape, lambda *_: zeros)


ANY = pl.BlockSpec(memory_space=pl.ANY)


def row_call(kernel, name, rows, block, scalars, blocked, fixed, pieces, outs, accs, scratch, flops):
    in_specs = (
        [pl.BlockSpec((block, a.shape[1]), lambda i, *_: (i, 0)) for a in blocked]
        + [whole_spec(a) for a in fixed]
        + [ANY] * len(pieces)
    )
    out_specs = [pl.BlockSpec((block, s.shape[1]), lambda i, *_: (i, 0)) for s in outs] + [
        whole_spec(s) for s in accs
    ]
    moved = sum(a.size * a.dtype.itemsize for a in list(blocked) + list(pieces) + list(outs))
    return pl.pallas_call(
        kernel,
        grid_spec=pltpu.PrefetchScalarGridSpec(
            num_scalar_prefetch=1,
            grid=(rows // block,),
            in_specs=in_specs,
            out_specs=out_specs,
            scratch_shapes=list(scratch) + [pltpu.SemaphoreType.DMA((len(pieces),))],
        ),
        out_shape=list(outs) + list(accs),
        compiler_params=PARAMS,
        cost_estimate=cost(flops, moved),
        name=name,
    )(scalars, *blocked, *fixed, *pieces)


def shaped(*shape, dtype=BF):
    return jax.ShapeDtypeStruct(shape, dtype)


def weight_grad(slots, a, b, name):
    rows, height = a.shape
    width = b.shape[1]
    part = height // 4
    flops = 2 * rows * height * width
    moved = 2 * (rows * height + rows * width + height * width)
    block = 384
    return pl.pallas_call(
        functools.partial(weight_grad_cols_kernel, 4),
        grid_spec=pltpu.PrefetchScalarGridSpec(
            num_scalar_prefetch=1,
            grid=(width // block,),
            in_specs=[
                pl.BlockSpec((rows, height), lambda t, s: (0, 0)),
                pl.BlockSpec((rows, block), lambda t, s: (0, t)),
            ],
            out_specs=[
                pl.BlockSpec((part, block), lambda t, s: (0, t)),
                pl.BlockSpec((part, block), lambda t, s: (0, t)),
                pl.BlockSpec((2 * part, block), lambda t, s: (0, t)),
                pl.BlockSpec((8, block), lambda t, s: (0, t)),
            ],
            scratch_shapes=[pltpu.VMEM((4, part, block), BF)],
        ),
        out_shape=[
            shaped(part, width),
            shaped(part, width),
            shaped(2 * part, width),
            shaped(8, width, dtype=F32),
        ],
        compiler_params=PARAMS,
        cost_estimate=cost(flops, moved),
        name=name,
    )(slots, a, b)


def plain_grad_kernel(a_ref, b_ref, o_ref):
    o_ref[...] = dot_tn(a_ref[...], b_ref[...]).astype(BF)


def plain_grad(a, b, name):
    rows, height = a.shape
    width = b.shape[1]
    block = 768
    tall = height > width
    steps = (height if tall else width) // block
    specs = [
        pl.BlockSpec((rows, block if tall else height), (lambda t: (0, t)) if tall else (lambda t: (0, 0))),
        pl.BlockSpec((rows, width if tall else block), (lambda t: (0, 0)) if tall else (lambda t: (0, t))),
    ]
    out = (
        pl.BlockSpec((block, width), lambda t: (t, 0)) if tall else pl.BlockSpec((height, block), lambda t: (0, t))
    )
    return pl.pallas_call(
        plain_grad_kernel,
        grid=(steps,),
        in_specs=specs,
        out_specs=out,
        out_shape=shaped(height, width),
        compiler_params=PARAMS,
        cost_estimate=cost(2 * rows * height * width, 2 * (rows * (height + width) + height * width)),
        name=name,
    )(a, b)


REDUCE_COLS = 768
REDUCE_LAG = 1


def reduce_kernel(flows, *refs):
    parts = [refs[3 * f : 3 * f + 3] for f in range(flows)]
    small_ref = refs[3 * flows]
    out_ref, total_ref = refs[3 * flows + 1 : 3 * flows + 3]
    come, onward, across, owned, half_in, quarter_in, quarter, far_in, small_in, small_sum = refs[
        3 * flows + 3 : 3 * flows + 13
    ]
    sent, got, small_sent, small_got = refs[3 * flows + 13 :]
    me = lax.axis_index("shard")
    place = lax.axis_index("rep")
    y = lax.rem(place, 2)
    z = lax.rem(lax.div(place, 2), 2)
    peers = [
        {"shard": me + 1 - 2 * lax.rem(me, 2)},
        {"shard": lax.rem(me + 2, 4)},
        {"rep": place + 1 - 2 * y},
        {"rep": place + 2 - 4 * z},
        {"rep": lax.rem(place + 4, 8)},
    ]
    barrier = pltpu.get_barrier_semaphore()
    for peer in peers:
        pl.semaphore_signal(barrier, inc=1, device_id=peer, device_id_type=pl.DeviceIdType.MESH)
    pl.semaphore_wait(barrier, len(peers))

    height = owned.shape[1]
    half, fourth = height // 2, height // 4
    width = owned.shape[2]
    chunks = [(f, c) for f in range(flows) for c in range(0, width, REDUCE_COLS)]
    started = []

    def rows(start, size):
        return pl.ds(pl.multiple_of(start, 16), size)

    def send(hop, n, source, target, peer):
        copy = pltpu.make_async_remote_copy(
            src_ref=source,
            dst_ref=target,
            send_sem=sent.at[hop, n],
            recv_sem=got.at[hop, n],
            device_id=peers[peer],
            device_id_type=pl.DeviceIdType.MESH,
        )
        copy.start()
        started.append(copy)
        return copy

    def small_send(hop, source):
        copy = pltpu.make_async_remote_copy(
            src_ref=source,
            dst_ref=small_in.at[hop],
            send_sem=small_sent.at[hop],
            recv_sem=small_got.at[hop],
            device_id=peers[hop],
            device_id_type=pl.DeviceIdType.MESH,
        )
        copy.start()
        started.append(copy)
        return copy

    def plus(*terms):
        return functools.reduce(jnp.add, [t.astype(F32) for t in terms])

    mine_half = y * half
    mine_fourth = y * half + z * fourth
    copies = {}
    for n, (f, c) in enumerate(chunks):
        cols = pl.ds(c, REDUCE_COLS)
        copies[0, n] = send(0, n, parts[f][2].at[:, cols], come.at[f, :, cols], 0)
    flying = small_send(0, small_ref)
    for n, (f, c) in enumerate(chunks):
        cols = pl.ds(c, REDUCE_COLS)
        copies[0, n].wait_recv()
        onward[f, :, cols] = plus(parts[f][1][:, cols], come[f, pl.ds(height, height), cols]).astype(BF)
        copies[1, n] = send(1, n, onward.at[f, :, cols], across.at[f, :, cols], 1)

    def small_step(hop):
        flying.wait_recv()
        total = plus(small_ref[...] if hop == 0 else small_sum[hop - 1], small_in[hop])
        if hop == 4:
            total_ref[...] = total
            return None
        small_sum[hop] = total
        return small_send(hop + 1, small_sum.at[hop])

    def step(stage, n):
        f, c = chunks[n]
        cols = pl.ds(c, REDUCE_COLS)
        copies[stage, n].wait_recv()
        if stage == 1:
            owned[f, :, cols] = plus(
                parts[f][0][:, cols], come[f, pl.ds(0, height), cols], across[f, :, cols]
            ).astype(BF)
            away = owned.at[f, rows((1 - y) * half, half), cols]
            copies[2, n] = send(2, n, away, half_in.at[f, :, cols], 2)
        elif stage == 2:
            owned[f, rows(mine_half, half), cols] = plus(
                owned[f, rows(mine_half, half), cols], half_in[f, :, cols]
            ).astype(BF)
            away = owned.at[f, rows(mine_half + (1 - z) * fourth, fourth), cols]
            copies[3, n] = send(3, n, away, quarter_in.at[f, :, cols], 3)
        elif stage == 3:
            quarter[f, :, cols] = plus(owned[f, rows(mine_fourth, fourth), cols], quarter_in[f, :, cols]).astype(BF)
            copies[4, n] = send(4, n, quarter.at[f, :, cols], far_in.at[f, :, cols], 4)
        elif stage == 4:
            out_ref[f, rows(mine_fourth, fourth), cols] = plus(quarter[f, :, cols], far_in[f, :, cols]).astype(BF)
            done = out_ref.at[f, rows(mine_fourth, fourth), cols]
            copies[5, n] = send(5, n, done, done, 3)
        elif stage == 5:
            done = out_ref.at[f, rows(mine_half, half), cols]
            copies[6, n] = send(6, n, done, done, 2)

    for wave in range(len(chunks) + 5 * REDUCE_LAG):
        for stage in range(6, 0, -1):
            n = wave - REDUCE_LAG * (stage - 1)
            if 0 <= n < len(chunks):
                step(stage, n)
        if wave < 5:
            flying = small_step(wave)
    for copy in started:
        copy.wait_send()


def reduce_call(terms, packed):
    flows = len(terms)
    height, width = terms[0][0].shape
    chunks = flows * (width // REDUCE_COLS)
    vmem = pl.BlockSpec(memory_space=pltpu.VMEM)
    total = flows * height * width
    return pl.pallas_call(
        functools.partial(reduce_kernel, flows),
        in_specs=[vmem] * (3 * flows + 1),
        out_specs=[vmem, vmem],
        out_shape=[shaped(flows, height, width), jax.ShapeDtypeStruct(packed.shape, F32)],
        scratch_shapes=[
            pltpu.VMEM((flows, 2 * height, width), BF),
            pltpu.VMEM((flows, height, width), BF),
            pltpu.VMEM((flows, height, width), BF),
            pltpu.VMEM((flows, height, width), BF),
            pltpu.VMEM((flows, height // 2, width), BF),
            pltpu.VMEM((flows, height // 4, width), BF),
            pltpu.VMEM((flows, height // 4, width), BF),
            pltpu.VMEM((flows, height // 4, width), BF),
            pltpu.VMEM((5,) + packed.shape, F32),
            pltpu.VMEM((4,) + packed.shape, F32),
            pltpu.SemaphoreType.DMA((7, chunks)),
            pltpu.SemaphoreType.DMA((7, chunks)),
            pltpu.SemaphoreType.DMA((5,)),
            pltpu.SemaphoreType.DMA((5,)),
        ],
        compiler_params=pltpu.CompilerParams(
            collective_id=0, has_side_effects=True, vmem_limit_bytes=40 * 2**20
        ),
        cost_estimate=cost(total, 20 * total),
        name="reduce_grads",
    )(*[t for three in terms for t in three], packed)


def swap(array, axis, bit):
    size = lax.axis_size(axis)
    return lax.ppermute(array, axis, [(i, i ^ bit) for i in range(size)])


def gather_hops(shards):
    side = lax.axis_index("rep") & 1
    halves = [s.shape[0] // 2 for s in shards]
    mine = [lax.dynamic_slice_in_dim(s, side * h, h, axis=0) for s, h in zip(shards, halves)]
    direct, core = yield [swap(m, "shard", 2) for m in mine], [swap(s, "shard", 1) for s in shards]
    relayed, cross = yield [swap(d, "rep", 1) for d in direct], [swap(d, "shard", 1) for d in direct]
    cross_relayed = yield [swap(r, "shard", 1) for r in relayed]
    return [list(p) for p in zip(shards, core, direct, relayed, cross, cross_relayed)]


def piece_starts(shard):
    height = shard.shape[0]
    me = lax.axis_index("shard")
    side = lax.axis_index("rep") & 1
    half = height // 2
    near, core, far, cross = [(me ^ o) * height for o in range(4)]
    return [near, core, far + side * half, far + (1 - side) * half, cross + side * half, cross + (1 - side) * half]


def added(*terms):
    return functools.reduce(jnp.add, [t.astype(F32) for t in terms]).astype(BF)


class Flow:
    def __init__(self, hops):
        self.hops = hops
        self.result = None
        self.flying = next(hops)

    def land(self, arrived):
        try:
            self.flying = self.hops.send(arrived)
        except StopIteration as stop:
            self.flying, self.result = None, stop.value


class Line:
    def __init__(self):
        self.flows = []
        self.recent = []

    def step(self, arrays, flows=None):
        moving = [f for f in (self.flows if flows is None else flows) if f.flying is not None]
        held = self.recent
        arrays, arrived, held = lax.optimization_barrier((arrays, [f.flying for f in moving], held))
        for flow, value in zip(moving, arrived):
            flow.land(value)
        self.recent = []
        return arrays

    def start(self, hops):
        flow = Flow(hops)
        self.flows.append(flow)
        return flow


def group_sum(grad):
    return lax.psum_scatter(grad, "shard", scatter_dimension=0, tiled=True)


def replica_sum(owned):
    return lax.psum(owned, "rep").astype(F32)


def local(
    tokens,
    segment_ids,
    cotangent,
    w_qkv,
    b_query,
    b_value,
    w_out,
    b_out,
    gain_one,
    shift_one,
    w_in,
    b_in,
    w_ffo,
    b_ffo,
    gain_two,
    shift_two,
):
    micro, sequences, length, width = tokens.shape
    total = micro * sequences
    rows = total * length
    group = lax.axis_size("shard")
    hidden_width = w_in.shape[1]
    x = tokens.reshape(rows, width)
    seg = segment_ids.reshape(total, length)
    cot = cotangent.reshape(rows, width)
    me = lax.axis_index("shard")
    direct = group == 4 and lax.axis_size("rep") == 8

    part = b_query.shape[0]
    line = Line()
    small_shards = (b_query, b_value, b_out, gain_one, shift_one, b_ffo, gain_two, shift_two, b_in)
    small = jnp.concatenate(small_shards).reshape(1, -1)
    if direct:
        qkv_flow = Flow(gather_hops([w_qkv]))
        near = swap(small, "shard", 1)
        pair = jnp.concatenate([small, near], axis=0)
        four = jnp.concatenate([pair, swap(pair, "shard", 2)], axis=0)
        order = [jnp.bitwise_xor(me, o) for o in range(4)]
        small_full = jnp.concatenate([lax.dynamic_slice_in_dim(four, o, 1, axis=0) for o in order], axis=0)
        (later,) = line.step([w_ffo], [qkv_flow])
        later_flow = Flow(gather_hops([later]))
        seg = line.step(seg, [qkv_flow])
        x_first = line.step(x, [qkv_flow])
        (qkv_pieces,) = qkv_flow.result
        qkv_starts = jnp.stack(piece_starts(w_qkv)).astype(jnp.int32)
        layer_lists = [[lax.all_gather(w, "shard", axis=0, tiled=True)] for w in (w_out, w_in)]
        layer_starts = jnp.stack([jnp.int32(0)] * 2 + piece_starts(w_ffo)).astype(jnp.int32)
        counts = (1, 1, 6)
    else:
        small_full = lax.all_gather(small, "shard", axis=0, tiled=True)
        qkv_pieces, *layer_lists = [
            [lax.all_gather(w, "shard", axis=0, tiled=True)] for w in (w_qkv, w_out, w_in, w_ffo)
        ]
        x_first = x
        qkv_starts = jnp.zeros((1,), jnp.int32)
        layer_starts = jnp.zeros((3,), jnp.int32)
        counts = (1, 1, 1)
    small_full = small_full.astype(F32)
    vectors = [small_full[:, i * part : (i + 1) * part].reshape(1, -1) for i in range(8)]
    bias_all = jnp.concatenate([vectors[0], jnp.zeros_like(vectors[0]), vectors[1]], axis=1)
    vec = jnp.concatenate(vectors[2:] + [jnp.zeros((2, width), F32)], axis=0)
    bias_in = small_full[:, 8 * part :].reshape(1, -1)

    windows = windows_of(seg)
    block = 256
    (projected,) = row_call(
        functools.partial(project_kernel, len(qkv_pieces)),
        "project",
        rows,
        block,
        qkv_starts,
        [x_first],
        [bias_all],
        qkv_pieces,
        [shaped(rows, 3 * width)],
        [],
        [pltpu.VMEM((width, 3 * width), BF)],
        6 * rows * width * width,
    )
    if direct:
        projected = line.step(projected, [later_flow])
    attended, lse = attend_forward(projected, windows, total)
    if direct:
        attended = line.step(attended, [later_flow])
        attended = line.step(attended, [later_flow])
        layer_lists = layer_lists + later_flow.result
    layer_pieces = sum(layer_lists, [])
    weights_scratch = [
        pltpu.VMEM((width, width), BF),
        pltpu.VMEM((width, hidden_width), BF),
        pltpu.VMEM((hidden_width, width), BF),
    ]
    layer_flops = 2 * rows * width * (width + 2 * hidden_width)
    output, normed, n_one, rstd_one, d_second, hidden, slope, sums_two = row_call(
        functools.partial(layer_forward_kernel, counts),
        "layer_forward",
        rows,
        block,
        layer_starts,
        [x, attended, cot],
        [vec, bias_in],
        layer_pieces,
        [
            shaped(rows, width),
            shaped(rows, width),
            shaped(rows, width),
            shaped(rows, 128, dtype=F32),
            shaped(rows, width),
            shaped(rows, hidden_width),
            shaped(rows, hidden_width),
        ],
        [shaped(24, width, dtype=F32)],
        weights_scratch,
        layer_flops,
    )

    place = [jnp.bitwise_xor(me, o) for o in range(4)]
    slots = jnp.stack(
        [(p & 1) * 2 + lax.shift_right_logical(p, 1) for p in place] + [jnp.bitwise_xor(me, j) for j in (1, 3, 2, 0)]
    ).astype(jnp.int32)

    grad_ffo = plain_grad(hidden, d_second, "grad_ffo")
    owned_ffo = group_sum(grad_ffo)
    d_pre, d_branch, d_attended, sums_one, sums_in = row_call(
        functools.partial(layer_backward_kernel, counts),
        "layer_backward",
        rows,
        block,
        layer_starts,
        [d_second, slope, n_one, rstd_one],
        [vec],
        layer_pieces,
        [shaped(rows, hidden_width), shaped(rows, width), shaped(rows, width)],
        [shaped(24, width, dtype=F32), shaped(8, hidden_width, dtype=F32)],
        weights_scratch,
        layer_flops,
    )
    grad_in = plain_grad(normed, d_pre, "grad_in")
    grad_out = plain_grad(attended, d_branch, "grad_out")
    d_attended, grad_in, grad_out, owned_ffo = lax.optimization_barrier((d_attended, grad_in, grad_out, owned_ffo))
    grad_ffo = replica_sum(owned_ffo)
    owned_in, owned_out = group_sum(grad_in), group_sum(grad_out)
    groups = 3
    d_heads = attend_backward(projected, d_attended, attended, lse, windows, total, groups)
    if direct:
        *terms, head_sums = weight_grad(slots, x, d_heads, "grad_qkv")
    else:
        grads = replica_sum(group_sum(plain_grad(x, d_heads, "grad_qkv")))
        head_sums = fold_rows(d_heads.astype(F32))

    def folded(sums):
        return [jnp.sum(sums[i : i + 8], axis=0) for i in range(0, sums.shape[0], 8)]

    d_gain_two, d_shift_two, d_ffo_bias = folded(sums_two)
    d_gain_one, d_shift_one, d_out_bias = folded(sums_one)
    (d_in_bias,) = folded(sums_in)
    cut = width // groups
    head_sums = jnp.sum(head_sums, axis=0).reshape(groups, 3, cut)
    d_query_bias = head_sums[:, 0].reshape(-1)
    d_value_bias = head_sums[:, 2].reshape(-1)
    smalls = (
        d_query_bias, d_value_bias, d_out_bias, d_gain_one, d_shift_one, d_ffo_bias, d_gain_two, d_shift_two,
        d_in_bias,
    )
    packed = jnp.concatenate([s.reshape(group, -1) for s in smalls], axis=1)
    (d_tokens,) = row_call(
        functools.partial(input_grad_kernel, len(qkv_pieces), groups),
        "input_grad",
        rows,
        block,
        qkv_starts,
        [d_branch, d_heads],
        [],
        qkv_pieces,
        [shaped(rows, width)],
        [],
        [pltpu.VMEM((width, 3 * width), BF)],
        6 * rows * width * width,
    )
    packed, grad_ffo, owned_in, owned_out = lax.optimization_barrier((packed, grad_ffo, owned_in, owned_out))
    grad_in, grad_out = replica_sum(owned_in), replica_sum(owned_out)
    if direct:
        reduced, packed = reduce_call([terms], packed)
        grads = reduced[0].astype(F32)
    else:
        packed = lax.psum(packed, ("shard", "rep"))
    grad_qkv = grads.reshape(part, groups, 3, cut).transpose(0, 2, 1, 3).reshape(part, 3 * width)
    mine = lax.dynamic_index_in_dim(packed, me, 0, keepdims=False)
    sm = [mine[i * part : (i + 1) * part] for i in range(8)]
    gqb, gvb, gob, gg1, gs1, gfb, gg2, gs2 = sm
    gib = mine[8 * part :]
    return (
        output.reshape(tokens.shape),
        d_tokens.reshape(tokens.shape),
        grad_qkv,
        gqb,
        gvb,
        grad_out,
        gob,
        gg1,
        gs1,
        grad_in,
        gib,
        grad_ffo,
        gfb,
        gg2,
        gs2,
    )


def solution(mesh):
    data = P(None, ("shard", "rep"), None, None)
    matrix = P("shard", None)
    vector = P("shard")
    return jax.shard_map(
        local,
        mesh=mesh,
        in_specs=(
            data,
            P(None, ("shard", "rep"), None),
            data,
            matrix,
            vector,
            vector,
            matrix,
            vector,
            vector,
            vector,
            matrix,
            vector,
            matrix,
            vector,
            vector,
            vector,
        ),
        out_specs=(
            data,
            data,
            matrix,
            vector,
            vector,
            matrix,
            vector,
            vector,
            vector,
            matrix,
            vector,
            matrix,
            vector,
            vector,
            vector,
        ),
        check_vma=False,
    )
```

```python
import functools
import math

import jax
import jax.numpy as jnp
from jax import lax
from jax.experimental import pallas as pl
from jax.experimental.pallas import tpu as pltpu
from jax.sharding import PartitionSpec as P

HEADS = 12
HEAD_DIM = 64
PAIR = 2 * HEAD_DIM
TILE = 128

epsilon = 1e-05
masked_score = -1e30
BF = jnp.bfloat16
F32 = jnp.float32
VMEM_LIMIT = 60 * 2**20


def dot_nn(a, b):
    return lax.dot_general(a, b, (((1,), (0,)), ((), ())), preferred_element_type=F32)


def dot_nt(a, b):
    return lax.dot_general(a, b, (((1,), (1,)), ((), ())), preferred_element_type=F32)


def dot_tn(a, b):
    return lax.dot_general(a, b, (((0,), (0,)), ((), ())), preferred_element_type=F32)


def head_rows(value):
    lane = lax.broadcasted_iota(jnp.int32, (1, PAIR), 1)
    first = jnp.where(lane < HEAD_DIM, value, 0.0).astype(BF)
    second = jnp.where(lane < HEAD_DIM, 0.0, value).astype(BF)
    return first, second


def stack_heads(block, rows):
    return jnp.concatenate([block * rows[0], block * rows[1]], axis=0)


def diagonal_back(transposed):
    kept = jnp.concatenate(
        [transposed[:HEAD_DIM, :TILE], transposed[HEAD_DIM:, TILE:]], axis=0
    )
    return kept.T


def for_windows(count, tiles, body):
    sizes = [t for t in range(1, tiles + 1) if t < 7 or t == tiles]
    below = 0
    for size in sizes:
        @pl.when((count > below) & (count <= size))
        def _(size=size):
            body(size)

        below = size


def attend_forward_kernel(pairs, tiles, low_ref, count_ref, q_ref, k_ref, v_ref, kseg_ref, qseg_ref, o_ref, lse_ref):
    place = pl.program_id(0) * tiles + pl.program_id(1)
    low = low_ref[place]
    count = count_ref[place]
    rows_of = head_rows(1.0 / math.sqrt(HEAD_DIM))

    def window(size):
        start = jnp.minimum(low, tiles - size) * TILE
        chunks = [pl.ds(pl.multiple_of(start + c * TILE, TILE), TILE) for c in range(size)]
        whole = pl.ds(pl.multiple_of(start, TILE), size * TILE)
        masks = [kseg_ref[c, :] == qseg_ref[0] for c in chunks]
        def first(p):
            lanes = slice(p * PAIR, (p + 1) * PAIR)
            queries = stack_heads(q_ref[:, lanes], rows_of)
            scores = []
            for c, mask in zip(chunks, masks):
                part = dot_nt(k_ref[c, lanes], queries)
                scores.append(
                    jnp.concatenate(
                        [
                            jnp.where(mask, part[:, :TILE], masked_score),
                            jnp.where(mask, part[:, TILE:], masked_score),
                        ],
                        axis=1,
                    )
                )
            return scores

        def second(p, scores):
            lanes = slice(p * PAIR, (p + 1) * PAIR)
            top = functools.reduce(jnp.maximum, [jnp.max(s, axis=0, keepdims=True) for s in scores])
            exps = [jnp.exp(s - top) for s in scores]
            total = functools.reduce(jnp.add, [jnp.sum(e, axis=0, keepdims=True) for e in exps])
            weights = jnp.concatenate([e.astype(BF) for e in exps], axis=0)
            mixed = dot_tn(v_ref[whole, lanes], weights) / total
            o_ref[:, lanes] = diagonal_back(mixed).astype(BF)
            lse_ref[0, p : p + 1, :] = top + jnp.log(total)

        ready = first(0)
        for p in range(pairs):
            after = first(p + 1) if p + 1 < pairs else None
            second(p, ready)
            ready = after

    for_windows(count, tiles, window)


def attend_backward_kernel(
    pairs, tiles, low_ref, count_ref, q_ref, k_ref, v_ref, do_ref, o_ref, lse_ref, kseg_ref, qseg_ref,
    out_ref, dk_acc, dv_acc,
):
    block = pl.program_id(2)
    first_pair = pl.program_id(1) * pairs
    place = pl.program_id(0) * tiles + block
    low = low_ref[place]
    count = count_ref[place]
    part = pairs * PAIR
    scale = 1.0 / math.sqrt(HEAD_DIM)
    scaled_rows = head_rows(scale)
    plain_rows = head_rows(1.0)

    @pl.when(block == 0)
    def _():
        dk_acc[...] = jnp.zeros_like(dk_acc)
        dv_acc[...] = jnp.zeros_like(dv_acc)

    def window(size):
        start = jnp.minimum(low, tiles - size) * TILE
        chunks = [pl.ds(pl.multiple_of(start + c * TILE, TILE), TILE) for c in range(size)]
        whole = pl.ds(pl.multiple_of(start, TILE), size * TILE)
        masks = [kseg_ref[c, :] == qseg_ref[0] for c in chunks]
        mine = pl.ds(pl.multiple_of(block * TILE, TILE), TILE)
        for p in range(pairs):
            lanes = slice(p * PAIR, (p + 1) * PAIR)
            queries = stack_heads(q_ref[:, lanes], scaled_rows)
            grads = do_ref[:, lanes]
            stacked = stack_heads(grads, plain_rows)
            product = (grads.astype(F32) * o_ref[:, lanes].astype(F32)).T
            row_dot = jnp.concatenate(
                [
                    jnp.sum(product[:HEAD_DIM], axis=0, keepdims=True),
                    jnp.sum(product[HEAD_DIM:], axis=0, keepdims=True),
                ],
                axis=1,
            )
            lse = lse_ref[0, pl.ds(first_pair + p, 1), :]
            kept = []
            weights = []
            all_scores = dot_nt(k_ref[whole, lanes], queries)
            all_d_probs = dot_nt(v_ref[whole, lanes], stacked)
            for n, mask in enumerate(masks):
                rows_n = slice(n * TILE, (n + 1) * TILE)
                part_scores = all_scores[rows_n] - lse
                d_probs = all_d_probs[rows_n]
                probs = jnp.exp(
                    jnp.concatenate(
                        [
                            jnp.where(mask, part_scores[:, :TILE], masked_score),
                            jnp.where(mask, part_scores[:, TILE:], masked_score),
                        ],
                        axis=1,
                    )
                )
                kept.append((probs * (d_probs - row_dot)).astype(BF))
                weights.append(probs.astype(BF))
            kept = jnp.concatenate(kept, axis=0)
            weights = jnp.concatenate(weights, axis=0)
            dv_acc[whole, lanes] += dot_nn(weights, stacked)
            dk_acc[whole, lanes] += dot_nn(kept, queries)
            mixed = dot_tn(k_ref[whole, lanes], kept) * scale
            out_ref[mine, lanes] = diagonal_back(mixed).astype(BF)

    for_windows(count, tiles, window)

    @pl.when(block == tiles - 1)
    def _():
        out_ref[:, part : 2 * part] = dk_acc[...].astype(BF)
        out_ref[:, 2 * part :] = dv_acc[...].astype(BF)


def windows_of(segments):
    sequences, length = segments.shape
    tiles = length // TILE
    blocked = segments.reshape(sequences, tiles, TILE)
    first = blocked[:, :, 0]
    last = blocked[:, :, TILE - 1]
    starts = jnp.sum((segments[:, None, :] < first[:, :, None]).astype(jnp.int32), axis=-1)
    ends = jnp.sum((segments[:, None, :] <= last[:, :, None]).astype(jnp.int32), axis=-1)
    bits = TILE.bit_length() - 1
    low = lax.shift_right_logical(starts, bits)
    count = lax.shift_right_logical(ends + TILE - 1, bits) - low
    key_ids = jnp.broadcast_to(segments.reshape(sequences * length, 1), (sequences * length, TILE))
    query_ids = blocked.reshape(sequences * tiles, 1, TILE)
    return low.reshape(-1), count.reshape(-1), key_ids, query_ids


def attend_forward(projected, windows, sequences):
    low, count, key_ids, query_ids = windows
    rows = projected.shape[0]
    width = projected.shape[1] // 3
    length = rows // sequences
    tiles = length // TILE
    pairs = width // PAIR
    return pl.pallas_call(
        functools.partial(attend_forward_kernel, pairs, tiles),
        grid_spec=pltpu.PrefetchScalarGridSpec(
            num_scalar_prefetch=2,
            grid=(sequences, tiles),
            in_specs=[
                pl.BlockSpec((TILE, width), lambda s, b, *_: (s * tiles + b, 0)),
                pl.BlockSpec((length, width), lambda s, b, *_: (s, 1)),
                pl.BlockSpec((length, width), lambda s, b, *_: (s, 2)),
                pl.BlockSpec((length, TILE), lambda s, b, *_: (s, 0)),
                pl.BlockSpec((1, 1, TILE), lambda s, b, *_: (s * tiles + b, 0, 0)),
            ],
            out_specs=[
                pl.BlockSpec((TILE, width), lambda s, b, *_: (s * tiles + b, 0)),
                pl.BlockSpec((1, 8, 2 * TILE), lambda s, b, *_: (s * tiles + b, 0, 0)),
            ],
        ),
        out_shape=[
            jax.ShapeDtypeStruct((rows, width), BF),
            jax.ShapeDtypeStruct((sequences * tiles, 8, 2 * TILE), F32),
        ],
        compiler_params=pltpu.CompilerParams(vmem_limit_bytes=VMEM_LIMIT),
        cost_estimate=cost(8 * 10**9, 16 * 10**6),
        name="attend_forward",
    )(low, count, projected, projected, projected, key_ids, query_ids)


def attend_backward(projected, d_attended, attended, lse, windows, sequences, groups):
    low, count, key_ids, query_ids = windows
    rows = projected.shape[0]
    width = projected.shape[1] // 3
    length = rows // sequences
    tiles = length // TILE
    part = width // groups
    pairs = part // PAIR
    query_spec = pl.BlockSpec((TILE, part), lambda s, g, b, *_: (s * tiles + b, g))
    return pl.pallas_call(
        functools.partial(attend_backward_kernel, pairs, tiles),
        grid_spec=pltpu.PrefetchScalarGridSpec(
            num_scalar_prefetch=2,
            grid=(sequences, groups, tiles),
            in_specs=[
                query_spec,
                pl.BlockSpec((length, part), lambda s, g, b, *_: (s, groups + g)),
                pl.BlockSpec((length, part), lambda s, g, b, *_: (s, 2 * groups + g)),
                query_spec,
                query_spec,
                pl.BlockSpec((1, 8, 2 * TILE), lambda s, g, b, *_: (s * tiles + b, 0, 0)),
                pl.BlockSpec((length, TILE), lambda s, g, b, *_: (s, 0)),
                pl.BlockSpec((1, 1, TILE), lambda s, g, b, *_: (s * tiles + b, 0, 0)),
            ],
            out_specs=pl.BlockSpec((length, 3 * part), lambda s, g, b, *_: (s, g)),
            scratch_shapes=[pltpu.VMEM((length, part), F32), pltpu.VMEM((length, part), F32)],
        ),
        out_shape=jax.ShapeDtypeStruct((rows, 3 * width), BF),
        compiler_params=pltpu.CompilerParams(vmem_limit_bytes=VMEM_LIMIT),
        cost_estimate=cost(30 * 10**9, 30 * 10**6),
        name="attend_backward",
    )(low, count, projected, projected, projected, d_attended, attended, lse, key_ids, query_ids)


def row_mean(values):
    return jnp.mean(values, axis=-1, keepdims=True)


def fold_rows(values):
    rows, width = values.shape
    return jnp.sum(values.reshape(rows // 8, 8, width), axis=0)


def load_pieces(starts_ref, pieces, targets, sems):
    copies = []
    for n, (piece, target) in enumerate(zip(pieces, targets)):
        height = piece.shape[0]
        start = pl.multiple_of(starts_ref[n], math.gcd(height, 128))
        copies.append(pltpu.make_async_copy(piece, target.at[pl.ds(start, height)], sems.at[n]))
    for copy in copies:
        copy.start()
    for copy in copies:
        copy.wait()


def gelu_parts(values):
    bell = jnp.exp(values * values * -0.5)
    t = 1.0 / (1.0 + jnp.abs(values) * (0.3275911 / math.sqrt(2.0)))
    poly = t * (
        0.5 * 0.254829592
        + t * (0.5 * -0.284496736 + t * (0.5 * 1.421413741 + t * (0.5 * -1.453152027 + t * (0.5 * 1.061405429))))
    )
    tail = poly * bell
    phi = jnp.where(values >= 0.0, 1.0 - tail, tail)
    return values * phi, phi + values * bell * (1.0 / math.sqrt(2.0 * math.pi))


def project_kernel(count, starts_ref, x_ref, bias_ref, *refs):
    pieces = refs[:count]
    o_ref, weight, sems = refs[count:]

    @pl.when(pl.program_id(0) == 0)
    def _():
        load_pieces(starts_ref, pieces, [weight] * count, sems)

    o_ref[...] = (dot_nn(x_ref[...], weight[...]) + bias_ref[...]).astype(BF)


FFN_CHUNK = 512


def layer_forward_kernel(
    counts, starts_ref, x_ref, att_ref, cot_ref, vec_ref, bin_ref, *refs
):
    total = sum(counts)
    pieces = refs[:total]
    (
        out_ref, normed_ref, none_ref, rstd_ref, dsec_ref, hidden_ref, slope_ref, sums_ref,
        w_out, w_in, w_ffo, sems,
    ) = refs[total:]
    targets = [w_out] * counts[0] + [w_in] * counts[1] + [w_ffo] * counts[2]

    @pl.when(pl.program_id(0) == 0)
    def _():
        load_pieces(starts_ref, pieces, targets, sems)
        sums_ref[...] = jnp.zeros_like(sums_ref)

    b_out, gain_one, shift_one, b_ffo, gain_two, shift_two = [vec_ref[i : i + 1, :] for i in range(6)]
    res = x_ref[...].astype(F32) + (dot_nn(att_ref[...], w_out[...]) + b_out)
    center = res - row_mean(res)
    rstd = lax.rsqrt(row_mean(center * center) + epsilon)
    n_one = center * rstd
    normed = (n_one * gain_one + shift_one).astype(BF)
    normed_ref[...] = normed
    none_ref[...] = n_one.astype(BF)
    rstd_ref[...] = jnp.broadcast_to(rstd, rstd_ref.shape)
    hidden_width = w_in.shape[1]
    second = None
    pres = []
    for c in range(0, hidden_width, FFN_CHUNK):
        cols = slice(c, c + FFN_CHUNK)
        pre = dot_nn(normed, w_in[:, cols]) + bin_ref[:, cols]
        value, slope = gelu_parts(pre)
        value = value.astype(BF)
        hidden_ref[:, cols] = value
        slope_ref[:, cols] = slope.astype(BF)
        term = dot_nn(value, w_ffo[cols, :])
        second = term if second is None else second + term
    res = normed.astype(F32) + (second + b_ffo)
    center = res - row_mean(res)
    rstd = lax.rsqrt(row_mean(center * center) + epsilon)
    n_two = center * rstd
    out_ref[...] = (n_two * gain_two + shift_two).astype(BF)
    cot = cot_ref[...].astype(F32)
    inner = cot * gain_two
    d_second = (rstd * (inner - row_mean(inner) - n_two * row_mean(inner * n_two))).astype(BF)
    dsec_ref[...] = d_second
    sums_ref[0:8, :] += fold_rows(cot * n_two)
    sums_ref[8:16, :] += fold_rows(cot)
    sums_ref[16:24, :] += fold_rows(d_second.astype(F32))


def layer_backward_kernel(counts, starts_ref, dsec_ref, slope_ref, none_ref, rstd_ref, vec_ref, *refs):
    total = sum(counts)
    pieces = refs[:total]
    dpre_ref, dbranch_ref, datt_ref, sums_ref, bin_ref, w_out, w_in, w_ffo, sems = refs[total:]
    targets = [w_out] * counts[0] + [w_in] * counts[1] + [w_ffo] * counts[2]

    @pl.when(pl.program_id(0) == 0)
    def _():
        load_pieces(starts_ref, pieces, targets, sems)
        sums_ref[...] = jnp.zeros_like(sums_ref)
        bin_ref[...] = jnp.zeros_like(bin_ref)

    gain_one = vec_ref[1:2, :]
    d_second = dsec_ref[...]
    d_norm = d_second.astype(F32)
    for c in range(0, w_in.shape[1], FFN_CHUNK):
        cols = slice(c, c + FFN_CHUNK)
        d_pre = (dot_nt(d_second, w_ffo[cols, :]) * slope_ref[:, cols].astype(F32)).astype(BF)
        dpre_ref[:, cols] = d_pre
        bin_ref[:, cols] += fold_rows(d_pre.astype(F32))
        d_norm = d_norm + dot_nt(d_pre, w_in[:, cols])
    n_one = none_ref[...].astype(F32)
    inner = d_norm * gain_one
    d_res = rstd_ref[:, 0:1] * (inner - row_mean(inner) - n_one * row_mean(inner * n_one))
    d_branch = d_res.astype(BF)
    dbranch_ref[...] = d_branch
    datt_ref[...] = dot_nt(d_branch, w_out[...]).astype(BF)
    sums_ref[0:8, :] += fold_rows(d_norm * n_one)
    sums_ref[8:16, :] += fold_rows(d_norm)
    sums_ref[16:24, :] += fold_rows(d_branch.astype(F32))


def input_grad_kernel(count, groups, starts_ref, dbranch_ref, *refs):
    grads = refs[0]
    pieces = refs[1 : 1 + count]
    o_ref, weight, sems = refs[1 + count :]

    @pl.when(pl.program_id(0) == 0)
    def _():
        load_pieces(starts_ref, pieces, [weight] * count, sems)

    width = dbranch_ref.shape[1]
    part = width // groups
    total = dbranch_ref[...].astype(F32)
    for g in range(groups):
        for n in range(3):
            here = (3 * g + n) * part
            first = n * width + g * part
            total = total + dot_nt(grads[:, here : here + part], weight[:, first : first + part])
    o_ref[...] = total.astype(BF)


def weight_grad_cols_kernel(slots, owner_ref, a_ref, b_ref, keep_ref, pass_ref, send_ref, sums_ref, held):
    terms = b_ref[...]
    sums_ref[...] = fold_rows(terms.astype(F32))
    part = dot_tn(a_ref[...], terms).astype(BF)
    height = keep_ref.shape[0]
    for owner in range(4):
        held[owner_ref[owner]] = part[owner * height : (owner + 1) * height]
    keep_ref[...] = held[0]
    pass_ref[...] = held[1]
    send_ref[0:height, :] = held[2]
    send_ref[height:, :] = held[3]


PARAMS = pltpu.CompilerParams(vmem_limit_bytes=VMEM_LIMIT)


def cost(flops, bytes_accessed):
    return pl.CostEstimate(flops=int(flops) // 16, bytes_accessed=int(bytes_accessed) // 16, transcendentals=0)


def whole_spec(array):
    zeros = (0,) * array.ndim
    return pl.BlockSpec(array.shape, lambda *_: zeros)


ANY = pl.BlockSpec(memory_space=pl.ANY)


def row_call(kernel, name, rows, block, scalars, blocked, fixed, pieces, outs, accs, scratch, flops):
    in_specs = (
        [pl.BlockSpec((block, a.shape[1]), lambda i, *_: (i, 0)) for a in blocked]
        + [whole_spec(a) for a in fixed]
        + [ANY] * len(pieces)
    )
    out_specs = [pl.BlockSpec((block, s.shape[1]), lambda i, *_: (i, 0)) for s in outs] + [
        whole_spec(s) for s in accs
    ]
    moved = sum(a.size * a.dtype.itemsize for a in list(blocked) + list(pieces) + list(outs))
    return pl.pallas_call(
        kernel,
        grid_spec=pltpu.PrefetchScalarGridSpec(
            num_scalar_prefetch=1,
            grid=(rows // block,),
            in_specs=in_specs,
            out_specs=out_specs,
            scratch_shapes=list(scratch) + [pltpu.SemaphoreType.DMA((len(pieces),))],
        ),
        out_shape=list(outs) + list(accs),
        compiler_params=PARAMS,
        cost_estimate=cost(flops, moved),
        name=name,
    )(scalars, *blocked, *fixed, *pieces)


def shaped(*shape, dtype=BF):
    return jax.ShapeDtypeStruct(shape, dtype)


def weight_grad(slots, a, b, name):
    rows, height = a.shape
    width = b.shape[1]
    part = height // 4
    flops = 2 * rows * height * width
    moved = 2 * (rows * height + rows * width + height * width)
    block = 768
    return pl.pallas_call(
        functools.partial(weight_grad_cols_kernel, 4),
        grid_spec=pltpu.PrefetchScalarGridSpec(
            num_scalar_prefetch=1,
            grid=(width // block,),
            in_specs=[
                pl.BlockSpec((rows, height), lambda t, s: (0, 0)),
                pl.BlockSpec((rows, block), lambda t, s: (0, t)),
            ],
            out_specs=[
                pl.BlockSpec((part, block), lambda t, s: (0, t)),
                pl.BlockSpec((part, block), lambda t, s: (0, t)),
                pl.BlockSpec((2 * part, block), lambda t, s: (0, t)),
                pl.BlockSpec((8, block), lambda t, s: (0, t)),
            ],
            scratch_shapes=[pltpu.VMEM((4, part, block), BF)],
        ),
        out_shape=[
            shaped(part, width),
            shaped(part, width),
            shaped(2 * part, width),
            shaped(8, width, dtype=F32),
        ],
        compiler_params=PARAMS,
        cost_estimate=cost(flops, moved),
        name=name,
    )(slots, a, b)


def plain_grad_kernel(a_ref, b_ref, o_ref):
    o_ref[...] = dot_tn(a_ref[...], b_ref[...]).astype(BF)


def plain_grad(a, b, name):
    rows, height = a.shape
    width = b.shape[1]
    block = 768
    tall = height > width
    steps = (height if tall else width) // block
    specs = [
        pl.BlockSpec((rows, block if tall else height), (lambda t: (0, t)) if tall else (lambda t: (0, 0))),
        pl.BlockSpec((rows, width if tall else block), (lambda t: (0, 0)) if tall else (lambda t: (0, t))),
    ]
    out = (
        pl.BlockSpec((block, width), lambda t: (t, 0)) if tall else pl.BlockSpec((height, block), lambda t: (0, t))
    )
    return pl.pallas_call(
        plain_grad_kernel,
        grid=(steps,),
        in_specs=specs,
        out_specs=out,
        out_shape=shaped(height, width),
        compiler_params=PARAMS,
        cost_estimate=cost(2 * rows * height * width, 2 * (rows * (height + width) + height * width)),
        name=name,
    )(a, b)


REDUCE_COLS = 768
REDUCE_LAG = 1


def reduce_kernel(flows, *refs):
    parts = [refs[3 * f : 3 * f + 3] for f in range(flows)]
    small_ref = refs[3 * flows]
    out_ref, total_ref = refs[3 * flows + 1 : 3 * flows + 3]
    come, onward, across, owned, half_in, quarter_in, quarter, far_in, small_in, small_sum = refs[
        3 * flows + 3 : 3 * flows + 13
    ]
    sent, got, small_sent, small_got = refs[3 * flows + 13 :]
    me = lax.axis_index("shard")
    place = lax.axis_index("rep")
    y = lax.rem(place, 2)
    z = lax.rem(lax.div(place, 2), 2)
    peers = [
        {"shard": me + 1 - 2 * lax.rem(me, 2)},
        {"shard": lax.rem(me + 2, 4)},
        {"rep": place + 1 - 2 * y},
        {"rep": place + 2 - 4 * z},
        {"rep": lax.rem(place + 4, 8)},
    ]
    barrier = pltpu.get_barrier_semaphore()
    for peer in peers:
        pl.semaphore_signal(barrier, inc=1, device_id=peer, device_id_type=pl.DeviceIdType.MESH)
    pl.semaphore_wait(barrier, len(peers))

    height = owned.shape[1]
    half, fourth = height // 2, height // 4
    width = owned.shape[2]
    chunks = [(f, c) for f in range(flows) for c in range(0, width, REDUCE_COLS)]
    started = []

    def rows(start, size):
        return pl.ds(pl.multiple_of(start, 16), size)

    def send(hop, n, source, target, peer):
        copy = pltpu.make_async_remote_copy(
            src_ref=source,
            dst_ref=target,
            send_sem=sent.at[hop, n],
            recv_sem=got.at[hop, n],
            device_id=peers[peer],
            device_id_type=pl.DeviceIdType.MESH,
        )
        copy.start()
        started.append(copy)
        return copy

    def small_send(hop, source):
        copy = pltpu.make_async_remote_copy(
            src_ref=source,
            dst_ref=small_in.at[hop],
            send_sem=small_sent.at[hop],
            recv_sem=small_got.at[hop],
            device_id=peers[hop],
            device_id_type=pl.DeviceIdType.MESH,
        )
        copy.start()
        started.append(copy)
        return copy

    def plus(*terms):
        return functools.reduce(jnp.add, [t.astype(F32) for t in terms])

    mine_half = y * half
    mine_fourth = y * half + z * fourth
    copies = {}
    for n, (f, c) in enumerate(chunks):
        cols = pl.ds(c, REDUCE_COLS)
        copies[0, n] = send(0, n, parts[f][2].at[:, cols], come.at[f, :, cols], 0)
    flying = small_send(0, small_ref)
    for n, (f, c) in enumerate(chunks):
        cols = pl.ds(c, REDUCE_COLS)
        copies[0, n].wait_recv()
        onward[f, :, cols] = plus(parts[f][1][:, cols], come[f, pl.ds(height, height), cols]).astype(BF)
        copies[1, n] = send(1, n, onward.at[f, :, cols], across.at[f, :, cols], 1)

    def small_step(hop):
        flying.wait_recv()
        total = plus(small_ref[...] if hop == 0 else small_sum[hop - 1], small_in[hop])
        if hop == 4:
            total_ref[...] = total
            return None
        small_sum[hop] = total
        return small_send(hop + 1, small_sum.at[hop])

    def step(stage, n):
        f, c = chunks[n]
        cols = pl.ds(c, REDUCE_COLS)
        copies[stage, n].wait_recv()
        if stage == 1:
            owned[f, :, cols] = plus(
                parts[f][0][:, cols], come[f, pl.ds(0, height), cols], across[f, :, cols]
            ).astype(BF)
            away = owned.at[f, rows((1 - y) * half, half), cols]
            copies[2, n] = send(2, n, away, half_in.at[f, :, cols], 2)
        elif stage == 2:
            owned[f, rows(mine_half, half), cols] = plus(
                owned[f, rows(mine_half, half), cols], half_in[f, :, cols]
            ).astype(BF)
            away = owned.at[f, rows(mine_half + (1 - z) * fourth, fourth), cols]
            copies[3, n] = send(3, n, away, quarter_in.at[f, :, cols], 3)
        elif stage == 3:
            quarter[f, :, cols] = plus(owned[f, rows(mine_fourth, fourth), cols], quarter_in[f, :, cols]).astype(BF)
            copies[4, n] = send(4, n, quarter.at[f, :, cols], far_in.at[f, :, cols], 4)
        elif stage == 4:
            out_ref[f, rows(mine_fourth, fourth), cols] = plus(quarter[f, :, cols], far_in[f, :, cols]).astype(BF)
            done = out_ref.at[f, rows(mine_fourth, fourth), cols]
            copies[5, n] = send(5, n, done, done, 3)
        elif stage == 5:
            done = out_ref.at[f, rows(mine_half, half), cols]
            copies[6, n] = send(6, n, done, done, 2)

    for wave in range(len(chunks) + 5 * REDUCE_LAG):
        for stage in range(6, 0, -1):
            n = wave - REDUCE_LAG * (stage - 1)
            if 0 <= n < len(chunks):
                step(stage, n)
        if wave < 5:
            flying = small_step(wave)
    for copy in started:
        copy.wait_send()


def reduce_call(terms, packed):
    flows = len(terms)
    height, width = terms[0][0].shape
    chunks = flows * (width // REDUCE_COLS)
    vmem = pl.BlockSpec(memory_space=pltpu.VMEM)
    total = flows * height * width
    return pl.pallas_call(
        functools.partial(reduce_kernel, flows),
        in_specs=[vmem] * (3 * flows + 1),
        out_specs=[vmem, vmem],
        out_shape=[shaped(flows, height, width), jax.ShapeDtypeStruct(packed.shape, F32)],
        scratch_shapes=[
            pltpu.VMEM((flows, 2 * height, width), BF),
            pltpu.VMEM((flows, height, width), BF),
            pltpu.VMEM((flows, height, width), BF),
            pltpu.VMEM((flows, height, width), BF),
            pltpu.VMEM((flows, height // 2, width), BF),
            pltpu.VMEM((flows, height // 4, width), BF),
            pltpu.VMEM((flows, height // 4, width), BF),
            pltpu.VMEM((flows, height // 4, width), BF),
            pltpu.VMEM((5,) + packed.shape, F32),
            pltpu.VMEM((4,) + packed.shape, F32),
            pltpu.SemaphoreType.DMA((7, chunks)),
            pltpu.SemaphoreType.DMA((7, chunks)),
            pltpu.SemaphoreType.DMA((5,)),
            pltpu.SemaphoreType.DMA((5,)),
        ],
        compiler_params=pltpu.CompilerParams(
            collective_id=0, has_side_effects=True, vmem_limit_bytes=40 * 2**20
        ),
        cost_estimate=cost(total, 20 * total),
        name="reduce_grads",
    )(*[t for three in terms for t in three], packed)


def swap(array, axis, bit):
    size = lax.axis_size(axis)
    return lax.ppermute(array, axis, [(i, i ^ bit) for i in range(size)])


def gather_hops(shards):
    side = lax.axis_index("rep") & 1
    halves = [s.shape[0] // 2 for s in shards]
    mine = [lax.dynamic_slice_in_dim(s, side * h, h, axis=0) for s, h in zip(shards, halves)]
    direct, core = yield [swap(m, "shard", 2) for m in mine], [swap(s, "shard", 1) for s in shards]
    relayed, cross = yield [swap(d, "rep", 1) for d in direct], [swap(d, "shard", 1) for d in direct]
    cross_relayed = yield [swap(r, "shard", 1) for r in relayed]
    return [list(p) for p in zip(shards, core, direct, relayed, cross, cross_relayed)]


def piece_starts(shard):
    height = shard.shape[0]
    me = lax.axis_index("shard")
    side = lax.axis_index("rep") & 1
    half = height // 2
    near, core, far, cross = [(me ^ o) * height for o in range(4)]
    return [near, core, far + side * half, far + (1 - side) * half, cross + side * half, cross + (1 - side) * half]


def added(*terms):
    return functools.reduce(jnp.add, [t.astype(F32) for t in terms]).astype(BF)


class Flow:
    def __init__(self, hops):
        self.hops = hops
        self.result = None
        self.flying = next(hops)

    def land(self, arrived):
        try:
            self.flying = self.hops.send(arrived)
        except StopIteration as stop:
            self.flying, self.result = None, stop.value


class Line:
    def __init__(self):
        self.flows = []
        self.recent = []

    def step(self, arrays, flows=None):
        moving = [f for f in (self.flows if flows is None else flows) if f.flying is not None]
        held = self.recent
        arrays, arrived, held = lax.optimization_barrier((arrays, [f.flying for f in moving], held))
        for flow, value in zip(moving, arrived):
            flow.land(value)
        self.recent = []
        return arrays

    def start(self, hops):
        flow = Flow(hops)
        self.flows.append(flow)
        return flow


def group_sum(grad):
    return lax.psum_scatter(grad, "shard", scatter_dimension=0, tiled=True)


def owned_hops(parts):
    keep, passed, sent = parts
    height = keep.shape[0]
    come = yield swap(sent, "shard", 1)
    onward = yield swap(added(passed, come[height:]), "shard", 2)
    return added(keep, come[:height], onward)


def replica_sum(owned):
    return lax.psum(owned, "rep").astype(F32)


def local(
    tokens,
    segment_ids,
    cotangent,
    w_qkv,
    b_query,
    b_value,
    w_out,
    b_out,
    gain_one,
    shift_one,
    w_in,
    b_in,
    w_ffo,
    b_ffo,
    gain_two,
    shift_two,
):
    micro, sequences, length, width = tokens.shape
    total = micro * sequences
    rows = total * length
    group = lax.axis_size("shard")
    hidden_width = w_in.shape[1]
    x = tokens.reshape(rows, width)
    seg = segment_ids.reshape(total, length)
    cot = cotangent.reshape(rows, width)
    me = lax.axis_index("shard")
    direct = group == 4 and lax.axis_size("rep") == 8

    part = b_query.shape[0]
    line = Line()
    small_shards = (b_query, b_value, b_out, gain_one, shift_one, b_ffo, gain_two, shift_two, b_in)
    small = jnp.concatenate(small_shards).reshape(1, -1)
    if direct:
        qkv_flow = Flow(gather_hops([w_qkv]))
        near = swap(small, "shard", 1)
        pair = jnp.concatenate([small, near], axis=0)
        four = jnp.concatenate([pair, swap(pair, "shard", 2)], axis=0)
        order = [jnp.bitwise_xor(me, o) for o in range(4)]
        small_full = jnp.concatenate([lax.dynamic_slice_in_dim(four, o, 1, axis=0) for o in order], axis=0)
        (later,) = line.step([w_ffo], [qkv_flow])
        later_flow = Flow(gather_hops([later]))
        seg = line.step(seg, [qkv_flow])
        x_first = line.step(x, [qkv_flow])
        (qkv_pieces,) = qkv_flow.result
        qkv_starts = jnp.stack(piece_starts(w_qkv)).astype(jnp.int32)
        layer_lists = [[lax.all_gather(w, "shard", axis=0, tiled=True)] for w in (w_out, w_in)]
        layer_starts = jnp.stack([jnp.int32(0)] * 2 + piece_starts(w_ffo)).astype(jnp.int32)
        counts = (1, 1, 6)
    else:
        small_full = lax.all_gather(small, "shard", axis=0, tiled=True)
        qkv_pieces, *layer_lists = [
            [lax.all_gather(w, "shard", axis=0, tiled=True)] for w in (w_qkv, w_out, w_in, w_ffo)
        ]
        x_first = x
        qkv_starts = jnp.zeros((1,), jnp.int32)
        layer_starts = jnp.zeros((3,), jnp.int32)
        counts = (1, 1, 1)
    small_full = small_full.astype(F32)
    vectors = [small_full[:, i * part : (i + 1) * part].reshape(1, -1) for i in range(8)]
    bias_all = jnp.concatenate([vectors[0], jnp.zeros_like(vectors[0]), vectors[1]], axis=1)
    vec = jnp.concatenate(vectors[2:] + [jnp.zeros((2, width), F32)], axis=0)
    bias_in = small_full[:, 8 * part :].reshape(1, -1)

    windows = windows_of(seg)
    block = 256
    (projected,) = row_call(
        functools.partial(project_kernel, len(qkv_pieces)),
        "project",
        rows,
        block,
        qkv_starts,
        [x_first],
        [bias_all],
        qkv_pieces,
        [shaped(rows, 3 * width)],
        [],
        [pltpu.VMEM((width, 3 * width), BF)],
        6 * rows * width * width,
    )
    if direct:
        projected = line.step(projected, [later_flow])
    attended, lse = attend_forward(projected, windows, total)
    if direct:
        attended = line.step(attended, [later_flow])
        attended = line.step(attended, [later_flow])
        layer_lists = layer_lists + later_flow.result
    layer_pieces = sum(layer_lists, [])
    weights_scratch = [
        pltpu.VMEM((width, width), BF),
        pltpu.VMEM((width, hidden_width), BF),
        pltpu.VMEM((hidden_width, width), BF),
    ]
    layer_flops = 2 * rows * width * (width + 2 * hidden_width)
    output, normed, n_one, rstd_one, d_second, hidden, slope, sums_two = row_call(
        functools.partial(layer_forward_kernel, counts),
        "layer_forward",
        rows,
        block,
        layer_starts,
        [x, attended, cot],
        [vec, bias_in],
        layer_pieces,
        [
            shaped(rows, width),
            shaped(rows, width),
            shaped(rows, width),
            shaped(rows, 128, dtype=F32),
            shaped(rows, width),
            shaped(rows, hidden_width),
            shaped(rows, hidden_width),
        ],
        [shaped(24, width, dtype=F32)],
        weights_scratch,
        layer_flops,
    )

    place = [jnp.bitwise_xor(me, o) for o in range(4)]
    slots = jnp.stack(
        [(p & 1) * 2 + lax.shift_right_logical(p, 1) for p in place] + [jnp.bitwise_xor(me, j) for j in (1, 3, 2, 0)]
    ).astype(jnp.int32)

    grad_ffo = plain_grad(hidden, d_second, "grad_ffo")
    owned_ffo = group_sum(grad_ffo)
    d_pre, d_branch, d_attended, sums_one, sums_in = row_call(
        functools.partial(layer_backward_kernel, counts),
        "layer_backward",
        rows,
        block,
        layer_starts,
        [d_second, slope, n_one, rstd_one],
        [vec],
        layer_pieces,
        [shaped(rows, hidden_width), shaped(rows, width), shaped(rows, width)],
        [shaped(24, width, dtype=F32), shaped(8, hidden_width, dtype=F32)],
        weights_scratch,
        layer_flops,
    )
    groups = 3
    if direct:
        *in_terms, _ = weight_grad(slots, normed, d_pre, "grad_in")
        in_flow = Flow(owned_hops(in_terms))
        d_branch, _ = lax.optimization_barrier((d_branch, in_terms[0]))
        *out_terms, _ = weight_grad(slots, attended, d_branch, "grad_out")
        out_flow = Flow(owned_hops(out_terms))
        d_attended, owned_ffo, _ = line.step((d_attended, owned_ffo, out_terms[0]), [in_flow])
        grad_ffo = replica_sum(owned_ffo)
        d_heads = attend_backward(projected, d_attended, attended, lse, windows, total, groups)
        d_heads = line.step(d_heads, [in_flow, out_flow])
        *terms, head_sums = weight_grad(slots, x, d_heads, "grad_qkv")
        d_branch, grad_ffo, owned_in, _ = line.step((d_branch, grad_ffo, in_flow.result, terms[0]), [out_flow])
        grad_in, grad_out = replica_sum(owned_in), replica_sum(out_flow.result)
    else:
        grad_ffo = replica_sum(owned_ffo)
        grad_in = replica_sum(group_sum(plain_grad(normed, d_pre, "grad_in")))
        grad_out = replica_sum(group_sum(plain_grad(attended, d_branch, "grad_out")))
        d_heads = attend_backward(projected, d_attended, attended, lse, windows, total, groups)
        grads = replica_sum(group_sum(plain_grad(x, d_heads, "grad_qkv")))
        head_sums = fold_rows(d_heads.astype(F32))

    def folded(sums):
        return [jnp.sum(sums[i : i + 8], axis=0) for i in range(0, sums.shape[0], 8)]

    d_gain_two, d_shift_two, d_ffo_bias = folded(sums_two)
    d_gain_one, d_shift_one, d_out_bias = folded(sums_one)
    (d_in_bias,) = folded(sums_in)
    cut = width // groups
    head_sums = jnp.sum(head_sums, axis=0).reshape(groups, 3, cut)
    d_query_bias = head_sums[:, 0].reshape(-1)
    d_value_bias = head_sums[:, 2].reshape(-1)
    smalls = (
        d_query_bias, d_value_bias, d_out_bias, d_gain_one, d_shift_one, d_ffo_bias, d_gain_two, d_shift_two,
        d_in_bias,
    )
    packed = jnp.concatenate([s.reshape(group, -1) for s in smalls], axis=1)
    (d_tokens,) = row_call(
        functools.partial(input_grad_kernel, len(qkv_pieces), groups),
        "input_grad",
        rows,
        block,
        qkv_starts,
        [d_branch, d_heads],
        [],
        qkv_pieces,
        [shaped(rows, width)],
        [],
        [pltpu.VMEM((width, 3 * width), BF)],
        6 * rows * width * width,
    )
    if direct:
        reduced, packed = reduce_call([terms], packed)
        grads = reduced[0].astype(F32)
    else:
        packed = lax.psum(packed, ("shard", "rep"))
    grad_qkv = grads.reshape(part, groups, 3, cut).transpose(0, 2, 1, 3).reshape(part, 3 * width)
    mine = lax.dynamic_index_in_dim(packed, me, 0, keepdims=False)
    sm = [mine[i * part : (i + 1) * part] for i in range(8)]
    gqb, gvb, gob, gg1, gs1, gfb, gg2, gs2 = sm
    gib = mine[8 * part :]
    return (
        output.reshape(tokens.shape),
        d_tokens.reshape(tokens.shape),
        grad_qkv,
        gqb,
        gvb,
        grad_out,
        gob,
        gg1,
        gs1,
        grad_in,
        gib,
        grad_ffo,
        gfb,
        gg2,
        gs2,
    )


def solution(mesh):
    data = P(None, ("shard", "rep"), None, None)
    matrix = P("shard", None)
    vector = P("shard")
    return jax.shard_map(
        local,
        mesh=mesh,
        in_specs=(
            data,
            P(None, ("shard", "rep"), None),
            data,
            matrix,
            vector,
            vector,
            matrix,
            vector,
            vector,
            vector,
            matrix,
            vector,
            matrix,
            vector,
            vector,
            vector,
        ),
        out_specs=(
            data,
            data,
            matrix,
            vector,
            vector,
            matrix,
            vector,
            vector,
            vector,
            matrix,
            vector,
            matrix,
            vector,
            vector,
            vector,
        ),
        check_vma=False,
    )
```

```python
import functools
import math

import jax
import jax.numpy as jnp
from jax import lax
from jax.experimental import pallas as pl
from jax.experimental.pallas import tpu as pltpu
from jax.sharding import PartitionSpec as P

HEADS = 12
HEAD_DIM = 64
PAIR = 2 * HEAD_DIM
TILE = 128

epsilon = 1e-05
masked_score = -1e30
BF = jnp.bfloat16
F32 = jnp.float32
VMEM_LIMIT = 60 * 2**20


def dot_nn(a, b):
    return lax.dot_general(a, b, (((1,), (0,)), ((), ())), preferred_element_type=F32)


def dot_nt(a, b):
    return lax.dot_general(a, b, (((1,), (1,)), ((), ())), preferred_element_type=F32)


def dot_tn(a, b):
    return lax.dot_general(a, b, (((0,), (0,)), ((), ())), preferred_element_type=F32)


def head_rows(value):
    lane = lax.broadcasted_iota(jnp.int32, (1, PAIR), 1)
    first = jnp.where(lane < HEAD_DIM, value, 0.0).astype(BF)
    second = jnp.where(lane < HEAD_DIM, 0.0, value).astype(BF)
    return first, second


def stack_heads(block, rows):
    return jnp.concatenate([block * rows[0], block * rows[1]], axis=0)


def diagonal_back(transposed):
    kept = jnp.concatenate(
        [transposed[:HEAD_DIM, :TILE], transposed[HEAD_DIM:, TILE:]], axis=0
    )
    return kept.T


def for_windows(count, tiles, body):
    sizes = [t for t in range(1, tiles + 1) if t < 7 or t == tiles]
    below = 0
    for size in sizes:
        @pl.when((count > below) & (count <= size))
        def _(size=size):
            body(size)

        below = size


def attend_forward_kernel(pairs, tiles, low_ref, count_ref, q_ref, k_ref, v_ref, kseg_ref, qseg_ref, o_ref, lse_ref):
    place = pl.program_id(0) * tiles + pl.program_id(1)
    low = low_ref[place]
    count = count_ref[place]
    rows_of = head_rows(1.0 / math.sqrt(HEAD_DIM))

    def window(size):
        start = jnp.minimum(low, tiles - size) * TILE
        chunks = [pl.ds(pl.multiple_of(start + c * TILE, TILE), TILE) for c in range(size)]
        whole = pl.ds(pl.multiple_of(start, TILE), size * TILE)
        masks = [kseg_ref[c, :] == qseg_ref[0] for c in chunks]
        def first(p):
            lanes = slice(p * PAIR, (p + 1) * PAIR)
            queries = stack_heads(q_ref[:, lanes], rows_of)
            scores = []
            for c, mask in zip(chunks, masks):
                part = dot_nt(k_ref[c, lanes], queries)
                scores.append(
                    jnp.concatenate(
                        [
                            jnp.where(mask, part[:, :TILE], masked_score),
                            jnp.where(mask, part[:, TILE:], masked_score),
                        ],
                        axis=1,
                    )
                )
            return scores

        def second(p, scores):
            lanes = slice(p * PAIR, (p + 1) * PAIR)
            top = functools.reduce(jnp.maximum, [jnp.max(s, axis=0, keepdims=True) for s in scores])
            exps = [jnp.exp(s - top) for s in scores]
            total = functools.reduce(jnp.add, [jnp.sum(e, axis=0, keepdims=True) for e in exps])
            weights = jnp.concatenate([e.astype(BF) for e in exps], axis=0)
            mixed = dot_tn(v_ref[whole, lanes], weights) / total
            o_ref[:, lanes] = diagonal_back(mixed).astype(BF)
            lse_ref[0, p : p + 1, :] = top + jnp.log(total)

        ready = first(0)
        for p in range(pairs):
            after = first(p + 1) if p + 1 < pairs else None
            second(p, ready)
            ready = after

    for_windows(count, tiles, window)


def attend_backward_kernel(
    pairs, tiles, low_ref, count_ref, q_ref, k_ref, v_ref, do_ref, o_ref, lse_ref, kseg_ref, qseg_ref,
    out_ref, dk_acc, dv_acc,
):
    block = pl.program_id(2)
    first_pair = pl.program_id(1) * pairs
    place = pl.program_id(0) * tiles + block
    low = low_ref[place]
    count = count_ref[place]
    part = pairs * PAIR
    scale = 1.0 / math.sqrt(HEAD_DIM)
    scaled_rows = head_rows(scale)
    plain_rows = head_rows(1.0)

    @pl.when(block == 0)
    def _():
        dk_acc[...] = jnp.zeros_like(dk_acc)
        dv_acc[...] = jnp.zeros_like(dv_acc)

    def window(size):
        start = jnp.minimum(low, tiles - size) * TILE
        chunks = [pl.ds(pl.multiple_of(start + c * TILE, TILE), TILE) for c in range(size)]
        whole = pl.ds(pl.multiple_of(start, TILE), size * TILE)
        masks = [kseg_ref[c, :] == qseg_ref[0] for c in chunks]
        mine = pl.ds(pl.multiple_of(block * TILE, TILE), TILE)
        for p in range(pairs):
            lanes = slice(p * PAIR, (p + 1) * PAIR)
            queries = stack_heads(q_ref[:, lanes], scaled_rows)
            grads = do_ref[:, lanes]
            stacked = stack_heads(grads, plain_rows)
            product = (grads.astype(F32) * o_ref[:, lanes].astype(F32)).T
            row_dot = jnp.concatenate(
                [
                    jnp.sum(product[:HEAD_DIM], axis=0, keepdims=True),
                    jnp.sum(product[HEAD_DIM:], axis=0, keepdims=True),
                ],
                axis=1,
            )
            lse = lse_ref[0, pl.ds(first_pair + p, 1), :]
            kept = []
            weights = []
            all_scores = dot_nt(k_ref[whole, lanes], queries)
            all_d_probs = dot_nt(v_ref[whole, lanes], stacked)
            for n, mask in enumerate(masks):
                rows_n = slice(n * TILE, (n + 1) * TILE)
                part_scores = all_scores[rows_n] - lse
                d_probs = all_d_probs[rows_n]
                probs = jnp.exp(
                    jnp.concatenate(
                        [
                            jnp.where(mask, part_scores[:, :TILE], masked_score),
                            jnp.where(mask, part_scores[:, TILE:], masked_score),
                        ],
                        axis=1,
                    )
                )
                kept.append((probs * (d_probs - row_dot)).astype(BF))
                weights.append(probs.astype(BF))
            kept = jnp.concatenate(kept, axis=0)
            weights = jnp.concatenate(weights, axis=0)
            dv_acc[whole, lanes] += dot_nn(weights, stacked)
            dk_acc[whole, lanes] += dot_nn(kept, queries)
            mixed = dot_tn(k_ref[whole, lanes], kept) * scale
            out_ref[mine, lanes] = diagonal_back(mixed).astype(BF)

    for_windows(count, tiles, window)

    @pl.when(block == tiles - 1)
    def _():
        out_ref[:, part : 2 * part] = dk_acc[...].astype(BF)
        out_ref[:, 2 * part :] = dv_acc[...].astype(BF)


def windows_of(segments):
    sequences, length = segments.shape
    tiles = length // TILE
    blocked = segments.reshape(sequences, tiles, TILE)
    first = blocked[:, :, 0]
    last = blocked[:, :, TILE - 1]
    starts = jnp.sum((segments[:, None, :] < first[:, :, None]).astype(jnp.int32), axis=-1)
    ends = jnp.sum((segments[:, None, :] <= last[:, :, None]).astype(jnp.int32), axis=-1)
    bits = TILE.bit_length() - 1
    low = lax.shift_right_logical(starts, bits)
    count = lax.shift_right_logical(ends + TILE - 1, bits) - low
    key_ids = jnp.broadcast_to(segments.reshape(sequences * length, 1), (sequences * length, TILE))
    query_ids = blocked.reshape(sequences * tiles, 1, TILE)
    return low.reshape(-1), count.reshape(-1), key_ids, query_ids


def attend_forward(projected, windows, sequences):
    low, count, key_ids, query_ids = windows
    rows = projected.shape[0]
    width = projected.shape[1] // 3
    length = rows // sequences
    tiles = length // TILE
    pairs = width // PAIR
    return pl.pallas_call(
        functools.partial(attend_forward_kernel, pairs, tiles),
        grid_spec=pltpu.PrefetchScalarGridSpec(
            num_scalar_prefetch=2,
            grid=(sequences, tiles),
            in_specs=[
                pl.BlockSpec((TILE, width), lambda s, b, *_: (s * tiles + b, 0)),
                pl.BlockSpec((length, width), lambda s, b, *_: (s, 1)),
                pl.BlockSpec((length, width), lambda s, b, *_: (s, 2)),
                pl.BlockSpec((length, TILE), lambda s, b, *_: (s, 0)),
                pl.BlockSpec((1, 1, TILE), lambda s, b, *_: (s * tiles + b, 0, 0)),
            ],
            out_specs=[
                pl.BlockSpec((TILE, width), lambda s, b, *_: (s * tiles + b, 0)),
                pl.BlockSpec((1, 8, 2 * TILE), lambda s, b, *_: (s * tiles + b, 0, 0)),
            ],
        ),
        out_shape=[
            jax.ShapeDtypeStruct((rows, width), BF),
            jax.ShapeDtypeStruct((sequences * tiles, 8, 2 * TILE), F32),
        ],
        compiler_params=pltpu.CompilerParams(vmem_limit_bytes=VMEM_LIMIT),
        cost_estimate=cost(8 * 10**9, 16 * 10**6),
        name="attend_forward",
    )(low, count, projected, projected, projected, key_ids, query_ids)


def attend_backward(projected, d_attended, attended, lse, windows, sequences, groups):
    low, count, key_ids, query_ids = windows
    rows = projected.shape[0]
    width = projected.shape[1] // 3
    length = rows // sequences
    tiles = length // TILE
    part = width // groups
    pairs = part // PAIR
    query_spec = pl.BlockSpec((TILE, part), lambda s, g, b, *_: (s * tiles + b, g))
    return pl.pallas_call(
        functools.partial(attend_backward_kernel, pairs, tiles),
        grid_spec=pltpu.PrefetchScalarGridSpec(
            num_scalar_prefetch=2,
            grid=(sequences, groups, tiles),
            in_specs=[
                query_spec,
                pl.BlockSpec((length, part), lambda s, g, b, *_: (s, groups + g)),
                pl.BlockSpec((length, part), lambda s, g, b, *_: (s, 2 * groups + g)),
                query_spec,
                query_spec,
                pl.BlockSpec((1, 8, 2 * TILE), lambda s, g, b, *_: (s * tiles + b, 0, 0)),
                pl.BlockSpec((length, TILE), lambda s, g, b, *_: (s, 0)),
                pl.BlockSpec((1, 1, TILE), lambda s, g, b, *_: (s * tiles + b, 0, 0)),
            ],
            out_specs=pl.BlockSpec((length, 3 * part), lambda s, g, b, *_: (s, g)),
            scratch_shapes=[pltpu.VMEM((length, part), F32), pltpu.VMEM((length, part), F32)],
        ),
        out_shape=jax.ShapeDtypeStruct((rows, 3 * width), BF),
        compiler_params=pltpu.CompilerParams(vmem_limit_bytes=VMEM_LIMIT),
        cost_estimate=cost(3 * 10**6, 3 * 10**4),
        name="attend_backward",
    )(low, count, projected, projected, projected, d_attended, attended, lse, key_ids, query_ids)


def row_mean(values):
    return jnp.mean(values, axis=-1, keepdims=True)


def fold_rows(values):
    rows, width = values.shape
    return jnp.sum(values.reshape(rows // 8, 8, width), axis=0)


def load_pieces(starts_ref, pieces, targets, sems):
    copies = []
    for n, (piece, target) in enumerate(zip(pieces, targets)):
        height = piece.shape[0]
        start = pl.multiple_of(starts_ref[n], math.gcd(height, 128))
        copies.append(pltpu.make_async_copy(piece, target.at[pl.ds(start, height)], sems.at[n]))
    for copy in copies:
        copy.start()
    for copy in copies:
        copy.wait()


def gelu_parts(values):
    bell = jnp.exp(values * values * -0.5)
    t = 1.0 / (1.0 + jnp.abs(values) * (0.3275911 / math.sqrt(2.0)))
    poly = t * (
        0.5 * 0.254829592
        + t * (0.5 * -0.284496736 + t * (0.5 * 1.421413741 + t * (0.5 * -1.453152027 + t * (0.5 * 1.061405429))))
    )
    tail = poly * bell
    phi = jnp.where(values >= 0.0, 1.0 - tail, tail)
    return values * phi, phi + values * bell * (1.0 / math.sqrt(2.0 * math.pi))


def project_kernel(count, starts_ref, x_ref, bias_ref, *refs):
    pieces = refs[:count]
    o_ref, weight, sems = refs[count:]

    @pl.when(pl.program_id(0) == 0)
    def _():
        load_pieces(starts_ref, pieces, [weight] * count, sems)

    o_ref[...] = (dot_nn(x_ref[...], weight[...]) + bias_ref[...]).astype(BF)


FFN_CHUNK = 512


def layer_forward_kernel(
    counts, starts_ref, x_ref, att_ref, cot_ref, vec_ref, bin_ref, *refs
):
    total = sum(counts)
    pieces = refs[:total]
    (
        out_ref, normed_ref, none_ref, rstd_ref, dsec_ref, hidden_ref, slope_ref, sums_ref,
        w_out, w_in, w_ffo, sems,
    ) = refs[total:]
    targets = [w_out] * counts[0] + [w_in] * counts[1] + [w_ffo] * counts[2]

    @pl.when(pl.program_id(0) == 0)
    def _():
        load_pieces(starts_ref, pieces, targets, sems)
        sums_ref[...] = jnp.zeros_like(sums_ref)

    b_out, gain_one, shift_one, b_ffo, gain_two, shift_two = [vec_ref[i : i + 1, :] for i in range(6)]
    res = x_ref[...].astype(F32) + (dot_nn(att_ref[...], w_out[...]) + b_out)
    center = res - row_mean(res)
    rstd = lax.rsqrt(row_mean(center * center) + epsilon)
    n_one = center * rstd
    normed = (n_one * gain_one + shift_one).astype(BF)
    normed_ref[...] = normed
    none_ref[...] = n_one.astype(BF)
    rstd_ref[...] = jnp.broadcast_to(rstd, rstd_ref.shape)
    hidden_width = w_in.shape[1]
    second = None
    pres = []
    for c in range(0, hidden_width, FFN_CHUNK):
        cols = slice(c, c + FFN_CHUNK)
        pre = dot_nn(normed, w_in[:, cols]) + bin_ref[:, cols]
        value, slope = gelu_parts(pre)
        value = value.astype(BF)
        hidden_ref[:, cols] = value
        slope_ref[:, cols] = slope.astype(BF)
        term = dot_nn(value, w_ffo[cols, :])
        second = term if second is None else second + term
    res = normed.astype(F32) + (second + b_ffo)
    center = res - row_mean(res)
    rstd = lax.rsqrt(row_mean(center * center) + epsilon)
    n_two = center * rstd
    out_ref[...] = (n_two * gain_two + shift_two).astype(BF)
    cot = cot_ref[...].astype(F32)
    inner = cot * gain_two
    d_second = (rstd * (inner - row_mean(inner) - n_two * row_mean(inner * n_two))).astype(BF)
    dsec_ref[...] = d_second
    sums_ref[0:8, :] += fold_rows(cot * n_two)
    sums_ref[8:16, :] += fold_rows(cot)
    sums_ref[16:24, :] += fold_rows(d_second.astype(F32))


def layer_backward_kernel(counts, starts_ref, dsec_ref, slope_ref, none_ref, rstd_ref, vec_ref, *refs):
    total = sum(counts)
    pieces = refs[:total]
    dpre_ref, dbranch_ref, datt_ref, sums_ref, bin_ref, w_out, w_in, w_ffo, sems = refs[total:]
    targets = [w_out] * counts[0] + [w_in] * counts[1] + [w_ffo] * counts[2]

    @pl.when(pl.program_id(0) == 0)
    def _():
        load_pieces(starts_ref, pieces, targets, sems)
        sums_ref[...] = jnp.zeros_like(sums_ref)
        bin_ref[...] = jnp.zeros_like(bin_ref)

    gain_one = vec_ref[1:2, :]
    d_second = dsec_ref[...]
    d_norm = d_second.astype(F32)
    for c in range(0, w_in.shape[1], FFN_CHUNK):
        cols = slice(c, c + FFN_CHUNK)
        d_pre = (dot_nt(d_second, w_ffo[cols, :]) * slope_ref[:, cols].astype(F32)).astype(BF)
        dpre_ref[:, cols] = d_pre
        bin_ref[:, cols] += fold_rows(d_pre.astype(F32))
        d_norm = d_norm + dot_nt(d_pre, w_in[:, cols])
    n_one = none_ref[...].astype(F32)
    inner = d_norm * gain_one
    d_res = rstd_ref[:, 0:1] * (inner - row_mean(inner) - n_one * row_mean(inner * n_one))
    d_branch = d_res.astype(BF)
    dbranch_ref[...] = d_branch
    datt_ref[...] = dot_nt(d_branch, w_out[...]).astype(BF)
    sums_ref[0:8, :] += fold_rows(d_norm * n_one)
    sums_ref[8:16, :] += fold_rows(d_norm)
    sums_ref[16:24, :] += fold_rows(d_branch.astype(F32))


def input_grad_kernel(count, groups, starts_ref, dbranch_ref, *refs):
    grads = refs[0]
    pieces = refs[1 : 1 + count]
    o_ref, weight, sems = refs[1 + count :]

    @pl.when(pl.program_id(0) == 0)
    def _():
        load_pieces(starts_ref, pieces, [weight] * count, sems)

    width = dbranch_ref.shape[1]
    part = width // groups
    total = dbranch_ref[...].astype(F32)
    for g in range(groups):
        for n in range(3):
            here = (3 * g + n) * part
            first = n * width + g * part
            total = total + dot_nt(grads[:, here : here + part], weight[:, first : first + part])
    o_ref[...] = total.astype(BF)


def weight_grad_cols_kernel(slots, owner_ref, a_ref, b_ref, keep_ref, pass_ref, send_ref, sums_ref, held):
    terms = b_ref[...]
    sums_ref[...] = fold_rows(terms.astype(F32))
    part = dot_tn(a_ref[...], terms).astype(BF)
    height = keep_ref.shape[0]
    for owner in range(4):
        held[owner_ref[owner]] = part[owner * height : (owner + 1) * height]
    keep_ref[...] = held[0]
    pass_ref[...] = held[1]
    send_ref[0:height, :] = held[2]
    send_ref[height:, :] = held[3]


PARAMS = pltpu.CompilerParams(vmem_limit_bytes=VMEM_LIMIT)


def cost(flops, bytes_accessed):
    return pl.CostEstimate(flops=int(flops) // 16, bytes_accessed=int(bytes_accessed) // 16, transcendentals=0)


def whole_spec(array):
    zeros = (0,) * array.ndim
    return pl.BlockSpec(array.shape, lambda *_: zeros)


ANY = pl.BlockSpec(memory_space=pl.ANY)


def row_call(kernel, name, rows, block, scalars, blocked, fixed, pieces, outs, accs, scratch, flops):
    in_specs = (
        [pl.BlockSpec((block, a.shape[1]), lambda i, *_: (i, 0)) for a in blocked]
        + [whole_spec(a) for a in fixed]
        + [ANY] * len(pieces)
    )
    out_specs = [pl.BlockSpec((block, s.shape[1]), lambda i, *_: (i, 0)) for s in outs] + [
        whole_spec(s) for s in accs
    ]
    moved = sum(a.size * a.dtype.itemsize for a in list(blocked) + list(pieces) + list(outs))
    return pl.pallas_call(
        kernel,
        grid_spec=pltpu.PrefetchScalarGridSpec(
            num_scalar_prefetch=1,
            grid=(rows // block,),
            in_specs=in_specs,
            out_specs=out_specs,
            scratch_shapes=list(scratch) + [pltpu.SemaphoreType.DMA((len(pieces),))],
        ),
        out_shape=list(outs) + list(accs),
        compiler_params=PARAMS,
        cost_estimate=cost(flops, moved),
        name=name,
    )(scalars, *blocked, *fixed, *pieces)


def shaped(*shape, dtype=BF):
    return jax.ShapeDtypeStruct(shape, dtype)


def weight_grad(slots, a, b, name):
    rows, height = a.shape
    width = b.shape[1]
    part = height // 4
    flops = 2 * rows * height * width
    moved = 2 * (rows * height + rows * width + height * width)
    block = 768
    return pl.pallas_call(
        functools.partial(weight_grad_cols_kernel, 4),
        grid_spec=pltpu.PrefetchScalarGridSpec(
            num_scalar_prefetch=1,
            grid=(width // block,),
            in_specs=[
                pl.BlockSpec((rows, height), lambda t, s: (0, 0)),
                pl.BlockSpec((rows, block), lambda t, s: (0, t)),
            ],
            out_specs=[
                pl.BlockSpec((part, block), lambda t, s: (0, t)),
                pl.BlockSpec((part, block), lambda t, s: (0, t)),
                pl.BlockSpec((2 * part, block), lambda t, s: (0, t)),
                pl.BlockSpec((8, block), lambda t, s: (0, t)),
            ],
            scratch_shapes=[pltpu.VMEM((4, part, block), BF)],
        ),
        out_shape=[
            shaped(part, width),
            shaped(part, width),
            shaped(2 * part, width),
            shaped(8, width, dtype=F32),
        ],
        compiler_params=PARAMS,
        cost_estimate=cost(flops, moved),
        name=name,
    )(slots, a, b)


def plain_grad_kernel(a_ref, b_ref, o_ref):
    o_ref[...] = dot_tn(a_ref[...], b_ref[...]).astype(BF)


def plain_grad(a, b, name):
    rows, height = a.shape
    width = b.shape[1]
    block = 768
    tall = height > width
    steps = (height if tall else width) // block
    specs = [
        pl.BlockSpec((rows, block if tall else height), (lambda t: (0, t)) if tall else (lambda t: (0, 0))),
        pl.BlockSpec((rows, width if tall else block), (lambda t: (0, 0)) if tall else (lambda t: (0, t))),
    ]
    out = (
        pl.BlockSpec((block, width), lambda t: (t, 0)) if tall else pl.BlockSpec((height, block), lambda t: (0, t))
    )
    return pl.pallas_call(
        plain_grad_kernel,
        grid=(steps,),
        in_specs=specs,
        out_specs=out,
        out_shape=shaped(height, width),
        compiler_params=PARAMS,
        cost_estimate=cost(2 * rows * height * width, 2 * (rows * (height + width) + height * width)),
        name=name,
    )(a, b)


REDUCE_COLS = 768
REDUCE_LAG = 1


def reduce_kernel(flows, *refs):
    parts = [refs[3 * f : 3 * f + 3] for f in range(flows)]
    small_ref = refs[3 * flows]
    out_ref, total_ref = refs[3 * flows + 1 : 3 * flows + 3]
    come, onward, across, owned, half_in, quarter_in, quarter, far_in, small_in, small_sum = refs[
        3 * flows + 3 : 3 * flows + 13
    ]
    sent, got, small_sent, small_got = refs[3 * flows + 13 :]
    me = lax.axis_index("shard")
    place = lax.axis_index("rep")
    y = lax.rem(place, 2)
    z = lax.rem(lax.div(place, 2), 2)
    peers = [
        {"shard": me + 1 - 2 * lax.rem(me, 2)},
        {"shard": lax.rem(me + 2, 4)},
        {"rep": place + 1 - 2 * y},
        {"rep": place + 2 - 4 * z},
        {"rep": lax.rem(place + 4, 8)},
    ]
    barrier = pltpu.get_barrier_semaphore()
    for peer in peers:
        pl.semaphore_signal(barrier, inc=1, device_id=peer, device_id_type=pl.DeviceIdType.MESH)
    pl.semaphore_wait(barrier, len(peers))

    height = owned.shape[1]
    half, fourth = height // 2, height // 4
    width = owned.shape[2]
    chunks = [(f, c) for f in range(flows) for c in range(0, width, REDUCE_COLS)]
    started = []

    def rows(start, size):
        return pl.ds(pl.multiple_of(start, 16), size)

    def send(hop, n, source, target, peer):
        copy = pltpu.make_async_remote_copy(
            src_ref=source,
            dst_ref=target,
            send_sem=sent.at[hop, n],
            recv_sem=got.at[hop, n],
            device_id=peers[peer],
            device_id_type=pl.DeviceIdType.MESH,
        )
        copy.start()
        started.append(copy)
        return copy

    def small_send(hop, source):
        copy = pltpu.make_async_remote_copy(
            src_ref=source,
            dst_ref=small_in.at[hop],
            send_sem=small_sent.at[hop],
            recv_sem=small_got.at[hop],
            device_id=peers[hop],
            device_id_type=pl.DeviceIdType.MESH,
        )
        copy.start()
        started.append(copy)
        return copy

    def plus(*terms):
        return functools.reduce(jnp.add, [t.astype(F32) for t in terms])

    mine_half = y * half
    mine_fourth = y * half + z * fourth
    copies = {}
    for n, (f, c) in enumerate(chunks):
        cols = pl.ds(c, REDUCE_COLS)
        copies[0, n] = send(0, n, parts[f][2].at[:, cols], come.at[f, :, cols], 0)
    flying = small_send(0, small_ref)
    for n, (f, c) in enumerate(chunks):
        cols = pl.ds(c, REDUCE_COLS)
        copies[0, n].wait_recv()
        onward[f, :, cols] = plus(parts[f][1][:, cols], come[f, pl.ds(height, height), cols]).astype(BF)
        copies[1, n] = send(1, n, onward.at[f, :, cols], across.at[f, :, cols], 1)

    def small_step(hop):
        flying.wait_recv()
        total = plus(small_ref[...] if hop == 0 else small_sum[hop - 1], small_in[hop])
        if hop == 4:
            total_ref[...] = total
            return None
        small_sum[hop] = total
        return small_send(hop + 1, small_sum.at[hop])

    def step(stage, n):
        f, c = chunks[n]
        cols = pl.ds(c, REDUCE_COLS)
        copies[stage, n].wait_recv()
        if stage == 1:
            owned[f, :, cols] = plus(
                parts[f][0][:, cols], come[f, pl.ds(0, height), cols], across[f, :, cols]
            ).astype(BF)
            away = owned.at[f, rows((1 - y) * half, half), cols]
            copies[2, n] = send(2, n, away, half_in.at[f, :, cols], 2)
        elif stage == 2:
            owned[f, rows(mine_half, half), cols] = plus(
                owned[f, rows(mine_half, half), cols], half_in[f, :, cols]
            ).astype(BF)
            away = owned.at[f, rows(mine_half + (1 - z) * fourth, fourth), cols]
            copies[3, n] = send(3, n, away, quarter_in.at[f, :, cols], 3)
        elif stage == 3:
            quarter[f, :, cols] = plus(owned[f, rows(mine_fourth, fourth), cols], quarter_in[f, :, cols]).astype(BF)
            copies[4, n] = send(4, n, quarter.at[f, :, cols], far_in.at[f, :, cols], 4)
        elif stage == 4:
            out_ref[f, rows(mine_fourth, fourth), cols] = plus(quarter[f, :, cols], far_in[f, :, cols]).astype(BF)
            done = out_ref.at[f, rows(mine_fourth, fourth), cols]
            copies[5, n] = send(5, n, done, done, 3)
        elif stage == 5:
            done = out_ref.at[f, rows(mine_half, half), cols]
            copies[6, n] = send(6, n, done, done, 2)

    for wave in range(len(chunks) + 5 * REDUCE_LAG):
        for stage in range(6, 0, -1):
            n = wave - REDUCE_LAG * (stage - 1)
            if 0 <= n < len(chunks):
                step(stage, n)
        if wave < 5:
            flying = small_step(wave)
    for copy in started:
        copy.wait_send()


def reduce_call(terms, packed):
    flows = len(terms)
    height, width = terms[0][0].shape
    chunks = flows * (width // REDUCE_COLS)
    vmem = pl.BlockSpec(memory_space=pltpu.VMEM)
    total = flows * height * width
    return pl.pallas_call(
        functools.partial(reduce_kernel, flows),
        in_specs=[vmem] * (3 * flows + 1),
        out_specs=[vmem, vmem],
        out_shape=[shaped(flows, height, width), jax.ShapeDtypeStruct(packed.shape, F32)],
        scratch_shapes=[
            pltpu.VMEM((flows, 2 * height, width), BF),
            pltpu.VMEM((flows, height, width), BF),
            pltpu.VMEM((flows, height, width), BF),
            pltpu.VMEM((flows, height, width), BF),
            pltpu.VMEM((flows, height // 2, width), BF),
            pltpu.VMEM((flows, height // 4, width), BF),
            pltpu.VMEM((flows, height // 4, width), BF),
            pltpu.VMEM((flows, height // 4, width), BF),
            pltpu.VMEM((5,) + packed.shape, F32),
            pltpu.VMEM((4,) + packed.shape, F32),
            pltpu.SemaphoreType.DMA((7, chunks)),
            pltpu.SemaphoreType.DMA((7, chunks)),
            pltpu.SemaphoreType.DMA((5,)),
            pltpu.SemaphoreType.DMA((5,)),
        ],
        compiler_params=pltpu.CompilerParams(
            collective_id=0, has_side_effects=True, vmem_limit_bytes=40 * 2**20
        ),
        cost_estimate=cost(total, 20 * total),
        name="reduce_grads",
    )(*[t for three in terms for t in three], packed)


def swap(array, axis, bit):
    size = lax.axis_size(axis)
    return lax.ppermute(array, axis, [(i, i ^ bit) for i in range(size)])


def gather_hops(shards):
    side = lax.axis_index("rep") & 1
    halves = [s.shape[0] // 2 for s in shards]
    mine = [lax.dynamic_slice_in_dim(s, side * h, h, axis=0) for s, h in zip(shards, halves)]
    direct, core = yield [swap(m, "shard", 2) for m in mine], [swap(s, "shard", 1) for s in shards]
    relayed, cross = yield [swap(d, "rep", 1) for d in direct], [swap(d, "shard", 1) for d in direct]
    cross_relayed = yield [swap(r, "shard", 1) for r in relayed]
    return [list(p) for p in zip(shards, core, direct, relayed, cross, cross_relayed)]


def piece_starts(shard):
    height = shard.shape[0]
    me = lax.axis_index("shard")
    side = lax.axis_index("rep") & 1
    half = height // 2
    near, core, far, cross = [(me ^ o) * height for o in range(4)]
    return [near, core, far + side * half, far + (1 - side) * half, cross + side * half, cross + (1 - side) * half]


def added(*terms):
    return functools.reduce(jnp.add, [t.astype(F32) for t in terms]).astype(BF)


class Flow:
    def __init__(self, hops):
        self.hops = hops
        self.result = None
        self.flying = next(hops)

    def land(self, arrived):
        try:
            self.flying = self.hops.send(arrived)
        except StopIteration as stop:
            self.flying, self.result = None, stop.value


class Line:
    def __init__(self):
        self.flows = []
        self.recent = []

    def step(self, arrays, flows=None):
        moving = [f for f in (self.flows if flows is None else flows) if f.flying is not None]
        held = self.recent
        arrays, arrived, held = lax.optimization_barrier((arrays, [f.flying for f in moving], held))
        for flow, value in zip(moving, arrived):
            flow.land(value)
        self.recent = []
        return arrays

    def start(self, hops):
        flow = Flow(hops)
        self.flows.append(flow)
        return flow


def group_sum(grad):
    return lax.psum_scatter(grad, "shard", scatter_dimension=0, tiled=True)


def owned_hops(parts):
    keep, passed, sent = parts
    height = keep.shape[0]
    come = yield swap(sent, "shard", 1)
    onward = yield swap(added(passed, come[height:]), "shard", 2)
    return added(keep, come[:height], onward)


def replica_sum(owned):
    return lax.psum(owned, "rep").astype(F32)


def local(
    tokens,
    segment_ids,
    cotangent,
    w_qkv,
    b_query,
    b_value,
    w_out,
    b_out,
    gain_one,
    shift_one,
    w_in,
    b_in,
    w_ffo,
    b_ffo,
    gain_two,
    shift_two,
):
    micro, sequences, length, width = tokens.shape
    total = micro * sequences
    rows = total * length
    group = lax.axis_size("shard")
    hidden_width = w_in.shape[1]
    x = tokens.reshape(rows, width)
    seg = segment_ids.reshape(total, length)
    cot = cotangent.reshape(rows, width)
    me = lax.axis_index("shard")
    direct = group == 4 and lax.axis_size("rep") == 8

    part = b_query.shape[0]
    line = Line()
    small_shards = (b_query, b_value, b_out, gain_one, shift_one, b_ffo, gain_two, shift_two, b_in)
    small = jnp.concatenate(small_shards).reshape(1, -1)
    if direct:
        qkv_flow = Flow(gather_hops([w_qkv]))
        near = swap(small, "shard", 1)
        pair = jnp.concatenate([small, near], axis=0)
        four = jnp.concatenate([pair, swap(pair, "shard", 2)], axis=0)
        order = [jnp.bitwise_xor(me, o) for o in range(4)]
        small_full = jnp.concatenate([lax.dynamic_slice_in_dim(four, o, 1, axis=0) for o in order], axis=0)
        (later,) = line.step([w_ffo], [qkv_flow])
        later_flow = Flow(gather_hops([later]))
        seg = line.step(seg, [qkv_flow])
        x_first = line.step(x, [qkv_flow])
        (qkv_pieces,) = qkv_flow.result
        qkv_starts = jnp.stack(piece_starts(w_qkv)).astype(jnp.int32)
        layer_lists = [[lax.all_gather(w, "shard", axis=0, tiled=True)] for w in (w_out, w_in)]
        layer_starts = jnp.stack([jnp.int32(0)] * 2 + piece_starts(w_ffo)).astype(jnp.int32)
        counts = (1, 1, 6)
    else:
        small_full = lax.all_gather(small, "shard", axis=0, tiled=True)
        qkv_pieces, *layer_lists = [
            [lax.all_gather(w, "shard", axis=0, tiled=True)] for w in (w_qkv, w_out, w_in, w_ffo)
        ]
        x_first = x
        qkv_starts = jnp.zeros((1,), jnp.int32)
        layer_starts = jnp.zeros((3,), jnp.int32)
        counts = (1, 1, 1)
    small_full = small_full.astype(F32)
    vectors = [small_full[:, i * part : (i + 1) * part].reshape(1, -1) for i in range(8)]
    bias_all = jnp.concatenate([vectors[0], jnp.zeros_like(vectors[0]), vectors[1]], axis=1)
    vec = jnp.concatenate(vectors[2:] + [jnp.zeros((2, width), F32)], axis=0)
    bias_in = small_full[:, 8 * part :].reshape(1, -1)

    windows = windows_of(seg)
    block = 256
    (projected,) = row_call(
        functools.partial(project_kernel, len(qkv_pieces)),
        "project",
        rows,
        block,
        qkv_starts,
        [x_first],
        [bias_all],
        qkv_pieces,
        [shaped(rows, 3 * width)],
        [],
        [pltpu.VMEM((width, 3 * width), BF)],
        6 * rows * width * width,
    )
    if direct:
        projected = line.step(projected, [later_flow])
    attended, lse = attend_forward(projected, windows, total)
    if direct:
        attended = line.step(attended, [later_flow])
        attended = line.step(attended, [later_flow])
        layer_lists = layer_lists + later_flow.result
    layer_pieces = sum(layer_lists, [])
    weights_scratch = [
        pltpu.VMEM((width, width), BF),
        pltpu.VMEM((width, hidden_width), BF),
        pltpu.VMEM((hidden_width, width), BF),
    ]
    layer_flops = 2 * rows * width * (width + 2 * hidden_width)
    output, normed, n_one, rstd_one, d_second, hidden, slope, sums_two = row_call(
        functools.partial(layer_forward_kernel, counts),
        "layer_forward",
        rows,
        block,
        layer_starts,
        [x, attended, cot],
        [vec, bias_in],
        layer_pieces,
        [
            shaped(rows, width),
            shaped(rows, width),
            shaped(rows, width),
            shaped(rows, 128, dtype=F32),
            shaped(rows, width),
            shaped(rows, hidden_width),
            shaped(rows, hidden_width),
        ],
        [shaped(24, width, dtype=F32)],
        weights_scratch,
        layer_flops,
    )

    place = [jnp.bitwise_xor(me, o) for o in range(4)]
    slots = jnp.stack(
        [(p & 1) * 2 + lax.shift_right_logical(p, 1) for p in place] + [jnp.bitwise_xor(me, j) for j in (1, 3, 2, 0)]
    ).astype(jnp.int32)

    grad_ffo = plain_grad(hidden, d_second, "grad_ffo")
    owned_ffo = group_sum(grad_ffo)
    d_pre, d_branch, d_attended, sums_one, sums_in = row_call(
        functools.partial(layer_backward_kernel, counts),
        "layer_backward",
        rows,
        block,
        layer_starts,
        [d_second, slope, n_one, rstd_one],
        [vec],
        layer_pieces,
        [shaped(rows, hidden_width), shaped(rows, width), shaped(rows, width)],
        [shaped(24, width, dtype=F32), shaped(8, hidden_width, dtype=F32)],
        weights_scratch,
        layer_flops,
    )
    groups = 3
    if direct:
        *in_terms, _ = weight_grad(slots, normed, d_pre, "grad_in")
        in_flow = Flow(owned_hops(in_terms))
        d_branch, _ = lax.optimization_barrier((d_branch, in_terms[0]))
        *out_terms, _ = weight_grad(slots, attended, d_branch, "grad_out")
        out_flow = Flow(owned_hops(out_terms))
        d_attended, owned_ffo, _ = line.step((d_attended, owned_ffo, out_terms[0]), [in_flow])
        grad_ffo = replica_sum(owned_ffo)
        d_heads = attend_backward(projected, d_attended, attended, lse, windows, total, groups)
        d_heads = line.step(d_heads, [in_flow, out_flow])
        *terms, head_sums = weight_grad(slots, x, d_heads, "grad_qkv")
        d_branch, grad_ffo, owned_in, _ = line.step((d_branch, grad_ffo, in_flow.result, terms[0]), [out_flow])
        grad_in, grad_out = replica_sum(owned_in), replica_sum(out_flow.result)
    else:
        grad_ffo = replica_sum(owned_ffo)
        grad_in = replica_sum(group_sum(plain_grad(normed, d_pre, "grad_in")))
        grad_out = replica_sum(group_sum(plain_grad(attended, d_branch, "grad_out")))
        d_heads = attend_backward(projected, d_attended, attended, lse, windows, total, groups)
        grads = replica_sum(group_sum(plain_grad(x, d_heads, "grad_qkv")))
        head_sums = fold_rows(d_heads.astype(F32))

    def folded(sums):
        return [jnp.sum(sums[i : i + 8], axis=0) for i in range(0, sums.shape[0], 8)]

    d_gain_two, d_shift_two, d_ffo_bias = folded(sums_two)
    d_gain_one, d_shift_one, d_out_bias = folded(sums_one)
    (d_in_bias,) = folded(sums_in)
    cut = width // groups
    head_sums = jnp.sum(head_sums, axis=0).reshape(groups, 3, cut)
    d_query_bias = head_sums[:, 0].reshape(-1)
    d_value_bias = head_sums[:, 2].reshape(-1)
    smalls = (
        d_query_bias, d_value_bias, d_out_bias, d_gain_one, d_shift_one, d_ffo_bias, d_gain_two, d_shift_two,
        d_in_bias,
    )
    packed = jnp.concatenate([s.reshape(group, -1) for s in smalls], axis=1)
    (d_tokens,) = row_call(
        functools.partial(input_grad_kernel, len(qkv_pieces), groups),
        "input_grad",
        rows,
        block,
        qkv_starts,
        [d_branch, d_heads],
        [],
        qkv_pieces,
        [shaped(rows, width)],
        [],
        [pltpu.VMEM((width, 3 * width), BF)],
        6 * rows * width * width,
    )
    if direct:
        reduced, packed = reduce_call([terms], packed)
        grads = reduced[0].astype(F32)
    else:
        packed = lax.psum(packed, ("shard", "rep"))
    grad_qkv = grads.reshape(part, groups, 3, cut).transpose(0, 2, 1, 3).reshape(part, 3 * width)
    mine = lax.dynamic_index_in_dim(packed, me, 0, keepdims=False)
    sm = [mine[i * part : (i + 1) * part] for i in range(8)]
    gqb, gvb, gob, gg1, gs1, gfb, gg2, gs2 = sm
    gib = mine[8 * part :]
    return (
        output.reshape(tokens.shape),
        d_tokens.reshape(tokens.shape),
        grad_qkv,
        gqb,
        gvb,
        grad_out,
        gob,
        gg1,
        gs1,
        grad_in,
        gib,
        grad_ffo,
        gfb,
        gg2,
        gs2,
    )


def solution(mesh):
    data = P(None, ("shard", "rep"), None, None)
    matrix = P("shard", None)
    vector = P("shard")
    return jax.shard_map(
        local,
        mesh=mesh,
        in_specs=(
            data,
            P(None, ("shard", "rep"), None),
            data,
            matrix,
            vector,
            vector,
            matrix,
            vector,
            vector,
            vector,
            matrix,
            vector,
            matrix,
            vector,
            vector,
            vector,
        ),
        out_specs=(
            data,
            data,
            matrix,
            vector,
            vector,
            matrix,
            vector,
            vector,
            vector,
            matrix,
            vector,
            matrix,
            vector,
            vector,
            vector,
        ),
        check_vma=False,
    )
```
